32 devices in a mesh: gx: 8 (over z, core), gy: 4 (over y, x).
Axes of the slice: x: 2, y: 2, z: 4, core: 2. Of those that a mesh axis runs over, the one named last changes fastest.
Arguments:
- residual: float32 [3, 128, 64, 128], P(None, 'gx', 'gy'), may hold values from -6 to 6
- stiffness: float32 [128, 64], P('gx', 'gy'), may hold values from 0.5 to 2
- local_inverse: bfloat16 [8, 4, 1024, 1024], P('gx', 'gy'), as said below
- coarse_basis: bfloat16 [8, 4, 8, 1024], P('gx', 'gy'), may hold values from -0.5 to 0.5
- coarse_rows: bfloat16 [8, 4, 8, 256], P('gx', 'gy'), as said below
- send_rows: int32 [8, 4, 4, 64], P('gx', 'gy'), may hold values from 0 to 767, as said below
- partition_map: int32 [32], replicated, may hold values from 0 to 31, as said below
Outputs:
- solution: float32 [3, 128, 64, 128], P(None, 'gx', 'gy')
- final: float32 [3, 128, 64, 128], P(None, 'gx', 'gy')
The draws below stay inside these ranges and needn't reach their ends.
Inputs may be any that keep to these rules, and one draw needn't show every extreme that they name: `send_rows`: for each subdomain, the lists j = 0, 1 (lower and upper neighbour along gx) and j = 2, 3 (lower and upper neighbour along gy) each name 64 distinct owned rows, all of them in the two layers of cells nearest that neighbour. `partition_map`: A permutation of the device numbers. `coarse_rows`: with its columns put in device order through partition_map, the 256-square matrix S is symmetric. `local_inverse`: each subdomain's block is symmetric.
All inputs are finite; a program needn't handle non-finite values.
Results may differ from the reference program's by a relative error of at most 0.0057.
Values may be sent and summed in bfloat16 or wider, within the bound.
A program may use at most 64 MiB of HBM per device.

```python
import math
import jax
import jax.numpy as jnp
from jax import lax

NV = 128
CX = 16
CY = 16
OV = 64
K = 8
M = 1024
NX = 128
NY = 64
KD = 256
N_GX = 8
N_GY = 4


def draw_local_inverse(key, part):
    device_count = NX // CX * (NY // CY)
    lower_end, upper_end, spread = (0.12, 0.26, 0.06)

    def one_block(number):
        block_key = jax.random.fold_in(key, number)
        noise_draw = jax.random.normal(jax.random.fold_in(block_key, 1), (M, M), jnp.float32)
        diagonal = jax.random.uniform(jax.random.fold_in(block_key, 2), (M,), jnp.float32, lower_end, upper_end)
        symmetric = (noise_draw + noise_draw.T) * (spread / math.sqrt(2.0 * M))
        return (symmetric + jnp.diag(diagonal)).astype(jnp.bfloat16)
    blocks = lax.map(one_block, jnp.arange(device_count, dtype=jnp.int32))
    return blocks.reshape(NX // CX, NY // CY, M, M)


def coarse_order(key):
    device_count = NX // CX * (NY // CY)
    return jax.random.permutation(jax.random.fold_in(key, 7), device_count).astype(jnp.int32)


def draw_partition_map(key, part):
    return coarse_order(key)


def draw_coarse_rows(key, part):
    device_count = NX // CX * (NY // CY)
    order_size = K * device_count
    back_scale, link_scale = (0.1, 0.25)
    noise_draw = jax.random.normal(jax.random.fold_in(key, 11), (order_size, order_size), jnp.float32)
    background = (noise_draw + noise_draw.T) * (back_scale / math.sqrt(2.0 * order_size))
    diagonal = jax.random.uniform(jax.random.fold_in(key, 12), (order_size,), jnp.float32, 0.1, 0.2)
    partners = jax.random.permutation(jax.random.fold_in(key, 13), device_count)
    first_half = partners[0::2]
    second_half = partners[1::2]
    link_blocks = jax.random.normal(jax.random.fold_in(key, 14), (device_count // 2, K, K), jnp.float32)
    link_blocks = link_blocks * (link_scale / math.sqrt(K))
    pair_terms = jnp.zeros((device_count, K, device_count, K), jnp.float32)
    pair_terms = pair_terms.at[first_half, :, second_half, :].set(link_blocks)
    pair_terms = pair_terms.at[second_half, :, first_half, :].set(jnp.swapaxes(link_blocks, 1, 2))
    whole_matrix = background + pair_terms.reshape(order_size, order_size) + jnp.diag(diagonal)
    positions = coarse_order(key)
    stored = jnp.zeros((order_size, device_count, K), jnp.float32)
    stored = stored.at[:, positions, :].set(whole_matrix.reshape(order_size, device_count, K))
    return stored.astype(jnp.bfloat16).reshape(NX // CX, NY // CY, K, order_size)


def draw_send_rows(key, part):
    device_count = NX // CX * (NY // CY)
    key_list = jax.random.split(key, device_count * 4)
    across_picks = jax.vmap(lambda one_key: jax.random.permutation(one_key, 6 * CY)[:OV])(key_list[:2 * device_count])
    along_picks = jax.vmap(lambda one_key: jax.random.permutation(one_key, 6 * CX)[:OV])(key_list[2 * device_count:])
    across_picks = across_picks.reshape(device_count, 2, OV)
    along_picks = along_picks.reshape(device_count, 2, OV)
    side_index = jnp.arange(2, dtype=jnp.int32)[None, :, None]
    component = across_picks // (2 * CY)
    remainder = across_picks % (2 * CY)
    layer_index = remainder // CY
    first_cell = jnp.where(side_index == 0, layer_index, CX - 1 - layer_index)
    across_rows = component * CX * CY + first_cell * CY + remainder % CY
    component = along_picks // (2 * CX)
    remainder = along_picks % (2 * CX)
    layer_index = remainder // CX
    second_cell = jnp.where(side_index == 0, layer_index, CY - 1 - layer_index)
    along_rows = component * CX * CY + remainder % CX * CY + second_cell
    all_rows = jnp.concatenate([across_rows, along_rows], axis=1)
    return all_rows.reshape(NX // CX, NY // CY, 4, OV).astype(jnp.int32)


def shard_levels(key, extent, cuts, smallest, high):
    level, own = 1.0, jax.random.fold_in(key, 6)
    for axis_at, blocks in cuts:
        heights = jnp.exp(jax.random.uniform(jax.random.fold_in(own, axis_at), (blocks,), jnp.float32, smallest / len(cuts), high / len(cuts)))
        level = level * jnp.repeat(heights, extent[axis_at] // blocks).reshape([-1 if axis == axis_at else 1 for axis in range(len(extent))])
    return level


def gaussian(own_key, extent, scale, bound, shards=(), kind=jnp.bfloat16):
    values = jax.random.normal(own_key, extent, jnp.float32) * scale
    if len(shards) > 0:
        values = shard_levels(own_key, extent, shards, -0.22, 0.18) * values
    return jnp.clip(values, min=-bound, max=bound).astype(kind)


def setup_inputs(seed: int = 0) -> dict:
    key_of = jax.random.split(jax.random.key(seed), 8)
    return {
        "residual": gaussian(key_of[0], (3, NX, NY, NV), 1.0, 6.0, ((1, 8), (2, 4)), jnp.float32),
        "stiffness": jnp.clip(jnp.exp(math.log(2.0) - 1.3862944 * jax.random.uniform(key_of[1], (NX, NY), jnp.float32) ** shard_levels(key_of[1], (NX, NY), ((0, 8), (1, 4)), -0.2, 0.2)), 0.5, 2.0),
        "local_inverse": draw_local_inverse(jax.random.fold_in(key_of[7], 71), 0),
        "coarse_basis": gaussian(key_of[3], (N_GX, N_GY, K, M), 0.08, 0.5, ((0, 8), (1, 4))),
        "coarse_rows": draw_coarse_rows(jax.random.fold_in(key_of[7], 71), 0),
        "send_rows": draw_send_rows(jax.random.fold_in(key_of[7], 71), 0),
        "partition_map": draw_partition_map(jax.random.fold_in(key_of[7], 71), 0),
    }


def from_lower(blocks, axis):
    edge = jnp.zeros_like(lax.slice_in_dim(blocks, 0, 1, axis=axis))
    return jnp.concatenate([edge, lax.slice_in_dim(blocks, 0, blocks.shape[axis] - 1, axis=axis)], axis=axis)


def from_upper(blocks, axis):
    edge = jnp.zeros_like(lax.slice_in_dim(blocks, 0, 1, axis=axis))
    return jnp.concatenate([lax.slice_in_dim(blocks, 1, blocks.shape[axis], axis=axis), edge], axis=axis)


def pick_rows(matrix, picks):
    return jnp.take(matrix, picks, axis=0)


def project_down(group):
    return jnp.dot(group[0], group[1], preferred_element_type=jnp.float32)


def apply_local(group):
    local_part = jnp.dot(group[0], group[1], preferred_element_type=jnp.float32)
    return local_part + jnp.dot(group[2].T, group[3], preferred_element_type=jnp.float32)


def add_back(update, picks, incoming):
    update = update.at[picks[0]].add(incoming[0])
    update = update.at[picks[1]].add(incoming[1])
    update = update.at[picks[2]].add(incoming[2])
    return update.at[picks[3]].add(incoming[3])


def operate(values, stiffness):
    padded = jnp.pad(values, ((0, 0), (1, 1), (1, 1), (0, 0)))
    beside = padded[:, 2:, 1:-1] + padded[:, :-2, 1:-1] + padded[:, 1:-1, 2:] + padded[:, 1:-1, :-2]
    return (4.0 + stiffness[None, :, :, None]) * values - beside


def correct(values, local_inverse, coarse_basis, coarse_rows, send_rows, partition_map):
    grid_rows = N_GX
    grid_cols = N_GY
    device_count = grid_rows * grid_cols
    own_count = 3 * CX * CY
    own_rows = values.reshape(3, grid_rows, CX, grid_cols, CY, NV).transpose(1, 3, 0, 2, 4, 5)
    own_rows = own_rows.reshape(grid_rows, grid_cols, own_count, NV)
    outgoing = jax.vmap(jax.vmap(pick_rows))(own_rows, send_rows)
    subdomain = jnp.concatenate([own_rows, from_lower(outgoing[:, :, 1], 0), from_upper(outgoing[:, :, 0], 0),
                                 from_lower(outgoing[:, :, 3], 1), from_upper(outgoing[:, :, 2], 1)], axis=2)
    subdomain = subdomain.astype(jnp.bfloat16)
    flat_sub = subdomain.reshape(device_count, M, NV)
    flat_inverse = local_inverse.reshape(device_count, M, M)
    flat_basis = coarse_basis.reshape(device_count, K, M)
    coarse_in = lax.map(project_down, (flat_basis, flat_sub)).astype(jnp.bfloat16)
    whole_matrix = coarse_rows.reshape(KD, device_count, K)[:, partition_map, :].reshape(KD, KD)
    coarse_out = jnp.dot(whole_matrix, coarse_in.reshape(KD, NV), preferred_element_type=jnp.float32)
    coarse_out = coarse_out.astype(jnp.bfloat16).reshape(device_count, K, NV)
    patch = lax.map(apply_local, (flat_inverse, flat_sub, flat_basis, coarse_out)).reshape(grid_rows, grid_cols, M, NV)
    own_patch = patch[:, :, :own_count]
    back_zero = from_lower(patch[:, :, own_count + OV:own_count + 2 * OV], 0)
    back_one = from_upper(patch[:, :, own_count:own_count + OV], 0)
    back_two = from_lower(patch[:, :, own_count + 3 * OV:], 1)
    back_three = from_upper(patch[:, :, own_count + 2 * OV:own_count + 3 * OV], 1)
    incoming = jnp.stack([back_zero, back_one, back_two, back_three], axis=2)
    update = jax.vmap(jax.vmap(add_back))(own_patch, send_rows, incoming)
    update = update.reshape(grid_rows, grid_cols, 3, CX, CY, NV).transpose(2, 0, 3, 1, 4, 5)
    return update.reshape(3, NX, NY, NV)


def reference(residual, stiffness, local_inverse, coarse_basis, coarse_rows, send_rows, partition_map):
    first_pass = correct(residual, local_inverse, coarse_basis, coarse_rows, send_rows, partition_map)
    middle = residual - operate(first_pass, stiffness)
    second_pass = correct(middle, local_inverse, coarse_basis, coarse_rows, send_rows, partition_map)
    solution = first_pass + second_pass
    return solution, residual - operate(solution, stiffness)
```

```python
import functools

import jax
import jax.numpy as jnp
from jax import lax
from jax.experimental import pallas as pl
from jax.experimental.pallas import tpu as pltpu
from jax.sharding import PartitionSpec as P

MESH = pl.DeviceIdType.MESH
F32 = jnp.float32
BF16 = jnp.bfloat16
HIGH = lax.Precision.HIGHEST


def dot(x, y, **kw):
    return jnp.dot(x, y, preferred_element_type=F32, **kw)


def tdot(x, y):
    return lax.dot_general(x, y, (((0,), (0,)), ((), ())), preferred_element_type=F32)


def fiota(shape, axis):
    return lax.broadcasted_iota(jnp.int32, shape, axis).astype(F32)


def fdiv(x, n):
    return jnp.floor((x + 0.5) * (1.0 / n))


def kernel(
    gx, gy, dims,
    res_hbm, stiff_hbm, inv_hbm, basis_hbm, crows_hbm, lists_hbm, pmap_hbm,
    sol_ref, fin_ref,
    res_v, stiff_ref, inv_v, basis_ref, crows_ref, lists_ref, pmap_ref, sub, sel, near, outs, msg_s, msg_r,
    dsend, drecv, qs, qr, gmat, pmat, gp, allbuf,
    sext, bsend, brecv, bextf, cmat, acmat, csend, diag, m_lo, m_hi, xs, mid,
    lsem, nsem_s, nsem_r, dsem_s, dsem_r, csem_s, csem_r, gs, gr,
):
    comps, cx, cy, nv = dims
    halo = comps * max(cx, cy)
    hrows = (comps * cy, comps * cy, comps * cx, comps * cx)
    own = comps * cx * cy
    layer = cx * cy
    ov = lists_ref.shape[1]
    kw, kd = crows_ref.shape
    n = gx * gy
    dr = drecv.shape[1] // 4
    a = lax.axis_index("gx")
    b = lax.axis_index("gy")

    wanted = [
        (lists_hbm, lists_ref), (res_hbm, res_v), (pmap_hbm, pmap_ref), (crows_hbm, crows_ref),
        (basis_hbm, basis_ref), (stiff_hbm, stiff_ref), (inv_hbm, inv_v),
    ]
    loads = [pltpu.make_async_copy(x, y, lsem.at[k]) for k, (x, y) in enumerate(wanted)]
    load_lists, load_res, load_pmap, load_crows, load_basis, load_stiff, load_inv = loads
    for load in loads:
        load.start()

    def flip(x, k):
        y, bit = x, 1
        while bit <= k:
            if k & bit:
                y = y + bit * (1 - 2 * lax.rem(lax.div(x, bit), 2))
            bit *= 2
        return y

    paired = gx & (gx - 1) == 0 and gy & (gy - 1) == 0
    others = [(i, j) for i in range(gx) for j in range(gy) if i or j]
    if paired:
        others.sort(key=lambda o: -((o[0] >> 1) + bin(o[1]).count("1") + 0.4 * (o[0] & 1)))
        to_a = [flip(a, i) for i in range(gx)]
        to_b = [flip(b, j) for j in range(gy)]
    else:
        to_a = [lax.rem(a + i, gx) for i in range(gx)]
        to_b = [lax.rem(b + j, gy) for j in range(gy)]

    def each_other(act):
        if n <= 64:
            for i, j in others:
                act((to_a[i], to_b[j]))
            return

        def row(i, _):
            ai = lax.rem(a + i, gx)
            for j in range(1, gy):
                act((ai, lax.rem(b + j, gy)))
            pl.when(i > 0)(lambda: act((ai, b)))
            return 0

        lax.fori_loop(jnp.int32(0), jnp.int32(gx), row, 0)

    barrier = pltpu.get_barrier_semaphore()
    each_other(lambda dev: pl.semaphore_signal(barrier, inc=1, device_id=dev, device_id_type=MESH))

    up = [(a + 1, b), (a - 1, b), (a, b + 1), (a, b - 1)]
    has_up = [a < gx - 1, a > 0, b < gy - 1, b > 0]
    down = [up[p ^ 1] for p in range(4)]
    has_down = [has_up[p ^ 1] for p in range(4)]
    corner = [(1, 1), (-1, -1), (1, -1), (-1, 1)]
    cdev = [(a + sx, b + sy) for sx, sy in corner]
    has_c = [
        jnp.logical_and(has_up[0 if sx > 0 else 1], has_up[2 if sy > 0 else 3]) for sx, sy in corner
    ]
    finish = []

    def send(copies, conds, wait):
        for p in (2, 3, 0, 1):
            @pl.when(conds[p])
            def _(p=p):
                for c in copies(p):
                    getattr(c, wait)()

    def trade(copies, to, fro):
        send(copies, to, "start")
        finish.append(lambda: send(copies, to, "wait_send"))
        return lambda: send(copies, fro, "wait_recv")

    def remote(src, dst, s, r, dev):
        return pltpu.make_async_remote_copy(
            src_ref=src, dst_ref=dst, send_sem=s, recv_sem=r, device_id=dev, device_id_type=MESH
        )

    wide_grid = 4 * max(cx, cy)

    def code(c, i, j):
        return (c * wide_grid + (i + cx)) * wide_grid + (j + cy)

    load_lists.wait()
    lists = lists_ref[...].astype(F32)
    columns = lists.T
    for p in range(4):
        count = 2 * hrows[p]
        q = fiota((1, count), 1)
        if p < 2:
            c = fdiv(q, 2 * cy)
            row = c * layer + (layer - 2 * cy) * (1 - p) + (q - c * 2 * cy)
        else:
            second = jnp.where(q >= comps * cx, 1.0, 0.0)
            row = (q - second * (comps * cx)) * cy + (cy - 2) * (3 - p) + second
        hit = jnp.broadcast_to(columns[:, (p ^ 1) : (p ^ 1) + 1], (ov, count)) == jnp.broadcast_to(row, (ov, count))
        near[p, :, :count] = jnp.where(hit, 1.0, 0.0).astype(BF16)

    lc = fdiv(lists, layer)
    li = fdiv(lists - lc * layer, cy)
    lj = lists - lc * layer - li * cy
    for p, (dx, dy) in enumerate(((-1, 0), (1, 0), (0, -1), (0, 1))):
        mine = code(lc, li + dx * cx, lj + dy * cy)[(p ^ 1) : (p ^ 1) + 1]
        pair = [mine, jnp.zeros_like(mine)]
        qs[p] = jnp.broadcast_to(jnp.concatenate(pair if p % 2 == 0 else pair[::-1], axis=1), (8, 2 * ov))

    load_res.wait()

    def gather(t, src):
        for p in range(4):
            if p < 2:
                skip = (layer - 2 * cy) * (1 - p)
                rows = [src[c * layer + skip : c * layer + skip + 2 * cy, :] for c in range(comps)]
            else:
                rows = [src[pl.ds((cy - 2) * (3 - p) + k, comps * cx, stride=cy), :] for k in range(2)]
            rows = jnp.concatenate(rows, axis=0).astype(BF16)
            outs[t, p * ov : (p + 1) * ov, :] = dot(near[p, :, : 2 * hrows[p]], rows).astype(BF16)

    gather(0, res_v)
    pl.semaphore_wait(barrier, n - 1)
    wait_q = trade(lambda p: [remote(qs.at[p], qr.at[p], csem_s.at[3, p], csem_r.at[3, p], up[p])], has_up, has_down)

    def start_margins(t):
        return trade(
            lambda p: [remote(outs.at[t, pl.ds(p * ov, ov)], sub.at[t, pl.ds(own + p * ov, ov)],
                              nsem_s.at[t, 0, p], nsem_r.at[t, 0, p], up[p])],
            has_up, has_down,
        )

    wait_margins = start_margins(0)
    sub[0, :own, :] = res_v[...].astype(BF16)

    for p in range(4):
        at = own + p * ov

        @pl.when(jnp.logical_not(has_down[p]))
        def _(p=p, at=at):
            for t in range(2):
                sub[t, at : at + ov, :] = jnp.zeros((ov, nv), BF16)
                msg_r[t, p] = jnp.zeros(msg_r.shape[2:], BF16)
            qr[p] = jnp.zeros(qr.shape[1:], F32)
            cmat[own + p * halo : own + (p + 1) * halo, :] = jnp.zeros((halo, kd), BF16)

        @pl.when(jnp.logical_not(has_up[p]))
        def _(p=p):
            sext[(p + 1) * kw : (p + 2) * kw, :] = jnp.zeros((kw, kd), F32)
            brecv[p * kw : (p + 1) * kw, :] = jnp.zeros((kw, 4 * ov), F32)

        @pl.when(jnp.logical_not(has_c[p ^ 1]))
        def _(p=p):
            for t in range(2):
                drecv[t, p * dr : (p + 1) * dr, :] = jnp.zeros((dr, nv), BF16)

    sext[5 * kw :, :] = jnp.zeros((sext.shape[0] - 5 * kw, kd), F32)

    load_pmap.wait()
    load_crows.wait()
    load_basis.wait()
    wide = min(kd, 256)
    pmf = jnp.broadcast_to(pmap_ref[...].astype(F32), (8, n))

    def order(c, _):
        q = fiota((1, wide), 1) + (c * wide).astype(F32)
        slot = fdiv(q, kw)
        slab = fdiv(slot, gx)
        dev = (slot - slab * gx) * gy + slab
        pick = jnp.where(fiota((n, wide), 0) == dev, 1.0, 0.0)
        place = dot(pmf, pick, precision=HIGH)[0:1] * kw + (q - slot * kw)
        perm = jnp.where(fiota((kd, wide), 0) == place, 1.0, 0.0).astype(BF16)
        sext[0:kw, pl.ds(pl.multiple_of(c * wide, wide), wide)] = dot(crows_ref[...], perm)
        return 0

    lax.fori_loop(jnp.int32(0), jnp.int32(kd // wide), order, 0)
    bsend[...] = basis_ref[:, own:].astype(F32)
    wait_coarse = trade(
        lambda p: [
            remote(sext.at[pl.ds(0, kw)], sext.at[pl.ds((p + 1) * kw, kw)], csem_s.at[0, p], csem_r.at[0, p], down[p]),
            remote(bsend, brecv.at[pl.ds(p * kw, kw)], csem_s.at[1, p], csem_r.at[1, p], down[p]),
        ],
        has_down, has_up,
    )

    rows = fiota((own, ov), 0)
    for h in range(2):
        two = [jnp.where(rows == lists[p : p + 1], 1.0, 0.0) for p in (2 * h, 2 * h + 1)]
        sel[:, 2 * ov * h : 2 * ov * (h + 1)] = jnp.concatenate(two, axis=1).astype(BF16)

    load_stiff.wait()
    r1 = fiota((layer, cy), 0)
    first = fdiv(r1, cy)
    mine = jnp.where(fiota((layer, cx), 1) == fdiv(fiota((layer, cx), 0), cy), 1.0, 0.0)
    spread = dot(mine, stiff_ref[...], precision=HIGH)
    spread = jnp.where(fiota((layer, cy), 1) == r1 - first * cy, spread, 0.0)
    diag[...] = jnp.broadcast_to(4.0 + jnp.sum(spread, axis=1, keepdims=True), (layer, nv))
    rr = fiota((layer, nv), 0)
    second = rr - fdiv(rr, cy) * cy
    m_lo[...] = jnp.where(second == 0.0, 0.0, 1.0)
    m_hi[...] = jnp.where(second == cy - 1.0, 0.0, 1.0)

    def ring_codes(p, lanes):
        w = fiota((halo, lanes), 0)
        per = cy if p < 2 else cx
        c = fdiv(w, per)
        along = w - c * per
        i, j = (along * 0.0 + (-1.0, cx)[p % 2], along) if p < 2 else (along, along * 0.0 + (-1.0, cy)[p % 2])
        return jnp.where(w < hrows[p], code(c, i, j), -1.0)

    def corner_codes(w, sx, sy):
        g = fdiv(w, 2 * comps)
        c = fdiv(w - g * (2 * comps), 2)
        k = w - g * (2 * comps) - 2 * c
        i = jnp.where(g == 0.0, (sx + 1) * 0.5 * (cx - 1), (sx + 1) * 0.5 * (cx - 1) + sx * (1.0 + k))
        j = jnp.where(g == 0.0, (sy + 1) * 0.5 * (cy - 1) + sy * (1.0 + k), (sy + 1) * 0.5 * (cy - 1))
        return c, i, j, g < 2.0

    w = fiota((1, 4 * dr), 1)
    m = fdiv(w, dr)
    sx = jnp.where(jnp.logical_or(m == 0.0, m == 2.0), 1.0, -1.0)
    sy = jnp.where(jnp.logical_or(m == 0.0, m == 3.0), 1.0, -1.0)
    c, i, j, real = corner_codes(w - m * dr, sx, sy)
    landed = jnp.where(real, code(c, i - sx * cx, j - sy * cy), -2.0)
    for p in range(4):
        at = slice(p * halo, (p + 1) * halo)
        pmat[at, :] = jnp.where(ring_codes(p, 4 * dr) == landed, 1.0, 0.0).astype(BF16)

    def fill_gmat():
        for h in range(2):
            q = (qr[2 * h] + qr[2 * h + 1])[0:1]
            lanes = slice(2 * ov * h, 2 * ov * (h + 1))
            for p in range(4):
                at = slice(p * halo, (p + 1) * halo)
                gmat[at, lanes] = jnp.where(ring_codes(p, 2 * ov) == q, 1.0, 0.0).astype(BF16)
                c, i, j, real = corner_codes(fiota((dr, 2 * ov), 0), *corner[p])
                at = slice(4 * halo + p * dr, 4 * halo + (p + 1) * dr)
                gmat[at, lanes] = jnp.where(jnp.where(real, code(c, i, j), -1.0) == q, 1.0, 0.0).astype(BF16)

    def layer_rows(ref, p):
        if p >= 2:
            return ref[pl.ds((cy - 1) * (3 - p), comps * cx, stride=cy), :]
        skip = (layer - cy) * (1 - p)
        return jnp.concatenate([ref[c * layer + skip : c * layer + skip + cy, :] for c in range(comps)], axis=0)

    def operate(x_ref, dst, src):
        zero = jnp.zeros((cy, nv), F32)
        for c in range(comps):
            at = pl.ds(c * layer, layer)
            x = x_ref[at, :]
            beside = jnp.concatenate([zero, x[:-cy]], axis=0) + jnp.concatenate([x[cy:], zero], axis=0)
            beside += pltpu.roll(x, 1, 0) * m_lo[...] + pltpu.roll(x, layer - 1, 0) * m_hi[...]
            value = beside - diag[...] * x
            dst[at, :] = value if src is None else src[at, :] + value

    def add_layers(dst, around):
        for c in range(comps):
            base = c * layer
            dst[base : base + cy, :] += around(0)[c * cy : (c + 1) * cy]
            dst[base + layer - cy : base + layer, :] += around(1)[c * cy : (c + 1) * cy]
        low = pl.ds(0, comps * cx, stride=cy)
        high = pl.ds(cy - 1, comps * cx, stride=cy)
        dst[low, :] = dst[low, :] + around(2)
        dst[high, :] = dst[high, :] + around(3)

    wait_edges = []
    slot = b * gx + a

    def correct(t, src, dst, wait_margins):
        if t == 0:
            load_inv.wait()
        part = dot(inv_v[:, :own], sub[t, :own, :])
        cpart = dot(basis_ref[:, :own], sub[t, :own, :])
        wait_margins()
        edge = sub[t, own:, :]
        cin = cpart + dot(basis_ref[:, own:], edge)
        allbuf[t, slot] = cin.astype(BF16)
        here = allbuf.at[t, slot]
        each_other(lambda dev: remote(here, here, gs.at[t], gr.at[t], dev).start())
        rest = allbuf.at[t, pl.ds(0, n - 1)]
        gathering = remote(rest, rest, gs.at[t], gr.at[t], (to_a[0], to_b[1]))

        pm = (part[own:] + dot(inv_v[own:, own:], edge)).astype(BF16)
        if t == 0:
            wait_q()
            fill_gmat()
        gp[...] = dot(gmat[...], pm)
        dsend[t] = gp[4 * halo :, :].astype(BF16)
        wait_corners = trade(
            lambda p: [remote(dsend.at[t, pl.ds(p * dr, dr)], drecv.at[t, pl.ds(p * dr, dr)],
                              dsem_s.at[t, p], dsem_r.at[t, p], cdev[p])],
            has_c, [has_c[p ^ 1] for p in range(4)],
        )
        xs[...] = part[:own] + dot(inv_v[:own, own:], edge)
        for p in range(4):
            msg_s[t, p, :ov, :] = pm[(p ^ 1) * ov : ((p ^ 1) + 1) * ov]
            msg_s[t, p, ov : ov + hrows[p], :] = layer_rows(xs, p).astype(BF16)
        wait_back = trade(
            lambda p: [remote(msg_s.at[t, p], msg_r.at[t, p], nsem_s.at[t, 1, p], nsem_r.at[t, 1, p], up[p])],
            has_up, has_down,
        )
        if t == 0:
            wait_coarse()
            rb = fdiv(fiota((4 * kw, 4 * ov), 0), kw)
            cb = fdiv(fiota((4 * kw, 4 * ov), 1), ov)
            margins = jnp.where(rb == cb, brecv[...], 0.0)
            margins = [pltpu.roll(margins[:, 2 * ov * h : 2 * ov * (h + 1)], ov, 1) for h in range(2)]
            margins = jnp.concatenate(margins, axis=1).astype(BF16)
            below = lax.dot_general(margins, sel[...], (((1,), (1,)), ((), ())), preferred_element_type=F32)
            zeros = jnp.zeros((sext.shape[0] - 5 * kw, own), F32)
            ext = jnp.concatenate([basis_ref[:, :own].astype(F32), below, zeros], axis=0)
            bextf[...] = ext.T
            edges = jnp.concatenate([layer_rows(bextf, p) for p in range(4)], axis=0).astype(BF16)

            def build(c, _):
                at = pl.ds(pl.multiple_of(c * wide, wide), wide)
                part_s = sext[:, at].astype(BF16)
                csend[:, at] = dot(edges, part_s).astype(BF16)
                return 0

            lax.fori_loop(jnp.int32(0), jnp.int32(kd // wide), build, 0)
            wait_edges.append(trade(
                lambda p: [remote(csend.at[pl.ds(p * halo, halo)], cmat.at[pl.ds(own + p * halo, halo)],
                                  csem_s.at[2, p], csem_r.at[2, p], up[p])],
                has_up, has_down,
            ))
        wait_back()
        backs = jnp.concatenate([msg_r[t, p, :ov, :] for p in range(4)], axis=0)
        xs[...] += dot(sel[...], backs)
        operate(xs, dst, src)
        wait_corners()
        gp[: 4 * halo, :] += dot(pmat[...], drecv[t])

        def around(p):
            return msg_r[t, p, ov : ov + hrows[p], :].astype(F32) + gp[p * halo : p * halo + hrows[p], :]

        add_layers(dst, around)
        if t == 0:
            wait_edges[0]()
            bext = bextf[...].astype(BF16)

            def fill(c, _):
                at = pl.ds(pl.multiple_of(c * nv, nv), nv)
                value = dot(bext, sext[:, at].astype(BF16))
                cmat[:own, at] = value.astype(BF16)
                sol_ref[...] = value
                operate(sol_ref, fin_ref, None)
                add_layers(fin_ref, lambda p: cmat[own + p * halo : own + p * halo + hrows[p], at].astype(F32))
                acmat[:, at] = fin_ref[...].astype(BF16)
                return 0

            lax.fori_loop(jnp.int32(0), jnp.int32(kd // nv), fill, 0)
        gathering.wait_recv()
        gathered = allbuf[t].astype(F32).reshape(kd, nv).astype(BF16)
        dst[...] += dot(acmat[...], gathered)
        finish.append(gathering.wait_send)
        return gathered

    gathered = correct(0, res_v, mid, wait_margins)
    gather(1, mid)
    wait_margins = start_margins(1)
    sub[1, :own, :] = mid[...].astype(BF16)
    sol_ref[...] = xs[...] + dot(cmat[:own, :], gathered)
    gathered = correct(1, mid, fin_ref, wait_margins)
    sol_ref[...] += xs[...] + dot(cmat[:own, :], gathered)
    for end in finish:
        end()


def solution(mesh):
    gx, gy = mesh.shape["gx"], mesh.shape["gy"]

    def per_device(residual, stiffness, local_inverse, coarse_basis, coarse_rows, send_rows, partition_map):
        comps, cx, cy, nv = residual.shape
        own, layer = comps * cx * cy, cx * cy
        m = local_inverse.shape[-1]
        ov = send_rows.shape[-1]
        kw, kd = coarse_rows.shape[-2:]
        halo = comps * max(cx, cy)
        lanes = -(-5 * kw // 128) * 128
        dr = -(-4 * comps // 16) * 16
        vm = pl.BlockSpec(memory_space=pltpu.VMEM)
        anywhere = pl.BlockSpec(memory_space=pl.ANY)
        dma = pltpu.SemaphoreType.DMA
        out = pl.pallas_call(
            functools.partial(kernel, gx, gy, (comps, cx, cy, nv)),
            out_shape=[pltpu.VMEM((own, nv), F32)] * 2,
            in_specs=[anywhere] * 7,
            out_specs=[vm, vm],
            scratch_shapes=[
                pltpu.VMEM((own, nv), F32),
                pltpu.VMEM((cx, cy), F32),
                pltpu.VMEM((m, m), BF16),
                pltpu.VMEM((kw, m), BF16),
                pltpu.VMEM((kw, kd), BF16),
                pltpu.VMEM((4, ov), jnp.int32),
                pltpu.VMEM((1, gx * gy), jnp.int32),
                pltpu.VMEM((2, m, nv), BF16),
                pltpu.VMEM((own, 4 * ov), BF16),
                pltpu.VMEM((4, ov, 2 * halo), BF16),
                pltpu.VMEM((2, 4 * ov, nv), BF16),
                pltpu.VMEM((2, 4, ov + halo, nv), BF16),
                pltpu.VMEM((2, 4, ov + halo, nv), BF16),
                pltpu.VMEM((2, 4 * dr, nv), BF16),
                pltpu.VMEM((2, 4 * dr, nv), BF16),
                pltpu.VMEM((4, 8, 2 * ov), F32),
                pltpu.VMEM((4, 8, 2 * ov), F32),
                pltpu.VMEM((4 * halo + 4 * dr, 4 * ov), BF16),
                pltpu.VMEM((4 * halo, 4 * dr), BF16),
                pltpu.VMEM((4 * halo + 4 * dr, nv), F32),
                pltpu.VMEM((2, gx * gy, kw, nv), BF16),
                pltpu.VMEM((lanes, kd), F32),
                pltpu.VMEM((kw, m - own), F32),
                pltpu.VMEM((4 * kw, m - own), F32),
                pltpu.VMEM((own, lanes), F32),
                pltpu.VMEM((own + 4 * halo, kd), BF16),
                pltpu.VMEM((own, kd), BF16),
                pltpu.VMEM((4 * halo, kd), BF16),
                pltpu.VMEM((layer, nv), F32),
                pltpu.VMEM((layer, nv), F32),
                pltpu.VMEM((layer, nv), F32),
                pltpu.VMEM((own, nv), F32),
                pltpu.VMEM((own, nv), F32),
                dma((7,)),
                dma((2, 2, 4)),
                dma((2, 2, 4)),
                dma((2, 4)),
                dma((2, 4)),
                dma((4, 4)),
                dma((4, 4)),
                dma((2,)),
                dma((2,)),
            ],
            compiler_params=pltpu.CompilerParams(collective_id=0, has_side_effects=True),
        )(
            residual.reshape(own, nv),
            stiffness,
            local_inverse[0, 0],
            coarse_basis[0, 0],
            coarse_rows[0, 0],
            send_rows[0, 0],
            partition_map.reshape(1, -1),
        )
        return tuple(o.reshape(residual.shape) for o in out)

    placed = (
        P(None, "gx", "gy", None),
        P("gx", "gy"),
        P("gx", "gy", None, None),
        P("gx", "gy", None, None),
        P("gx", "gy", None, None),
        P("gx", "gy", None, None),
        P(),
    )
    return jax.shard_map(
        per_device,
        mesh=mesh,
        in_specs=placed,
        out_specs=(P(None, "gx", "gy", None), P(None, "gx", "gy", None)),
        check_vma=False,
    )
```

```python
import functools

import jax
import jax.numpy as jnp
from jax import lax
from jax.experimental import pallas as pl
from jax.experimental.pallas import tpu as pltpu
from jax.sharding import PartitionSpec as P

MESH = pl.DeviceIdType.MESH
F32 = jnp.float32
BF16 = jnp.bfloat16
HIGH = lax.Precision.HIGHEST


def dot(x, y, **kw):
    return jnp.dot(x, y, preferred_element_type=F32, **kw)


def tdot(x, y):
    return lax.dot_general(x, y, (((0,), (0,)), ((), ())), preferred_element_type=F32)


def fiota(shape, axis):
    return lax.broadcasted_iota(jnp.int32, shape, axis).astype(F32)


def fdiv(x, n):
    return jnp.floor((x + 0.5) * (1.0 / n))


def kernel(
    gx, gy, dims,
    res_hbm, stiff_hbm, inv_hbm, basis_hbm, crows_hbm, lists_hbm, pmap_hbm,
    sol_ref, fin_ref,
    res_v, stiff_ref, inv_v, basis_ref, crows_ref, lists_ref, pmap_ref, sub, sel, near, outs,
    ybuf, ycode, rowc, qb, sb, gmat, mmat, pmat, pmat2, ring, msg_s, dsend, msg2_s, msg2_r, dsend2, drecv2,
    qs, qr, ts, tr, allbuf, ball, sall, sext, bt, bextf, abf, bextb, abextb, am_s, am_r, edge2,
    diag, m_lo, m_hi, xs, mid,
    lsem, nsem_s, nsem_r, dsem_s, dsem_r, csem_s, csem_r, rsem_s, rsem_r, gs, gr,
):
    comps, cx, cy, nv = dims
    halo = comps * max(cx, cy)
    hrows = (comps * cy, comps * cy, comps * cx, comps * cx)
    own = comps * cx * cy
    layer = cx * cy
    ov = lists_ref.shape[1]
    kw, kd = crows_ref.shape
    n = gx * gy
    mrows = msg_s.shape[1]
    crows = mrows - ov - 3 * halo
    dr, dr2 = dsend.shape[1], dsend2.shape[0] // 4
    yedge = 4 * ov
    ymsg = yedge + 4 * halo
    ycorner = ymsg + 4 * mrows
    ny = ybuf.shape[0]
    nine = ball.shape[0]
    lanes = bextf.shape[1]
    a = lax.axis_index("gx")
    b = lax.axis_index("gy")

    wanted = [
        (lists_hbm, lists_ref), (res_hbm, res_v), (pmap_hbm, pmap_ref), (crows_hbm, crows_ref),
        (basis_hbm, basis_ref), (stiff_hbm, stiff_ref), (inv_hbm, inv_v),
    ]
    loads = [pltpu.make_async_copy(x, y, lsem.at[k]) for k, (x, y) in enumerate(wanted)]
    load_lists, load_res, load_pmap, load_crows, load_basis, load_stiff, load_inv = loads
    for load in loads:
        load.start()

    def flip(x, k):
        y, bit = x, 1
        while bit <= k:
            if k & bit:
                y = y + bit * (1 - 2 * lax.rem(lax.div(x, bit), 2))
            bit *= 2
        return y

    paired = gx & (gx - 1) == 0 and gy & (gy - 1) == 0
    others = [(i, j) for i in range(gx) for j in range(gy) if i or j]
    if paired:
        others.sort(key=lambda o: -((o[0] >> 1) + bin(o[1]).count("1") + 0.4 * (o[0] & 1)))
        to_a = [flip(a, i) for i in range(gx)]
        to_b = [flip(b, j) for j in range(gy)]
    else:
        to_a = [lax.rem(a + i, gx) for i in range(gx)]
        to_b = [lax.rem(b + j, gy) for j in range(gy)]

    def each_other(act):
        if n <= 64:
            for i, j in others:
                act((to_a[i], to_b[j]))
            return

        def row(i, _):
            ai = lax.rem(a + i, gx)
            for j in range(1, gy):
                act((ai, lax.rem(b + j, gy)))
            pl.when(i > 0)(lambda: act((ai, b)))
            return 0

        lax.fori_loop(jnp.int32(0), jnp.int32(gx), row, 0)

    barrier = pltpu.get_barrier_semaphore()
    each_other(lambda dev: pl.semaphore_signal(barrier, inc=1, device_id=dev, device_id_type=MESH))

    up = [(a + 1, b), (a - 1, b), (a, b + 1), (a, b - 1)]
    has_up = [a < gx - 1, a > 0, b < gy - 1, b > 0]
    down = [up[p ^ 1] for p in range(4)]
    has_down = [has_up[p ^ 1] for p in range(4)]
    corner = [(1, 1), (-1, -1), (1, -1), (-1, 1)]
    cdev = [(a + sx, b + sy) for sx, sy in corner]
    has_c = [
        jnp.logical_and(has_up[0 if sx > 0 else 1], has_up[2 if sy > 0 else 3]) for sx, sy in corner
    ]
    finish = []

    def send(copies, conds, wait):
        for p in (2, 3, 0, 1):
            @pl.when(conds[p])
            def _(p=p):
                for c in copies(p):
                    getattr(c, wait)()

    def trade(copies, to, fro):
        send(copies, to, "start")
        finish.append(lambda: send(copies, to, "wait_send"))
        return lambda: send(copies, fro, "wait_recv")

    def remote(src, dst, s, r, dev):
        return pltpu.make_async_remote_copy(
            src_ref=src, dst_ref=dst, send_sem=s, recv_sem=r, device_id=dev, device_id_type=MESH
        )

    wide_grid = 4 * max(cx, cy)

    def code(c, i, j):
        return (c * wide_grid + (i + cx)) * wide_grid + (j + cy)

    load_lists.wait()
    lists = lists_ref[...].astype(F32)
    columns = lists.T
    for p in range(4):
        count = 2 * hrows[p]
        q = fiota((1, count), 1)
        if p < 2:
            c = fdiv(q, 2 * cy)
            row = c * layer + (layer - 2 * cy) * (1 - p) + (q - c * 2 * cy)
        else:
            second = jnp.where(q >= comps * cx, 1.0, 0.0)
            row = (q - second * (comps * cx)) * cy + (cy - 2) * (3 - p) + second
        hit = jnp.broadcast_to(columns[:, (p ^ 1) : (p ^ 1) + 1], (ov, count)) == jnp.broadcast_to(row, (ov, count))
        near[p, :, :count] = jnp.where(hit, 1.0, 0.0).astype(BF16)

    lc = fdiv(lists, layer)
    li = fdiv(lists - lc * layer, cy)
    lj = lists - lc * layer - li * cy
    block = fdiv(fiota((1, 4 * ov), 1), ov)

    def in_line(x):
        return jnp.concatenate([x[(p ^ 1) : (p ^ 1) + 1] for p in range(4)], axis=1)

    sides = ((-1, 0), (1, 0), (0, -1), (0, 1))
    for p, (dx, dy) in enumerate(sides):
        line = in_line(code(lc, li + dx * cx, lj + dy * cy))
        qs[p, 0:1, :] = jnp.where(block == p, line, 0.0)
        qs[p, 1:2, :] = line

    load_res.wait()

    def gather(t, src):
        for p in range(4):
            if p < 2:
                skip = (layer - 2 * cy) * (1 - p)
                rows = [src[c * layer + skip : c * layer + skip + 2 * cy, :] for c in range(comps)]
            else:
                rows = [src[pl.ds((cy - 2) * (3 - p) + k, comps * cx, stride=cy), :] for k in range(2)]
            rows = jnp.concatenate(rows, axis=0).astype(BF16)
            outs[t, p * ov : (p + 1) * ov, :] = dot(near[p, :, : 2 * hrows[p]], rows).astype(BF16)

    gather(0, res_v)
    pl.semaphore_wait(barrier, n - 1)

    def start_margins(t):
        return trade(
            lambda p: [
                remote(outs.at[t, pl.ds(p * ov, ov)], sub.at[t, pl.ds(own + p * ov, ov)],
                       nsem_s.at[0, p], nsem_r.at[0, p], up[p]),
                remote(qs.at[p], qr.at[p], csem_s.at[0, p], csem_r.at[0, p], up[p]),
            ],
            has_up, has_down,
        )

    wait_margins = start_margins(0)
    has_cd = [has_c[p ^ 1] for p in range(4)]
    wait_raw = trade(
        lambda p: [
            remote(basis_hbm, ball.at[1 + p], csem_s.at[1, p], csem_r.at[1, p], up[p]),
            remote(crows_hbm, sall.at[1 + p], csem_s.at[2, p], csem_r.at[2, p], up[p]),
        ],
        has_up, has_down,
    )
    wait_raw_c = trade(
        lambda p: [
            remote(basis_hbm, ball.at[5 + p], rsem_s.at[0, p], rsem_r.at[0, p], cdev[p]),
            remote(crows_hbm, sall.at[5 + p], rsem_s.at[1, p], rsem_r.at[1, p], cdev[p]),
        ],
        has_c, has_cd,
    )
    sub[0, :own, :] = res_v[...].astype(BF16)

    for p in range(4):
        @pl.when(jnp.logical_not(has_down[p]))
        def _(p=p):
            sub[0, own + p * ov : own + (p + 1) * ov, :] = jnp.zeros((ov, nv), BF16)
            ybuf[ymsg + p * mrows : ymsg + (p + 1) * mrows, :] = jnp.zeros((mrows, nv), BF16)
            msg2_r[p] = jnp.zeros(msg2_r.shape[1:], BF16)
            qr[p] = jnp.zeros(qr.shape[1:], F32)
            tr[p] = jnp.zeros(tr.shape[1:], F32)
            am_r[p * ov : (p + 1) * ov, :] = jnp.zeros((ov, kd), BF16)
            ball[1 + p] = jnp.zeros(ball.shape[1:], BF16)
            sall[1 + p] = jnp.zeros(sall.shape[1:], BF16)

        @pl.when(jnp.logical_not(has_cd[p]))
        def _(p=p):
            ybuf[ycorner + p * dr : ycorner + (p + 1) * dr, :] = jnp.zeros((dr, nv), BF16)
            drecv2[p * dr2 : (p + 1) * dr2, :] = jnp.zeros((dr2, nv), BF16)
            ball[5 + p] = jnp.zeros(ball.shape[1:], BF16)
            sall[5 + p] = jnp.zeros(sall.shape[1:], BF16)

    if ny > ycorner + 4 * dr:
        ybuf[ycorner + 4 * dr :, :] = jnp.zeros((ny - ycorner - 4 * dr, nv), BF16)

    load_stiff.wait()
    r1 = fiota((layer, cy), 0)
    first = fdiv(r1, cy)
    mine = jnp.where(fiota((layer, cx), 1) == fdiv(fiota((layer, cx), 0), cy), 1.0, 0.0)
    spread = dot(mine, stiff_ref[...], precision=HIGH)
    spread = jnp.where(fiota((layer, cy), 1) == r1 - first * cy, spread, 0.0)
    diag[...] = jnp.broadcast_to(4.0 + jnp.sum(spread, axis=1, keepdims=True), (layer, nv))
    rr = fiota((layer, nv), 0)
    second = rr - fdiv(rr, cy) * cy
    m_lo[...] = jnp.where(second == 0.0, 0.0, 1.0)
    m_hi[...] = jnp.where(second == cy - 1.0, 0.0, 1.0)

    cells = jnp.where(fiota((layer, 4 * ov), 0) == in_line(li * cy + lj), 1.0, 0.0)
    at_cells = lax.dot_general(
        diag[...], cells, (((0,), (0,)), ((), ())), precision=HIGH, preferred_element_type=F32
    )[0:8]
    for p in range(4):
        ts[p] = jnp.where(jnp.broadcast_to(block, (8, 4 * ov)) == p, at_cells, 0.0)
    wait_t = trade(
        lambda p: [remote(ts.at[p], tr.at[p], csem_s.at[3, p], csem_r.at[3, p], up[p])], has_up, has_down
    )

    def edge_cells(w, p, depth, outside):
        per = cy if p < 2 else cx
        c = fdiv(w, per)
        along = w - c * per
        size = cx if p < 2 else cy
        if outside:
            off = along * 0.0 + (-1.0 - depth, size + depth)[p % 2]
        else:
            off = along * 0.0 + (size - 1.0 - depth, 1.0 * depth)[p % 2]
        return (c, off, along, w < hrows[p]) if p < 2 else (c, along, off, w < hrows[p])

    def beside_cells(w, p):
        v = fdiv(w, 3 * comps)
        u = 1.0 - 2.0 * v
        c = fdiv(w - v * (3 * comps), 3)
        kk = w - v * (3 * comps) - 3 * c
        deep, far = jnp.where(kk == 1.0, 1.0, 0.0), jnp.where(kk == 2.0, 1.0, 0.0)
        size, size2 = (cx, cy) if p < 2 else (cy, cx)
        along = (size - 1.0 - deep) if p % 2 == 0 else deep
        out = jnp.where(v == 0.0, size2 + far, -1.0 - far)
        return (c, along, out, v < 2.0) if p < 2 else (c, out, along, v < 2.0)

    def corner_cells(w, sx, sy):
        ex, ey = (cx - 1.0 if sx > 0 else 0.0), (cy - 1.0 if sy > 0 else 0.0)
        ox, oy = (1.0 * cx if sx > 0 else -1.0), (1.0 * cy if sy > 0 else -1.0)
        g = fdiv(w, 2 * comps)
        depth = fdiv(g, 2)
        kind = g - 2 * depth
        c = fdiv(w - g * (2 * comps), 2)
        k = w - g * (2 * comps) - 2 * c
        i = jnp.where(kind == 0.0, ex - sx * depth, ox + sx * k)
        j = jnp.where(kind == 0.0, oy + sy * k, ey - sy * depth)
        w2 = w - 12 * comps
        c2 = fdiv(w2, 3)
        kk = w2 - 3 * c2
        tail = w2 >= 0.0
        i = jnp.where(tail, ex - sx * jnp.where(kk == 1.0, 1.0, 0.0), i)
        j = jnp.where(tail, ey - sy * jnp.where(kk == 2.0, 1.0, 0.0), j)
        return jnp.where(tail, c2, c), i, j, w < 15 * comps

    nowhere = -16.0 * wide_grid * wide_grid

    def coded(cell, dx=0, dy=0):
        c, i, j, real = cell
        return jnp.where(real, code(c, i - dx * cx, j - dy * cy), nowhere)

    def row_of(count):
        return fiota((1, count), 1)

    tail = []
    for p in range(4):
        c, i, j, real = edge_cells(row_of(halo), p, 0, False)
        if p >= 2:
            real = jnp.logical_and(real, jnp.logical_and(i > 0.0, i < cx - 1.0))
        tail.append(coded((c, i, j, real)))
    for p in range(4):
        ux, uy = -sides[p][0], -sides[p][1]
        tail.append(code(lc, li, lj)[p : p + 1])
        tail += [coded(edge_cells(row_of(halo), p, d, True)) for d in range(3)]
        tail.append(coded(beside_cells(row_of(crows), p), ux, uy))
    for m in range(4):
        tail.append(coded(corner_cells(row_of(dr), *corner[m]), *corner[m]))
    if ny > ycorner + 4 * dr:
        tail.append(jnp.full((1, ny - ycorner - 4 * dr), nowhere, F32))
    ycode[0:1, yedge:] = jnp.concatenate(tail, axis=1)

    def column_of(count):
        return fiota((count, 128), 0)

    rlist = [coded(edge_cells(column_of(halo), p, 0, True)) for p in range(4)]
    rlist += [coded(corner_cells(column_of(dr2), *corner[m])) for m in range(4)]
    rlist += [coded(beside_cells(column_of(crows), p)) for p in range(4)]
    rlist += [coded(corner_cells(column_of(dr - dr2) + dr2, *corner[m])) for m in range(4)]
    rowc[...] = jnp.concatenate(rlist, axis=0)

    def hits(rows, row):
        parts = []
        for at in range(0, row.shape[1], 128):
            piece = row[:, at : at + 128]
            parts.append(jnp.where(rows[:, : piece.shape[1]] == piece, 1.0, 0.0))
        return (jnp.concatenate(parts, axis=1) if len(parts) > 1 else parts[0]).astype(BF16)

    pmat[...] = hits(rowc[: 4 * halo, :], ycode[0:1, ycorner : ycorner + 4 * dr])
    short = [coded(corner_cells(row_of(dr2), *corner[m]), *corner[m]) for m in range(4)]
    pmat2[...] = hits(rowc[: 4 * halo, :], jnp.concatenate(short, axis=1))

    rows = fiota((own, ov), 0)
    for h in range(2):
        two = [jnp.where(rows == lists[p : p + 1], 1.0, 0.0) for p in (2 * h, 2 * h + 1)]
        sel[:, 2 * ov * h : 2 * ov * (h + 1)] = jnp.concatenate(two, axis=1).astype(BF16)

    def layer_rows(ref, p, depth=0):
        if p >= 2:
            return ref[pl.ds(cy - 1 - depth if p == 2 else depth, comps * cx, stride=cy), :]
        skip = layer - cy - depth * cy if p == 0 else depth * cy
        return jnp.concatenate([ref[c * layer + skip : c * layer + skip + cy, :] for c in range(comps)], axis=0)

    def operate(x_ref, dst, src):
        zero = jnp.zeros((cy, nv), F32)
        for c in range(comps):
            at = pl.ds(c * layer, layer)
            x = x_ref[at, :]
            beside = jnp.concatenate([zero, x[:-cy]], axis=0) + jnp.concatenate([x[cy:], zero], axis=0)
            beside += pltpu.roll(x, 1, 0) * m_lo[...] + pltpu.roll(x, layer - 1, 0) * m_hi[...]
            value = beside - diag[...] * x
            dst[at, :] = value if src is None else src[at, :] + value

    def add_layers(dst, around):
        for c in range(comps):
            base = c * layer
            dst[base : base + cy, :] += around(0)[c * cy : (c + 1) * cy]
            dst[base + layer - cy : base + layer, :] += around(1)[c * cy : (c + 1) * cy]
        low = pl.ds(0, comps * cx, stride=cy)
        high = pl.ds(cy - 1, comps * cx, stride=cy)
        dst[low, :] = dst[low, :] + around(2)
        dst[high, :] = dst[high, :] + around(3)

    def ring_side(p):
        return ring[p * halo : p * halo + hrows[p], :]

    slot = b * gx + a

    def start_gather(t, cin):
        allbuf[t, slot] = cin.astype(BF16)
        here = allbuf.at[t, slot]
        each_other(lambda dev: remote(here, here, gs.at[t], gr.at[t], dev).start())
        rest = allbuf.at[t, pl.ds(0, n - 1)]
        gathering = remote(rest, rest, gs.at[t], gr.at[t], (to_a[0], to_b[1]))
        finish.append(gathering.wait_send)

        def arrived():
            gathering.wait_recv()
            return allbuf[t].astype(F32).reshape(kd, nv).astype(BF16)

        return arrived

    load_basis.wait()
    load_inv.wait()
    part = dot(inv_v[:, :own], sub[0, :own, :])
    cpart = dot(basis_ref[:, :own], sub[0, :own, :])
    wait_margins()
    edge = sub[0, own:, :]
    arrived = start_gather(0, cpart + dot(basis_ref[:, own:], edge))
    ycode[0:1, :yedge] = (qr[0] + qr[1] + qr[2] + qr[3])[0:1]
    pm = (part[own:] + dot(inv_v[own:, own:], edge)).astype(BF16)
    ybuf[:yedge, :] = pm
    xs[...] = part[:own] + dot(inv_v[:own, own:], edge)
    ybuf[yedge:ymsg, :] = jnp.concatenate([layer_rows(xs, p) for p in range(4)], axis=0).astype(BF16)
    gmat[...] = hits(rowc[...], ycode[0:1, :ymsg])
    made = dot(gmat[...], ybuf[:ymsg, :])
    ring[...] = made[: 4 * halo]
    made = made[4 * halo :].astype(BF16)
    late = 4 * dr2 + 4 * crows
    for p in range(4):
        msg_s[p, :ov, :] = pm[(p ^ 1) * ov : ((p ^ 1) + 1) * ov]
        for d in range(3):
            msg_s[p, ov + d * halo : ov + d * halo + hrows[p], :] = layer_rows(xs, p, d).astype(BF16)
        msg_s[p, ov + 3 * halo :, :] = made[4 * dr2 + p * crows : 4 * dr2 + (p + 1) * crows]
        dsend[p, :dr2, :] = made[p * dr2 : (p + 1) * dr2]
        dsend[p, dr2:, :] = made[late + p * (dr - dr2) : late + (p + 1) * (dr - dr2)]
    wait_corners = trade(
        lambda p: [remote(dsend.at[p], ybuf.at[pl.ds(ycorner + p * dr, dr)], dsem_s.at[0, p], dsem_r.at[0, p], cdev[p])],
        has_c, has_cd,
    )
    wait_back = trade(
        lambda p: [remote(msg_s.at[p], ybuf.at[pl.ds(ymsg + p * mrows, mrows)], nsem_s.at[1, p], nsem_r.at[1, p], up[p])],
        has_up, has_down,
    )

    load_pmap.wait()
    load_crows.wait()
    wait_raw()
    wait_raw_c()
    ball[0] = basis_ref[...]
    sall[0] = crows_ref[...]
    spare = lanes - nine * kw
    stacked = jnp.concatenate([ball[...].astype(F32).reshape(nine * kw, -1), jnp.zeros((spare, own + 4 * ov), F32)], axis=0)
    bt[...] = stacked.T
    group = fdiv(fiota((1, lanes), 1), kw)

    def of(e, value):
        return jnp.where(group == e, value, 0.0)

    def margin(k):
        return bt[own + k * ov : own + (k + 1) * ov, :]

    theirs = jnp.concatenate([of(1.0 + p, margin(p ^ 1)) for p in range(4)], axis=0).astype(BF16)
    bextf[...] = of(0.0, bt[:own, :]) + dot(sel[...], theirs)
    around_b = jnp.concatenate([of(1.0 + p, layer_rows(bt, p)) for p in range(4)], axis=0)
    around_b += dot(gmat[: 4 * halo, :yedge], of(0.0, bt[own:, :]).astype(BF16))
    for m, (sx, sy) in enumerate(corner):
        ky, py = (0 if sx < 0 else 1), (3 if sy < 0 else 2)
        kx, px = (2 if sy < 0 else 3), (1 if sx < 0 else 0)
        lines = [qr[py, 1:2, ky * ov : (ky + 1) * ov], qr[px, 1:2, kx * ov : (kx + 1) * ov]]
        oh = hits(rowc[: 4 * halo, :], jnp.concatenate(lines, axis=1))
        around_b += dot(oh, of(5.0 + m, jnp.concatenate([margin(ky), margin(kx)], axis=0)).astype(BF16))
    edge2[: 4 * halo, :] = around_b
    operate(bextf, abf, None)
    add_layers(abf, lambda p: edge2[p * halo : p * halo + hrows[p], :])
    bextb[...] = bextf[...].astype(BF16)
    abextb[...] = abf[...].astype(BF16)
    gather(1, abf)

    wide = min(kd, 256)
    pmf = jnp.broadcast_to(pmap_ref[...].astype(F32), (8, n))
    spare_s = jnp.zeros((spare, kd), F32)
    stacked_s = jnp.concatenate([sall[...].astype(F32).reshape(nine * kw, kd), spare_s], axis=0).astype(BF16)

    def order(c, _):
        q = fiota((1, wide), 1) + (c * wide).astype(F32)
        at_slot = fdiv(q, kw)
        slab = fdiv(at_slot, gx)
        dev = (at_slot - slab * gx) * gy + slab
        pick = jnp.where(fiota((n, wide), 0) == dev, 1.0, 0.0)
        place = dot(pmf, pick, precision=HIGH)[0:1] * kw + (q - at_slot * kw)
        perm = jnp.where(fiota((kd, wide), 0) == place, 1.0, 0.0).astype(BF16)
        at = pl.ds(pl.multiple_of(c * wide, wide), wide)
        sext[:, at] = dot(stacked_s, perm).astype(BF16)
        am_s[:, at] = dot(outs[1], sext[:, at]).astype(BF16)
        return 0

    lax.fori_loop(jnp.int32(0), jnp.int32(kd // wide), order, 0)
    wait_am = trade(
        lambda p: [remote(am_s.at[pl.ds(p * ov, ov)], am_r.at[pl.ds(p * ov, ov)], csem_s.at[4, p], csem_r.at[4, p], up[p])],
        has_up, has_down,
    )

    def as_column(line):
        return jnp.broadcast_to(jnp.broadcast_to(line, (8, 4 * ov)).T[:, 0:1], (4 * ov, 128))

    qb[...] = as_column(ycode[0:1, :yedge])
    wait_t()
    sb[...] = as_column((tr[0] + tr[1] + tr[2] + tr[3])[0:1])

    def relate(c, _):
        at = pl.ds(pl.multiple_of(c * 128, 128), 128)
        gap = jnp.abs(ycode[0:1, at] - qb[...])
        mmat[: 4 * ov, at] = jnp.where(gap == 0.0, 1.0, 0.0).astype(BF16)
        mmat[4 * ov :, at] = jnp.where(jnp.logical_or(gap == 1.0, gap == wide_grid), 1.0, 0.0).astype(BF16)
        return 0

    lax.fori_loop(jnp.int32(0), jnp.int32(ny // 128), relate, 0)

    wait_back()
    wait_corners()
    seen = dot(mmat[...], ybuf[...])
    edge2m = sub[0, own:, :].astype(F32) + seen[4 * ov :] - sb[...] * seen[: 4 * ov]
    edge2[: 4 * ov, :] = edge2m
    backs = jnp.concatenate([ybuf[ymsg + p * mrows : ymsg + p * mrows + ov, :] for p in range(4)], axis=0)
    xs[...] += dot(sel[...], backs)
    operate(xs, mid, res_v)
    ring[...] += dot(pmat[...], ybuf[ycorner : ycorner + 4 * dr, :])
    add_layers(mid, lambda p: ring_side(p) + ybuf[ymsg + p * mrows + ov : ymsg + p * mrows + ov + hrows[p], :].astype(F32))
    wait_am()
    gathered = arrived()
    cout = dot(sext[...], gathered).astype(BF16)
    sub[1, own:, :] = (edge2[: 4 * ov, :] + dot(am_r[...], gathered)).astype(BF16)
    mid[...] += dot(abextb[...], cout)
    sub[1, :own, :] = mid[...].astype(BF16)

    arrived = start_gather(1, dot(basis_ref[...], sub[1]))
    sol_ref[...] = xs[...] + dot(bextb[...], cout)
    pm = dot(inv_v[own:, :], sub[1]).astype(BF16)
    made = dot(gmat[: 4 * halo + 4 * dr2, :yedge], pm)
    ring[...] = made[: 4 * halo]
    dsend2[...] = made[4 * halo :].astype(BF16)
    wait_corners = trade(
        lambda p: [remote(dsend2.at[pl.ds(p * dr2, dr2)], drecv2.at[pl.ds(p * dr2, dr2)], dsem_s.at[1, p], dsem_r.at[1, p], cdev[p])],
        has_c, has_cd,
    )
    xs[...] = dot(inv_v[:own, :], sub[1])
    for p in range(4):
        msg2_s[p, :ov, :] = pm[(p ^ 1) * ov : ((p ^ 1) + 1) * ov]
        msg2_s[p, ov : ov + hrows[p], :] = layer_rows(xs, p).astype(BF16)
    wait_back = trade(
        lambda p: [remote(msg2_s.at[p], msg2_r.at[p], nsem_s.at[2, p], nsem_r.at[2, p], up[p])],
        has_up, has_down,
    )
    wait_back()
    backs = jnp.concatenate([msg2_r[p, :ov, :] for p in range(4)], axis=0)
    xs[...] += dot(sel[...], backs)
    sol_ref[...] += xs[...]
    operate(xs, fin_ref, mid)
    wait_corners()
    ring[...] += dot(pmat2[...], drecv2[...])
    add_layers(fin_ref, lambda p: ring_side(p) + msg2_r[p, ov : ov + hrows[p], :].astype(F32))
    gathered = arrived()
    cout = dot(sext[...], gathered).astype(BF16)
    fin_ref[...] += dot(abextb[...], cout)
    sol_ref[...] += dot(bextb[...], cout)
    for end in finish:
        end()


def emit(sol_ref, fin_ref, sol_hbm, fin_hbm, sem):
    pairs = ((sol_ref, sol_hbm), (fin_ref, fin_hbm))
    copies = [pltpu.make_async_copy(x, y, sem.at[k]) for k, (x, y) in enumerate(pairs)]
    for c in copies:
        c.start()
    for c in copies:
        c.wait()


def solution(mesh):
    gx, gy = mesh.shape["gx"], mesh.shape["gy"]

    def per_device(residual, stiffness, local_inverse, coarse_basis, coarse_rows, send_rows, partition_map):
        comps, cx, cy, nv = residual.shape
        own, layer = comps * cx * cy, cx * cy
        m = local_inverse.shape[-1]
        ov = send_rows.shape[-1]
        kw, kd = coarse_rows.shape[-2:]
        halo = comps * max(cx, cy)
        def whole(count, of):
            return -(-count // of) * of

        lanes = whole(9 * kw, 128)
        dr, dr2 = whole(15 * comps, 16), whole(4 * comps, 16)
        crows = whole(6 * comps, 16)
        mrows = ov + 3 * halo + crows
        ny = whole(4 * (ov + halo + mrows + dr), 128)
        grows = 4 * (halo + crows + dr)
        vm = pl.BlockSpec(memory_space=pltpu.VMEM)
        anywhere = pl.BlockSpec(memory_space=pl.ANY)
        dma = pltpu.SemaphoreType.DMA
        out = pl.pallas_call(
            functools.partial(kernel, gx, gy, (comps, cx, cy, nv)),
            out_shape=[pltpu.VMEM((own, nv), F32)] * 2,
            in_specs=[anywhere] * 7,
            out_specs=[vm, vm],
            scratch_shapes=[
                pltpu.VMEM((own, nv), F32),
                pltpu.VMEM((cx, cy), F32),
                pltpu.VMEM((m, m), BF16),
                pltpu.VMEM((kw, m), BF16),
                pltpu.VMEM((kw, kd), BF16),
                pltpu.VMEM((4, ov), jnp.int32),
                pltpu.VMEM((1, gx * gy), jnp.int32),
                pltpu.VMEM((2, m, nv), BF16),
                pltpu.VMEM((own, 4 * ov), BF16),
                pltpu.VMEM((4, ov, 2 * halo), BF16),
                pltpu.VMEM((2, 4 * ov, nv), BF16),
                pltpu.VMEM((ny, nv), BF16),
                pltpu.VMEM((8, ny), F32),
                pltpu.VMEM((grows, 128), F32),
                pltpu.VMEM((4 * ov, 128), F32),
                pltpu.VMEM((4 * ov, 128), F32),
                pltpu.VMEM((grows, 4 * ov + 4 * halo), BF16),
                pltpu.VMEM((8 * ov, ny), BF16),
                pltpu.VMEM((4 * halo, 4 * dr), BF16),
                pltpu.VMEM((4 * halo, 4 * dr2), BF16),
                pltpu.VMEM((4 * halo, nv), F32),
                pltpu.VMEM((4, mrows, nv), BF16),
                pltpu.VMEM((4, dr, nv), BF16),
                pltpu.VMEM((4, ov + halo, nv), BF16),
                pltpu.VMEM((4, ov + halo, nv), BF16),
                pltpu.VMEM((4 * dr2, nv), BF16),
                pltpu.VMEM((4 * dr2, nv), BF16),
                pltpu.VMEM((4, 8, 4 * ov), F32),
                pltpu.VMEM((4, 8, 4 * ov), F32),
                pltpu.VMEM((4, 8, 4 * ov), F32),
                pltpu.VMEM((4, 8, 4 * ov), F32),
                pltpu.VMEM((2, gx * gy, kw, nv), BF16),
                pltpu.VMEM((9, kw, m), BF16),
                pltpu.VMEM((9, kw, kd), BF16),
                pltpu.VMEM((lanes, kd), BF16),
                pltpu.VMEM((m, lanes), F32),
                pltpu.VMEM((own, lanes), F32),
                pltpu.VMEM((own, lanes), F32),
                pltpu.VMEM((own, lanes), BF16),
                pltpu.VMEM((own, lanes), BF16),
                pltpu.VMEM((4 * ov, kd), BF16),
                pltpu.VMEM((4 * ov, kd), BF16),
                pltpu.VMEM((max(4 * ov, 4 * halo), nv), F32),
                pltpu.VMEM((layer, nv), F32),
                pltpu.VMEM((layer, nv), F32),
                pltpu.VMEM((layer, nv), F32),
                pltpu.VMEM((own, nv), F32),
                pltpu.VMEM((own, nv), F32),
                dma((7,)),
                dma((3, 4)),
                dma((3, 4)),
                dma((2, 4)),
                dma((2, 4)),
                dma((5, 4)),
                dma((5, 4)),
                dma((2, 4)),
                dma((2, 4)),
                dma((2,)),
                dma((2,)),
            ],
            compiler_params=pltpu.CompilerParams(collective_id=0, has_side_effects=True),
        )(
            residual.reshape(own, nv),
            stiffness,
            local_inverse[0, 0],
            coarse_basis[0, 0],
            coarse_rows[0, 0],
            send_rows[0, 0],
            partition_map.reshape(1, -1),
        )
        out = pl.pallas_call(
            emit,
            out_shape=[jax.ShapeDtypeStruct((own, nv), F32)] * 2,
            in_specs=[vm, vm],
            out_specs=[anywhere, anywhere],
            scratch_shapes=[dma((2,))],
        )(*[pltpu.with_memory_space_constraint(o, pltpu.VMEM) for o in out])
        return tuple(o.reshape(residual.shape) for o in out)

    placed = (
        P(None, "gx", "gy", None),
        P("gx", "gy"),
        P("gx", "gy", None, None),
        P("gx", "gy", None, None),
        P("gx", "gy", None, None),
        P("gx", "gy", None, None),
        P(),
    )
    return jax.shard_map(
        per_device,
        mesh=mesh,
        in_specs=placed,
        out_specs=(P(None, "gx", "gy", None), P(None, "gx", "gy", None)),
        check_vma=False,
    )
```

```python
import functools

import jax
import jax.numpy as jnp
from jax import lax
from jax.experimental import pallas as pl
from jax.experimental.pallas import tpu as pltpu
from jax.sharding import PartitionSpec as P

MESH = pl.DeviceIdType.MESH
F32 = jnp.float32
BF16 = jnp.bfloat16
HIGH = lax.Precision.HIGHEST


def dot(x, y, **kw):
    return jnp.dot(x, y, preferred_element_type=F32, **kw)


def split(x, y):
    cut = x.shape[0] // 32 * 16
    return jnp.concatenate([dot(x[:cut, :], y), dot(x[cut:, :], y)], axis=0)


def tdot(x, y):
    return lax.dot_general(x, y, (((0,), (0,)), ((), ())), preferred_element_type=F32)


def fiota(shape, axis):
    return lax.broadcasted_iota(jnp.int32, shape, axis).astype(F32)


def fdiv(x, n):
    return jnp.floor((x + 0.5) * (1.0 / n))


def kernel(
    gx, gy, dims,
    res_hbm, stiff_hbm, inv_hbm, basis_hbm, crows_hbm, lists_hbm, pmap_hbm,
    sol_ref, fin_ref,
    res_v, stiff_ref, inv_v, basis_ref, crows_ref, lists_ref, pmap_ref, sub, sel, near, outs,
    ybuf, ycode, lines, rowc, qb, sb, gmat, gstat, cown, cmarg, mc, inve, pmv, ring, msg_s, dsend,
    msg2_s, msg2_r, dsend2, drecv2,
    qs, qr, ts, tr, allbuf, ball, sall, sext, bt, bextf, abf, bextb, abextb, am_s, am_r, edge2,
    diag, m_lo, m_hi, xs, mid,
    lsem, ready, nsem_s, nsem_r, dsem_s, dsem_r, csem_s, csem_r, rsem_s, rsem_r, gs, gr,
):
    comps, cx, cy, nv = dims
    halo = comps * max(cx, cy)
    hrows = (comps * cy, comps * cy, comps * cx, comps * cx)
    own = comps * cx * cy
    layer = cx * cy
    ov = lists_ref.shape[1]
    kw, kd = crows_ref.shape
    n = gx * gy
    mrows = msg_s.shape[1]
    crows = mrows - ov - 3 * halo
    dr, dr2 = dsend.shape[1], dsend2.shape[0] // 4
    yedge = 4 * ov
    ycorner = 4 * mrows
    gpm = 4 * (dr + crows)
    nine = ball.shape[0]
    lanes = bextf.shape[1]
    a = lax.axis_index("gx")
    b = lax.axis_index("gy")

    wanted = [
        (lists_hbm, lists_ref), (res_hbm, res_v), (pmap_hbm, pmap_ref), (crows_hbm, crows_ref),
        (basis_hbm, basis_ref), (stiff_hbm, stiff_ref), (inv_hbm, inv_v),
    ]
    loads = [pltpu.make_async_copy(x, y, lsem.at[k]) for k, (x, y) in enumerate(wanted)]
    load_lists, load_res, load_pmap, load_crows, load_basis, load_stiff, load_inv = loads
    for load in loads:
        load.start()

    def flip(x, k):
        y, bit = x, 1
        while bit <= k:
            if k & bit:
                y = y + bit * (1 - 2 * lax.rem(lax.div(x, bit), 2))
            bit *= 2
        return y

    paired = gx & (gx - 1) == 0 and gy & (gy - 1) == 0
    others = [(i, j) for i in range(gx) for j in range(gy) if i or j]
    if paired:
        others.sort(key=lambda o: -((o[0] >> 1) + bin(o[1]).count("1") + 0.4 * (o[0] & 1)))
        to_a = [flip(a, i) for i in range(gx)]
        to_b = [flip(b, j) for j in range(gy)]
    else:
        to_a = [lax.rem(a + i, gx) for i in range(gx)]
        to_b = [lax.rem(b + j, gy) for j in range(gy)]

    half = len(others) // 2

    def each_other(act, chosen=None):
        if n <= 64:
            for i, j in others if chosen is None else (others[:half], others[half:])[chosen]:
                act((to_a[i], to_b[j]))
            return
        if chosen == 1:
            return

        def row(i, _):
            ai = lax.rem(a + i, gx)
            for j in range(1, gy):
                act((ai, lax.rem(b + j, gy)))
            pl.when(i > 0)(lambda: act((ai, b)))
            return 0

        lax.fori_loop(jnp.int32(0), jnp.int32(gx), row, 0)

    barrier = pltpu.get_barrier_semaphore()

    def peers(size):
        return sorted(range(1, size), key=lambda o: min(o, size - o))

    def signal(sem, dev):
        pl.semaphore_signal(sem, inc=1, device_id=dev, device_id_type=MESH)

    for o in peers(gy):
        signal(barrier, (a, lax.rem(b + o, gy)))
    for o in peers(gx):
        signal(barrier, (lax.rem(a + o, gx), b))

    up = [(a + 1, b), (a - 1, b), (a, b + 1), (a, b - 1)]
    has_up = [a < gx - 1, a > 0, b < gy - 1, b > 0]
    down = [up[p ^ 1] for p in range(4)]
    has_down = [has_up[p ^ 1] for p in range(4)]
    corner = [(1, 1), (-1, -1), (1, -1), (-1, 1)]
    cdev = [(a + sx, b + sy) for sx, sy in corner]
    has_c = [
        jnp.logical_and(has_up[0 if sx > 0 else 1], has_up[2 if sy > 0 else 3]) for sx, sy in corner
    ]
    finish = []

    def send(copies, conds, wait):
        for p in (2, 3, 0, 1):
            @pl.when(conds[p])
            def _(p=p):
                for c in copies(p):
                    getattr(c, wait)()

    def trade(copies, to, fro):
        send(copies, to, "start")
        finish.append(lambda: send(copies, to, "wait_send"))
        return lambda: send(copies, fro, "wait_recv")

    def remote(src, dst, s, r, dev):
        return pltpu.make_async_remote_copy(
            src_ref=src, dst_ref=dst, send_sem=s, recv_sem=r, device_id=dev, device_id_type=MESH
        )

    wide_grid = 4 * max(cx, cy)

    def code(c, i, j):
        return (c * wide_grid + (i + cx)) * wide_grid + (j + cy)

    load_lists.wait()
    lists = lists_ref[...].astype(F32)
    columns = lists.T
    for p in range(4):
        count = 2 * hrows[p]
        q = fiota((1, count), 1)
        if p < 2:
            c = fdiv(q, 2 * cy)
            row = c * layer + (layer - 2 * cy) * (1 - p) + (q - c * 2 * cy)
        else:
            second = jnp.where(q >= comps * cx, 1.0, 0.0)
            row = (q - second * (comps * cx)) * cy + (cy - 2) * (3 - p) + second
        hit = jnp.broadcast_to(columns[:, (p ^ 1) : (p ^ 1) + 1], (ov, count)) == jnp.broadcast_to(row, (ov, count))
        near[p, :, :count] = jnp.where(hit, 1.0, 0.0).astype(BF16)

    lc = fdiv(lists, layer)
    li = fdiv(lists - lc * layer, cy)
    lj = lists - lc * layer - li * cy
    block = fdiv(fiota((1, 4 * ov), 1), ov)

    def in_line(x):
        return jnp.concatenate([x[(p ^ 1) : (p ^ 1) + 1] for p in range(4)], axis=1)

    sides = ((-1, 0), (1, 0), (0, -1), (0, 1))
    for p, (dx, dy) in enumerate(sides):
        line = in_line(code(lc, li + dx * cx, lj + dy * cy))
        qs[p, 0:1, :] = jnp.where(block == p, line, 0.0)
        qs[p, 1:2, :] = line

    load_res.wait()

    def gather(t, src):
        for p in range(4):
            if p < 2:
                skip = (layer - 2 * cy) * (1 - p)
                rows = [src[c * layer + skip : c * layer + skip + 2 * cy, :] for c in range(comps)]
            else:
                rows = [src[pl.ds((cy - 2) * (3 - p) + k, comps * cx, stride=cy), :] for k in range(2)]
            rows = jnp.concatenate(rows, axis=0).astype(BF16)
            outs[t, p * ov : (p + 1) * ov, :] = dot(near[p, :, : 2 * hrows[p]], rows).astype(BF16)

    gather(0, res_v)
    pl.semaphore_wait(barrier, gx + gy - 2)

    def start_margins(t):
        return trade(
            lambda p: [
                remote(outs.at[t, pl.ds(p * ov, ov)], sub.at[t, pl.ds(own + p * ov, ov)],
                       nsem_s.at[0, p], nsem_r.at[0, p], up[p]),
                remote(qs.at[p], qr.at[p], csem_s.at[0, p], csem_r.at[0, p], up[p]),
            ],
            has_up, has_down,
        )

    wait_margins = start_margins(0)
    has_cd = [has_c[p ^ 1] for p in range(4)]
    for o in peers(gy):
        signal(ready, (a, lax.rem(b + o, gy)))
    wait_raw = trade(
        lambda p: [
            remote(basis_hbm, ball.at[1 + p], csem_s.at[1, p], csem_r.at[1, p], up[p]),
            remote(crows_hbm, sall.at[1 + p], csem_s.at[2, p], csem_r.at[2, p], up[p]),
        ],
        has_up, has_down,
    )
    sub[0, :own, :] = res_v[...].astype(BF16)

    for p in range(4):
        @pl.when(jnp.logical_not(has_down[p]))
        def _(p=p):
            sub[0, own + p * ov : own + (p + 1) * ov, :] = jnp.zeros((ov, nv), BF16)
            ybuf[p * mrows : (p + 1) * mrows, :] = jnp.zeros((mrows, nv), BF16)
            msg2_r[p] = jnp.zeros(msg2_r.shape[1:], BF16)
            qr[p] = jnp.zeros(qr.shape[1:], F32)
            tr[p] = jnp.zeros(tr.shape[1:], F32)
            am_r[p * ov : (p + 1) * ov, :] = jnp.zeros((ov, kd), BF16)
            ball[1 + p] = jnp.zeros(ball.shape[1:], BF16)
            sall[1 + p] = jnp.zeros(sall.shape[1:], BF16)

        @pl.when(jnp.logical_not(has_cd[p]))
        def _(p=p):
            ybuf[ycorner + p * dr : ycorner + (p + 1) * dr, :] = jnp.zeros((dr, nv), BF16)
            drecv2[p * dr2 : (p + 1) * dr2, :] = jnp.zeros((dr2, nv), BF16)
            ball[5 + p] = jnp.zeros(ball.shape[1:], BF16)
            sall[5 + p] = jnp.zeros(sall.shape[1:], BF16)

    load_stiff.wait()
    r1 = fiota((layer, cy), 0)
    first = fdiv(r1, cy)
    mine = jnp.where(fiota((layer, cx), 1) == fdiv(fiota((layer, cx), 0), cy), 1.0, 0.0)
    spread = dot(mine, stiff_ref[...], precision=HIGH)
    spread = jnp.where(fiota((layer, cy), 1) == r1 - first * cy, spread, 0.0)
    diag[...] = jnp.broadcast_to(4.0 + jnp.sum(spread, axis=1, keepdims=True), (layer, nv))
    rr = fiota((layer, nv), 0)
    second = rr - fdiv(rr, cy) * cy
    m_lo[...] = jnp.where(second == 0.0, 0.0, 1.0)
    m_hi[...] = jnp.where(second == cy - 1.0, 0.0, 1.0)

    cells = jnp.where(fiota((layer, 4 * ov), 0) == in_line(li * cy + lj), 1.0, 0.0)
    at_cells = lax.dot_general(
        diag[...], cells, (((0,), (0,)), ((), ())), precision=HIGH, preferred_element_type=F32
    )[0:8]
    for p in range(4):
        ts[p] = jnp.where(jnp.broadcast_to(block, (8, 4 * ov)) == p, at_cells, 0.0)
    wait_t = trade(
        lambda p: [remote(ts.at[p], tr.at[p], csem_s.at[3, p], csem_r.at[3, p], up[p])], has_up, has_down
    )

    pl.semaphore_wait(ready, gy - 1)
    wait_raw_c = trade(
        lambda p: [
            remote(basis_hbm, ball.at[5 + p], rsem_s.at[0, p], rsem_r.at[0, p], cdev[p]),
            remote(crows_hbm, sall.at[5 + p], rsem_s.at[1, p], rsem_r.at[1, p], cdev[p]),
        ],
        has_c, has_cd,
    )

    def edge_cells(w, p, depth, outside):
        per = cy if p < 2 else cx
        c = fdiv(w, per)
        along = w - c * per
        size = cx if p < 2 else cy
        if outside:
            off = along * 0.0 + (-1.0 - depth, size + depth)[p % 2]
        else:
            off = along * 0.0 + (size - 1.0 - depth, 1.0 * depth)[p % 2]
        return (c, off, along, w < hrows[p]) if p < 2 else (c, along, off, w < hrows[p])

    def beside_cells(w, p):
        v = fdiv(w, 3 * comps)
        u = 1.0 - 2.0 * v
        c = fdiv(w - v * (3 * comps), 3)
        kk = w - v * (3 * comps) - 3 * c
        deep, far = jnp.where(kk == 1.0, 1.0, 0.0), jnp.where(kk == 2.0, 1.0, 0.0)
        size, size2 = (cx, cy) if p < 2 else (cy, cx)
        along = (size - 1.0 - deep) if p % 2 == 0 else deep
        out = jnp.where(v == 0.0, size2 + far, -1.0 - far)
        return (c, along, out, v < 2.0) if p < 2 else (c, out, along, v < 2.0)

    def corner_cells(w, sx, sy):
        ex, ey = (cx - 1.0 if sx > 0 else 0.0), (cy - 1.0 if sy > 0 else 0.0)
        ox, oy = (1.0 * cx if sx > 0 else -1.0), (1.0 * cy if sy > 0 else -1.0)
        g = fdiv(w, 2 * comps)
        depth = fdiv(g, 2)
        kind = g - 2 * depth
        c = fdiv(w - g * (2 * comps), 2)
        k = w - g * (2 * comps) - 2 * c
        i = jnp.where(kind == 0.0, ex - sx * depth, ox + sx * k)
        j = jnp.where(kind == 0.0, oy + sy * k, ey - sy * depth)
        w2 = w - 12 * comps
        c2 = fdiv(w2, 3)
        kk = w2 - 3 * c2
        tail = w2 >= 0.0
        i = jnp.where(tail, ex - sx * jnp.where(kk == 1.0, 1.0, 0.0), i)
        j = jnp.where(tail, ey - sy * jnp.where(kk == 2.0, 1.0, 0.0), j)
        return jnp.where(tail, c2, c), i, j, w < 15 * comps

    nowhere = -16.0 * wide_grid * wide_grid

    def coded(cell, dx=0, dy=0):
        c, i, j, real = cell
        return jnp.where(real, code(c, i - dx * cx, j - dy * cy), nowhere)

    def row_of(count):
        return fiota((1, count), 1)

    def deduped(cell, p):
        c, i, j, real = cell
        return (c, i, j, real if p < 2 else jnp.logical_and(real, jnp.logical_and(i > 0.0, i < cx - 1.0)))

    back_code = [code(lc, li, lj)[p : p + 1] for p in range(4)]
    edge_code = [coded(edge_cells(row_of(halo), p, 0, False)) for p in range(4)]
    deep_code = [[coded(edge_cells(row_of(halo), p, d, True)) for d in range(3)] for p in range(4)]
    beside_code = [coded(beside_cells(row_of(crows), p), -sides[p][0], -sides[p][1]) for p in range(4)]
    corner_code = [coded(corner_cells(row_of(dr), *corner[m]), *corner[m]) for m in range(4)]
    short_code = [coded(corner_cells(row_of(dr2), *corner[m]), *corner[m]) for m in range(4)]
    ycode[0:1, yedge:] = jnp.concatenate(
        [coded(deduped(edge_cells(row_of(halo), p, 0, False), p)) for p in range(4)], axis=1
    )
    line = []
    for p in range(4):
        line += [back_code[p]] + deep_code[p] + [beside_code[p]]
    line = jnp.concatenate(line + corner_code, axis=1)
    lines[...] = jnp.full(lines.shape, nowhere, F32)
    lines[0:1, : line.shape[1]] = line
    line = jnp.concatenate(back_code + [deep_code[p][0] for p in range(4)] + short_code, axis=1)
    lines[1:2, : line.shape[1]] = line

    def column_of(count):
        return fiota((count, 128), 0)

    rlist = [coded(corner_cells(column_of(dr2), *corner[m])) for m in range(4)]
    rlist += [coded(beside_cells(column_of(crows), p)) for p in range(4)]
    rlist += [coded(corner_cells(column_of(dr - dr2) + dr2, *corner[m])) for m in range(4)]
    rlist += [coded(edge_cells(column_of(halo), p, 0, True)) for p in range(4)]
    rowc[...] = jnp.concatenate(rlist, axis=0)

    def hits(rows, row):
        parts = []
        for at in range(0, row.shape[1], 128):
            piece = row[:, at : at + 128]
            parts.append(jnp.where(rows[:, : piece.shape[1]] == piece, 1.0, 0.0))
        return (jnp.concatenate(parts, axis=1) if len(parts) > 1 else parts[0]).astype(BF16)

    def adjacent(gap):
        return jnp.where(jnp.logical_or(gap == 1.0, gap == wide_grid), 1.0, 0.0)

    def coefficient(gap, weight):
        return jnp.where(gap == 0.0, -weight, adjacent(gap)).astype(BF16)

    gmat[...] = jnp.zeros(gmat.shape, BF16)
    first_rest = 4 * (dr2 + crows)
    gstat[...] = hits(rowc[first_rest:gpm, :], ycode[0:1, yedge:])

    rows = fiota((own, ov), 0)
    for h in range(2):
        two = [jnp.where(rows == lists[p : p + 1], 1.0, 0.0) for p in (2 * h, 2 * h + 1)]
        sel[:, 2 * ov * h : 2 * ov * (h + 1)] = jnp.concatenate(two, axis=1).astype(BF16)

    def layer_rows(ref, p, depth=0):
        if p >= 2:
            return ref[pl.ds(cy - 1 - depth if p == 2 else depth, comps * cx, stride=cy), :]
        skip = layer - cy - depth * cy if p == 0 else depth * cy
        return jnp.concatenate([ref[c * layer + skip : c * layer + skip + cy, :] for c in range(comps)], axis=0)

    def operate(x_ref, dst, src):
        zero = jnp.zeros((cy, nv), F32)
        for c in range(comps):
            at = pl.ds(c * layer, layer)
            x = x_ref[at, :]
            beside = jnp.concatenate([zero, x[:-cy]], axis=0) + jnp.concatenate([x[cy:], zero], axis=0)
            beside += pltpu.roll(x, 1, 0) * m_lo[...] + pltpu.roll(x, layer - 1, 0) * m_hi[...]
            value = beside - diag[...] * x
            dst[at, :] = value if src is None else src[at, :] + value

    def add_layers(dst, around):
        for c in range(comps):
            base = c * layer
            dst[base : base + cy, :] += around(0)[c * cy : (c + 1) * cy]
            dst[base + layer - cy : base + layer, :] += around(1)[c * cy : (c + 1) * cy]
        low = pl.ds(0, comps * cx, stride=cy)
        high = pl.ds(cy - 1, comps * cx, stride=cy)
        dst[low, :] = dst[low, :] + around(2)
        dst[high, :] = dst[high, :] + around(3)

    def ring_side(p):
        return ring[p * halo : p * halo + hrows[p], :]

    slot = b * gx + a

    def start_gather(t, cin):
        allbuf[t, slot] = cin.astype(BF16)
        here = allbuf.at[t, slot]
        rest = allbuf.at[t, pl.ds(0, n - 1)]
        gathering = remote(rest, rest, gs.at[t], gr.at[t], (to_a[0], to_b[1]))
        finish.append(gathering.wait_send)

        def go(chosen):
            each_other(lambda dev: remote(here, here, gs.at[t], gr.at[t], dev).start(), chosen)

        def arrived():
            gathering.wait_recv()
            return allbuf[t].astype(F32).reshape(kd, nv).astype(BF16)

        return go, arrived

    load_basis.wait()
    load_inv.wait()
    part = split(inv_v.at[:, pl.ds(0, own)], sub[0, :own, :])
    cpart = dot(basis_ref[:, :own], sub[0, :own, :])
    wait_margins()
    edge = sub[0, own:, :]
    go, arrived = start_gather(0, cpart + dot(basis_ref[:, own:], edge))
    go(0)
    q = (qr[0] + qr[1] + qr[2] + qr[3])[0:1]
    ycode[0:1, :yedge] = q
    tiles = (slice(0, 2 * ov), slice(2 * ov, 4 * ov))
    for tile in tiles:
        gmat[: 4 * dr2, tile] = hits(rowc[: 4 * dr2, :], q[:, tile])
        gmat[first_rest:gpm, tile] = hits(rowc[first_rest:gpm, :], q[:, tile])
    for h in range(2):
        at = slice(4 * dr2 + 2 * h * crows, 4 * dr2 + 2 * (h + 1) * crows)
        gmat[at, tiles[1 - h]] = hits(rowc[at, :], q[:, tiles[1 - h]])
    pmv[...] = part[own:] + dot(inv_v[own:, own:], edge)
    pm = pmv[...].astype(BF16)
    xs[...] = part[:own] + split(inv_v.at[pl.ds(0, own), pl.ds(own, 4 * ov)], edge)
    edges = jnp.concatenate([layer_rows(xs, p) for p in range(4)], axis=0).astype(BF16)
    made = split(gmat.at[pl.ds(0, gpm), :], pm)
    made_first = made[:first_rest].astype(BF16)
    made_rest = (made[first_rest:] + dot(gstat[...], edges)).astype(BF16)
    for p in range(4):
        msg_s[p, :ov, :] = pm[(p ^ 1) * ov : ((p ^ 1) + 1) * ov]
        msg_s[p, ov : ov + halo, :] = edges[p * halo : (p + 1) * halo]
        for d in range(1, 3):
            msg_s[p, ov + d * halo : ov + d * halo + hrows[p], :] = layer_rows(xs, p, d).astype(BF16)
        msg_s[p, ov + 3 * halo :, :] = made_first[4 * dr2 + p * crows : 4 * dr2 + (p + 1) * crows]
        dsend[p, :dr2, :] = made_first[p * dr2 : (p + 1) * dr2]
        dsend[p, dr2:, :] = made_rest[p * (dr - dr2) : (p + 1) * (dr - dr2)]
    wait_corners = trade(
        lambda p: [remote(dsend.at[p], ybuf.at[pl.ds(ycorner + p * dr, dr)], dsem_s.at[0, p], dsem_r.at[0, p], cdev[p])],
        has_c, has_cd,
    )
    wait_back = trade(
        lambda p: [remote(msg_s.at[p], ybuf.at[pl.ds(p * mrows, mrows)], nsem_s.at[1, p], nsem_r.at[1, p], up[p])],
        has_up, has_down,
    )
    go(1)
    for h in range(2):
        at = slice(gpm + 2 * h * halo, gpm + 2 * (h + 1) * halo)
        gmat[at, tiles[h]] = hits(rowc[at, :], q[:, tiles[h]])

    load_pmap.wait()
    load_crows.wait()
    wait_raw()
    wait_raw_c()
    ball[0] = basis_ref[...]
    sall[0] = crows_ref[...]
    spare = lanes - nine * kw
    stacked = jnp.concatenate([ball[...].astype(F32).reshape(nine * kw, -1), jnp.zeros((spare, own + 4 * ov), F32)], axis=0)
    bt[...] = stacked.T
    group = fdiv(fiota((1, lanes), 1), kw)

    def of(e, value):
        return jnp.where(group == e, value, 0.0)

    def margin(k):
        return bt[own + k * ov : own + (k + 1) * ov, :]

    theirs = jnp.concatenate([of(1.0 + p, margin(p ^ 1)) for p in range(4)], axis=0).astype(BF16)
    bextf[...] = of(0.0, bt[:own, :]) + dot(sel[...], theirs)
    around_b = jnp.concatenate([of(1.0 + p, layer_rows(bt, p)) for p in range(4)], axis=0)
    around_b += dot(gmat[gpm:, :], of(0.0, bt[own:, :]).astype(BF16))
    for m, (sx, sy) in enumerate(corner):
        ky, py = (0 if sx < 0 else 1), (3 if sy < 0 else 2)
        kx, px = (2 if sy < 0 else 3), (1 if sx < 0 else 0)
        pair = [qr[py, 1:2, ky * ov : (ky + 1) * ov], qr[px, 1:2, kx * ov : (kx + 1) * ov]]
        oh = hits(rowc[gpm:, :], jnp.concatenate(pair, axis=1))
        around_b += dot(oh, of(5.0 + m, jnp.concatenate([margin(ky), margin(kx)], axis=0)).astype(BF16))
    edge2[: 4 * halo, :] = around_b
    operate(bextf, abf, None)
    add_layers(abf, lambda p: edge2[p * halo : p * halo + hrows[p], :])
    bextb[...] = bextf[...].astype(BF16)
    abextb[...] = abf[...].astype(BF16)
    gather(1, abf)

    wide = min(kd, 256)
    pmf = jnp.broadcast_to(pmap_ref[...].astype(F32), (8, n))
    spare_s = jnp.zeros((spare, kd), F32)
    stacked_s = jnp.concatenate([sall[...].astype(F32).reshape(nine * kw, kd), spare_s], axis=0).astype(BF16)

    def order(c, _):
        q = fiota((1, wide), 1) + (c * wide).astype(F32)
        at_slot = fdiv(q, kw)
        slab = fdiv(at_slot, gx)
        dev = (at_slot - slab * gx) * gy + slab
        pick = jnp.where(fiota((n, wide), 0) == dev, 1.0, 0.0)
        place = dot(pmf, pick, precision=HIGH)[0:1] * kw + (q - at_slot * kw)
        perm = jnp.where(fiota((kd, wide), 0) == place, 1.0, 0.0).astype(BF16)
        at = pl.ds(pl.multiple_of(c * wide, wide), wide)
        sext[:, at] = dot(stacked_s, perm).astype(BF16)
        am_s[:, at] = dot(outs[1], sext[:, at]).astype(BF16)
        return 0

    lax.fori_loop(jnp.int32(0), jnp.int32(kd // wide), order, 0)
    wait_am = trade(
        lambda p: [remote(am_s.at[pl.ds(p * ov, ov)], am_r.at[pl.ds(p * ov, ov)], csem_s.at[4, p], csem_r.at[4, p], up[p])],
        has_up, has_down,
    )

    def as_column(line):
        return jnp.broadcast_to(jnp.broadcast_to(line, (8, 4 * ov)).T[:, 0:1], (4 * ov, 128))

    qb[...] = as_column(ycode[0:1, :yedge])
    wait_t()
    sb[...] = as_column((tr[0] + tr[1] + tr[2] + tr[3])[0:1])
    pm = pmv[...].astype(BF16)
    for h in range(0, cmarg.shape[1], 128):
        gap = jnp.abs(lines[0:1, h : h + 128] - qb[...])
        cmarg[:, h : h + 128] = coefficient(gap, sb[...])
    for p in range(4):
        at = slice(p * ov, (p + 1) * ov)
        line = jnp.concatenate([ycode[0:1, at], edge_code[p ^ 1]], axis=1)
        mc[p] = adjacent(jnp.abs(line - qb[at, : ov + halo])).astype(BF16)
        near_edge = jnp.concatenate([pm[at], msg_s[p ^ 1, ov : ov + halo, :]], axis=0)
        known = sub[0, own + p * ov : own + (p + 1) * ov, :].astype(F32)
        edge2[at, :] = known + dot(mc[p], near_edge) - sb[at, :] * pmv[at, :]

    rc = fiota((layer, 128), 0)
    ri = fdiv(rc, cy)
    here_code = code(0.0, ri, rc - ri * cy)

    def fill_own(c, _):
        at = pl.ds(pl.multiple_of(c * layer, layer), layer)
        shift = c.astype(F32) * (wide_grid * wide_grid)
        for h in range(0, cown.shape[1], 128):
            gap = jnp.abs(here_code + shift - lines[1:2, h : h + 128])
            cown[at, h : h + 128] = coefficient(gap, diag[:, :128])
        return 0

    lax.fori_loop(jnp.int32(0), jnp.int32(comps), fill_own, 0)

    r = fiota((2 * comps * cx, own), 0)
    lower = jnp.where(r >= comps * cx, 1.0, 0.0)
    wanted_row = (r - lower * (comps * cx)) * cy + (cy - 1) * (1.0 - lower)
    pick = jnp.where(fiota((2 * comps * cx, own), 1) == wanted_row, 1.0, 0.0).astype(BF16)
    inve[...] = dot(pick, inv_v[:own, :]).astype(BF16)

    operate(xs, mid, res_v)
    ring[...] = dot(gmat[gpm:, :], pm)
    add_layers(mid, ring_side)

    wait_am()
    gathered = arrived()
    cout = dot(sext[...], gathered).astype(BF16)
    edge2[: 4 * ov, :] += dot(am_r[...], gathered)
    mid[...] += dot(abextb[...], cout)

    wait_back()
    wait_corners()

    def piece(p, at, count):
        return ybuf[p * mrows + at : p * mrows + at + count, :]

    pieces = 4 * (mrows + dr)
    sub[1, own:, :] = (edge2[: 4 * ov, :] + dot(cmarg[:, :pieces], ybuf[...])).astype(BF16)
    backs = jnp.concatenate([piece(p, 0, ov) for p in range(4)], axis=0)
    rest = [piece(p, ov, halo) for p in range(4)]
    rest += [ybuf[ycorner + m * dr : ycorner + m * dr + dr2, :] for m in range(4)]
    sol_ref[...] = split(cown, jnp.concatenate([backs] + rest, axis=0))
    value = mid[...] + sol_ref[...]
    mid[...] = value
    sub[1, :own, :] = value.astype(BF16)

    go, arrived = start_gather(1, dot(basis_ref[...], sub[1]))
    go(0)
    lhs = [inv_v[own:, :]]
    lhs += [inv_v[c * layer + layer - cy : (c + 1) * layer, :] for c in range(comps)]
    lhs += [inv_v[c * layer : c * layer + cy, :] for c in range(comps)]
    made = split(jnp.concatenate(lhs + [inve[...]], axis=0), sub[1])
    pm = made[: 4 * ov].astype(BF16)
    at = 4 * ov
    for p in range(4):
        msg2_s[p, :ov, :] = pm[(p ^ 1) * ov : ((p ^ 1) + 1) * ov]
        msg2_s[p, ov : ov + hrows[p], :] = made[at : at + hrows[p]].astype(BF16)
        at += hrows[p]
    dsend2[...] = dot(gmat[: 4 * dr2, :], pm).astype(BF16)
    wait_corners = trade(
        lambda p: [remote(dsend2.at[pl.ds(p * dr2, dr2)], drecv2.at[pl.ds(p * dr2, dr2)], dsem_s.at[1, p], dsem_r.at[1, p], cdev[p])],
        has_c, has_cd,
    )
    wait_back = trade(
        lambda p: [remote(msg2_s.at[p], msg2_r.at[p], nsem_s.at[2, p], nsem_r.at[2, p], up[p])],
        has_up, has_down,
    )
    go(1)
    sol_ref[...] = xs[...] + dot(bextb[...], cout)
    sol_ref[...] += dot(sel[...], backs)
    xs[...] = split(inv_v.at[pl.ds(0, own), :], sub[1])
    sol_ref[...] += xs[...]
    operate(xs, fin_ref, mid)
    ring[...] = dot(gmat[gpm:, :], pm)
    add_layers(fin_ref, ring_side)
    wait_back()
    wait_corners()
    backs = jnp.concatenate([msg2_r[p, :ov, :] for p in range(4)], axis=0)
    rest = jnp.concatenate([msg2_r[p, ov:, :] for p in range(4)] + [drecv2[...]], axis=0)
    both = jnp.concatenate([backs, rest], axis=0)
    xs[...] = split(cown, both)
    fin_ref[...] += xs[...]
    sol_ref[...] += split(sel, backs)
    gathered = arrived()
    cout = dot(sext[...], gathered).astype(BF16)
    fin_ref[...] += split(abextb, cout)
    sol_ref[...] += split(bextb, cout)
    for end in finish:
        end()


def emit(sol_ref, fin_ref, sol_hbm, fin_hbm, sem):
    pairs = ((sol_ref, sol_hbm), (fin_ref, fin_hbm))
    copies = [pltpu.make_async_copy(x, y, sem.at[k]) for k, (x, y) in enumerate(pairs)]
    for c in copies:
        c.start()
    for c in copies:
        c.wait()


def solution(mesh):
    gx, gy = mesh.shape["gx"], mesh.shape["gy"]

    def per_device(residual, stiffness, local_inverse, coarse_basis, coarse_rows, send_rows, partition_map):
        comps, cx, cy, nv = residual.shape
        own, layer = comps * cx * cy, cx * cy
        m = local_inverse.shape[-1]
        ov = send_rows.shape[-1]
        kw, kd = coarse_rows.shape[-2:]
        halo = comps * max(cx, cy)
        def whole(count, of):
            return -(-count // of) * of

        lanes = whole(9 * kw, 128)
        dr, dr2 = whole(15 * comps, 16), whole(4 * comps, 16)
        crows = whole(6 * comps, 16)
        mrows = ov + 3 * halo + crows
        width = whole(4 * (mrows + dr), 128)
        grows = 4 * (halo + crows + dr)
        vm = pl.BlockSpec(memory_space=pltpu.VMEM)
        anywhere = pl.BlockSpec(memory_space=pl.ANY)
        dma = pltpu.SemaphoreType.DMA
        out = pl.pallas_call(
            functools.partial(kernel, gx, gy, (comps, cx, cy, nv)),
            out_shape=[pltpu.VMEM((own, nv), F32)] * 2,
            in_specs=[anywhere] * 7,
            out_specs=[vm, vm],
            scratch_shapes=[
                pltpu.VMEM((own, nv), F32),
                pltpu.VMEM((cx, cy), F32),
                pltpu.VMEM((m, m), BF16),
                pltpu.VMEM((kw, m), BF16),
                pltpu.VMEM((kw, kd), BF16),
                pltpu.VMEM((4, ov), jnp.int32),
                pltpu.VMEM((1, gx * gy), jnp.int32),
                pltpu.VMEM((2, m, nv), BF16),
                pltpu.VMEM((own, 4 * ov), BF16),
                pltpu.VMEM((4, ov, 2 * halo), BF16),
                pltpu.VMEM((2, 4 * ov, nv), BF16),
                pltpu.VMEM((4 * (mrows + dr), nv), BF16),
                pltpu.VMEM((8, 4 * ov + 4 * halo), F32),
                pltpu.VMEM((8, width), F32),
                pltpu.VMEM((grows, 128), F32),
                pltpu.VMEM((4 * ov, 128), F32),
                pltpu.VMEM((4 * ov, 128), F32),
                pltpu.VMEM((grows, 4 * ov), BF16),
                pltpu.VMEM((4 * (dr - dr2), 4 * halo), BF16),
                pltpu.VMEM((own, 4 * (ov + halo + dr2)), BF16),
                pltpu.VMEM((4 * ov, width), BF16),
                pltpu.VMEM((4, ov, ov + halo), BF16),
                pltpu.VMEM((2 * comps * cx, m), BF16),
                pltpu.VMEM((4 * ov, nv), F32),
                pltpu.VMEM((4 * halo, nv), F32),
                pltpu.VMEM((4, mrows, nv), BF16),
                pltpu.VMEM((4, dr, nv), BF16),
                pltpu.VMEM((4, ov + halo, nv), BF16),
                pltpu.VMEM((4, ov + halo, nv), BF16),
                pltpu.VMEM((4 * dr2, nv), BF16),
                pltpu.VMEM((4 * dr2, nv), BF16),
                pltpu.VMEM((4, 8, 4 * ov), F32),
                pltpu.VMEM((4, 8, 4 * ov), F32),
                pltpu.VMEM((4, 8, 4 * ov), F32),
                pltpu.VMEM((4, 8, 4 * ov), F32),
                pltpu.VMEM((2, gx * gy, kw, nv), BF16),
                pltpu.VMEM((9, kw, m), BF16),
                pltpu.VMEM((9, kw, kd), BF16),
                pltpu.VMEM((lanes, kd), BF16),
                pltpu.VMEM((m, lanes), F32),
                pltpu.VMEM((own, lanes), F32),
                pltpu.VMEM((own, lanes), F32),
                pltpu.VMEM((own, lanes), BF16),
                pltpu.VMEM((own, lanes), BF16),
                pltpu.VMEM((4 * ov, kd), BF16),
                pltpu.VMEM((4 * ov, kd), BF16),
                pltpu.VMEM((max(4 * ov, 4 * halo), nv), F32),
                pltpu.VMEM((layer, nv), F32),
                pltpu.VMEM((layer, nv), F32),
                pltpu.VMEM((layer, nv), F32),
                pltpu.VMEM((own, nv), F32),
                pltpu.VMEM((own, nv), F32),
                dma((7,)),
                pltpu.SemaphoreType.REGULAR,
                dma((3, 4)),
                dma((3, 4)),
                dma((2, 4)),
                dma((2, 4)),
                dma((5, 4)),
                dma((5, 4)),
                dma((2, 4)),
                dma((2, 4)),
                dma((2,)),
                dma((2,)),
            ],
            compiler_params=pltpu.CompilerParams(collective_id=0, has_side_effects=True),
        )(
            residual.reshape(own, nv),
            stiffness,
            local_inverse[0, 0],
            coarse_basis[0, 0],
            coarse_rows[0, 0],
            send_rows[0, 0],
            partition_map.reshape(1, -1),
        )
        out = pl.pallas_call(
            emit,
            out_shape=[jax.ShapeDtypeStruct((own, nv), F32)] * 2,
            in_specs=[vm, vm],
            out_specs=[anywhere, anywhere],
            scratch_shapes=[dma((2,))],
        )(*[pltpu.with_memory_space_constraint(o, pltpu.VMEM) for o in out])
        return tuple(o.reshape(residual.shape) for o in out)

    placed = (
        P(None, "gx", "gy", None),
        P("gx", "gy"),
        P("gx", "gy", None, None),
        P("gx", "gy", None, None),
        P("gx", "gy", None, None),
        P("gx", "gy", None, None),
        P(),
    )
    return jax.shard_map(
        per_device,
        mesh=mesh,
        in_specs=placed,
        out_specs=(P(None, "gx", "gy", None), P(None, "gx", "gy", None)),
        check_vma=False,
    )
```

```python
import functools

import jax
import jax.numpy as jnp
from jax import lax
from jax.experimental import pallas as pl
from jax.experimental.pallas import tpu as pltpu
from jax.sharding import PartitionSpec as P

MESH = pl.DeviceIdType.MESH
F32 = jnp.float32
BF16 = jnp.bfloat16
HIGH = lax.Precision.HIGHEST


def dot(x, y, **kw):
    return jnp.dot(x, y, preferred_element_type=F32, **kw)


def split(x, y):
    cut = x.shape[0] // 32 * 16
    return jnp.concatenate([dot(x[:cut, :], y), dot(x[cut:, :], y)], axis=0)


def tdot(x, y):
    return lax.dot_general(x, y, (((0,), (0,)), ((), ())), preferred_element_type=F32)


def fiota(shape, axis):
    return lax.broadcasted_iota(jnp.int32, shape, axis).astype(F32)


def fdiv(x, n):
    return jnp.floor((x + 0.5) * (1.0 / n))


def kernel(
    gx, gy, dims,
    res_hbm, stiff_hbm, inv_hbm, basis_hbm, crows_hbm, lists_hbm, pmap_hbm,
    sol_ref, fin_ref,
    res_v, stiff_ref, inv_v, basis_ref, crows_ref, lists_ref, pmap_ref, sub, sel, near, outs,
    ybuf, ycode, lines, rowc, qb, sb, gmat, gstat, cown, cmarg, mc, inve, pmv, ring, msg_s, dsend,
    msg2_s, msg2_r, dsend2, drecv2,
    qs, qr, ts, tr, allbuf, ball, sall, sext, bt, bextf, abf, bextb, abextb, am_s, am_r, edge2,
    diag, m_lo, m_hi, xs, mid,
    lsem, ready, nsem_s, nsem_r, dsem_s, dsem_r, csem_s, csem_r, rsem_s, rsem_r, gs, gr,
):
    comps, cx, cy, nv = dims
    halo = comps * max(cx, cy)
    hrows = (comps * cy, comps * cy, comps * cx, comps * cx)
    own = comps * cx * cy
    layer = cx * cy
    ov = lists_ref.shape[1]
    kw, kd = crows_ref.shape
    n = gx * gy
    mrows = msg_s.shape[1]
    crows = mrows - ov - 3 * halo
    dr, dr2 = dsend.shape[1], dsend2.shape[0] // 4
    yedge = 4 * ov
    ycorner = 4 * mrows
    gpm = 4 * (dr + crows)
    nine = ball.shape[0]
    lanes = bextf.shape[1]
    a = lax.axis_index("gx")
    b = lax.axis_index("gy")

    wanted = [
        (lists_hbm, lists_ref), (res_hbm, res_v), (pmap_hbm, pmap_ref), (crows_hbm, crows_ref),
        (basis_hbm, basis_ref), (stiff_hbm, stiff_ref), (inv_hbm, inv_v),
    ]
    loads = [pltpu.make_async_copy(x, y, lsem.at[k]) for k, (x, y) in enumerate(wanted)]
    load_lists, load_res, load_pmap, load_crows, load_basis, load_stiff, load_inv = loads
    for load in loads:
        load.start()

    def flip(x, k):
        y, bit = x, 1
        while bit <= k:
            if k & bit:
                y = y + bit * (1 - 2 * lax.rem(lax.div(x, bit), 2))
            bit *= 2
        return y

    paired = gx & (gx - 1) == 0 and gy & (gy - 1) == 0
    others = [(i, j) for i in range(gx) for j in range(gy) if i or j]
    if paired:
        others.sort(key=lambda o: -((o[0] >> 1) + bin(o[1]).count("1") + 0.4 * (o[0] & 1)))
        to_a = [flip(a, i) for i in range(gx)]
        to_b = [flip(b, j) for j in range(gy)]
    else:
        to_a = [lax.rem(a + i, gx) for i in range(gx)]
        to_b = [lax.rem(b + j, gy) for j in range(gy)]

    half = len(others) // 2

    def each_other(act, chosen=None):
        if n <= 64:
            for i, j in others if chosen is None else (others[:half], others[half:])[chosen]:
                act((to_a[i], to_b[j]))
            return
        if chosen == 1:
            return

        def row(i, _):
            ai = lax.rem(a + i, gx)
            for j in range(1, gy):
                act((ai, lax.rem(b + j, gy)))
            pl.when(i > 0)(lambda: act((ai, b)))
            return 0

        lax.fori_loop(jnp.int32(0), jnp.int32(gx), row, 0)

    barrier = pltpu.get_barrier_semaphore()

    def peers(size):
        return sorted(range(1, size), key=lambda o: min(o, size - o))

    def signal(sem, dev):
        pl.semaphore_signal(sem, inc=1, device_id=dev, device_id_type=MESH)

    for o in peers(gy):
        signal(barrier, (a, lax.rem(b + o, gy)))
    for o in peers(gx):
        signal(barrier, (lax.rem(a + o, gx), b))

    up = [(a + 1, b), (a - 1, b), (a, b + 1), (a, b - 1)]
    has_up = [a < gx - 1, a > 0, b < gy - 1, b > 0]
    down = [up[p ^ 1] for p in range(4)]
    has_down = [has_up[p ^ 1] for p in range(4)]
    corner = [(1, 1), (-1, -1), (1, -1), (-1, 1)]
    cdev = [(a + sx, b + sy) for sx, sy in corner]
    has_c = [
        jnp.logical_and(has_up[0 if sx > 0 else 1], has_up[2 if sy > 0 else 3]) for sx, sy in corner
    ]
    finish = []

    for p in range(4):
        pl.when(has_c[p])(lambda p=p: signal(barrier, cdev[p]))

    def send(copies, conds, wait):
        for p in (2, 3, 0, 1):
            @pl.when(conds[p])
            def _(p=p):
                for c in copies(p):
                    getattr(c, wait)()

    def trade(copies, to, fro):
        send(copies, to, "start")
        finish.append(lambda: send(copies, to, "wait_send"))
        return lambda: send(copies, fro, "wait_recv")

    def remote(src, dst, s, r, dev):
        return pltpu.make_async_remote_copy(
            src_ref=src, dst_ref=dst, send_sem=s, recv_sem=r, device_id=dev, device_id_type=MESH
        )

    wide_grid = 4 * max(cx, cy)

    def code(c, i, j):
        return (c * wide_grid + (i + cx)) * wide_grid + (j + cy)

    load_lists.wait()
    lists = lists_ref[...].astype(F32)
    columns = lists.T
    for p in range(4):
        count = 2 * hrows[p]
        q = fiota((1, count), 1)
        if p < 2:
            c = fdiv(q, 2 * cy)
            row = c * layer + (layer - 2 * cy) * (1 - p) + (q - c * 2 * cy)
        else:
            second = jnp.where(q >= comps * cx, 1.0, 0.0)
            row = (q - second * (comps * cx)) * cy + (cy - 2) * (3 - p) + second
        hit = jnp.broadcast_to(columns[:, (p ^ 1) : (p ^ 1) + 1], (ov, count)) == jnp.broadcast_to(row, (ov, count))
        near[p, :, :count] = jnp.where(hit, 1.0, 0.0).astype(BF16)

    lc = fdiv(lists, layer)
    li = fdiv(lists - lc * layer, cy)
    lj = lists - lc * layer - li * cy
    block = fdiv(fiota((1, 4 * ov), 1), ov)

    def in_line(x):
        return jnp.concatenate([x[(p ^ 1) : (p ^ 1) + 1] for p in range(4)], axis=1)

    sides = ((-1, 0), (1, 0), (0, -1), (0, 1))
    for p, (dx, dy) in enumerate(sides):
        line = in_line(code(lc, li + dx * cx, lj + dy * cy))
        qs[p, 0:1, :] = jnp.where(block == p, line, 0.0)
        qs[p, 1:2, :] = line

    load_res.wait()

    def gather(t, src):
        for p in range(4):
            if p < 2:
                skip = (layer - 2 * cy) * (1 - p)
                rows = [src[c * layer + skip : c * layer + skip + 2 * cy, :] for c in range(comps)]
            else:
                rows = [src[pl.ds((cy - 2) * (3 - p) + k, comps * cx, stride=cy), :] for k in range(2)]
            rows = jnp.concatenate(rows, axis=0).astype(BF16)
            outs[t, p * ov : (p + 1) * ov, :] = dot(near[p, :, : 2 * hrows[p]], rows).astype(BF16)

    gather(0, res_v)
    met = gx + gy - 2 + sum(c.astype(jnp.int32) for c in has_c)
    pl.semaphore_wait(barrier, met)

    def start_margins(t):
        return trade(
            lambda p: [
                remote(outs.at[t, pl.ds(p * ov, ov)], sub.at[t, pl.ds(own + p * ov, ov)],
                       nsem_s.at[0, p], nsem_r.at[0, p], up[p]),
                remote(qs.at[p], qr.at[p], csem_s.at[0, p], csem_r.at[0, p], up[p]),
            ],
            has_up, has_down,
        )

    wait_margins = start_margins(0)
    has_cd = [has_c[p ^ 1] for p in range(4)]
    for o in peers(gy):
        signal(ready, (a, lax.rem(b + o, gy)))
    load_basis.wait()
    load_crows.wait()
    wait_raw = trade(
        lambda p: [
            remote(basis_ref, ball.at[1 + p], csem_s.at[1, p], csem_r.at[1, p], up[p]),
            remote(crows_ref, sall.at[1 + p], csem_s.at[2, p], csem_r.at[2, p], up[p]),
        ],
        has_up, has_down,
    )
    wait_raw_c = trade(
        lambda p: [
            remote(basis_ref.at[:, pl.ds(own, 4 * ov)], ball.at[5 + p, :, pl.ds(own, 4 * ov)], rsem_s.at[0, p], rsem_r.at[0, p], cdev[p]),
            remote(crows_ref, sall.at[5 + p], rsem_s.at[1, p], rsem_r.at[1, p], cdev[p]),
        ],
        has_c, has_cd,
    )
    sub[0, :own, :] = res_v[...].astype(BF16)

    for p in range(4):
        @pl.when(jnp.logical_not(has_down[p]))
        def _(p=p):
            sub[0, own + p * ov : own + (p + 1) * ov, :] = jnp.zeros((ov, nv), BF16)
            ybuf[p * mrows : (p + 1) * mrows, :] = jnp.zeros((mrows, nv), BF16)
            msg2_r[p] = jnp.zeros(msg2_r.shape[1:], BF16)
            qr[p] = jnp.zeros(qr.shape[1:], F32)
            tr[p] = jnp.zeros(tr.shape[1:], F32)
            am_r[p * ov : (p + 1) * ov, :] = jnp.zeros((ov, kd), BF16)
            ball[1 + p] = jnp.zeros(ball.shape[1:], BF16)
            sall[1 + p] = jnp.zeros(sall.shape[1:], BF16)

        @pl.when(jnp.logical_not(has_cd[p]))
        def _(p=p):
            ybuf[ycorner + p * dr : ycorner + (p + 1) * dr, :] = jnp.zeros((dr, nv), BF16)
            drecv2[p * dr2 : (p + 1) * dr2, :] = jnp.zeros((dr2, nv), BF16)
            ball[5 + p, :, own:] = jnp.zeros((kw, 4 * ov), BF16)
            sall[5 + p] = jnp.zeros(sall.shape[1:], BF16)

    for p in range(4):
        ball[5 + p, :, :own] = jnp.zeros((kw, own), BF16)

    load_stiff.wait()
    r1 = fiota((layer, cy), 0)
    first = fdiv(r1, cy)
    mine = jnp.where(fiota((layer, cx), 1) == fdiv(fiota((layer, cx), 0), cy), 1.0, 0.0)
    spread = dot(mine, stiff_ref[...], precision=HIGH)
    spread = jnp.where(fiota((layer, cy), 1) == r1 - first * cy, spread, 0.0)
    diag[...] = jnp.broadcast_to(4.0 + jnp.sum(spread, axis=1, keepdims=True), (layer, nv))
    rr = fiota((layer, nv), 0)
    second = rr - fdiv(rr, cy) * cy
    m_lo[...] = jnp.where(second == 0.0, 0.0, 1.0)
    m_hi[...] = jnp.where(second == cy - 1.0, 0.0, 1.0)

    cells = jnp.where(fiota((layer, 4 * ov), 0) == in_line(li * cy + lj), 1.0, 0.0)
    at_cells = lax.dot_general(
        diag[...], cells, (((0,), (0,)), ((), ())), precision=HIGH, preferred_element_type=F32
    )[0:8]
    for p in range(4):
        ts[p] = jnp.where(jnp.broadcast_to(block, (8, 4 * ov)) == p, at_cells, 0.0)
    wait_t = trade(
        lambda p: [remote(ts.at[p], tr.at[p], csem_s.at[3, p], csem_r.at[3, p], up[p])], has_up, has_down
    )

    def edge_cells(w, p, depth, outside):
        per = cy if p < 2 else cx
        c = fdiv(w, per)
        along = w - c * per
        size = cx if p < 2 else cy
        if outside:
            off = along * 0.0 + (-1.0 - depth, size + depth)[p % 2]
        else:
            off = along * 0.0 + (size - 1.0 - depth, 1.0 * depth)[p % 2]
        return (c, off, along, w < hrows[p]) if p < 2 else (c, along, off, w < hrows[p])

    def beside_cells(w, p):
        v = fdiv(w, 3 * comps)
        u = 1.0 - 2.0 * v
        c = fdiv(w - v * (3 * comps), 3)
        kk = w - v * (3 * comps) - 3 * c
        deep, far = jnp.where(kk == 1.0, 1.0, 0.0), jnp.where(kk == 2.0, 1.0, 0.0)
        size, size2 = (cx, cy) if p < 2 else (cy, cx)
        along = (size - 1.0 - deep) if p % 2 == 0 else deep
        out = jnp.where(v == 0.0, size2 + far, -1.0 - far)
        return (c, along, out, v < 2.0) if p < 2 else (c, out, along, v < 2.0)

    def corner_cells(w, sx, sy):
        ex, ey = (cx - 1.0 if sx > 0 else 0.0), (cy - 1.0 if sy > 0 else 0.0)
        ox, oy = (1.0 * cx if sx > 0 else -1.0), (1.0 * cy if sy > 0 else -1.0)
        g = fdiv(w, 2 * comps)
        depth = fdiv(g, 2)
        kind = g - 2 * depth
        c = fdiv(w - g * (2 * comps), 2)
        k = w - g * (2 * comps) - 2 * c
        i = jnp.where(kind == 0.0, ex - sx * depth, ox + sx * k)
        j = jnp.where(kind == 0.0, oy + sy * k, ey - sy * depth)
        w2 = w - 12 * comps
        c2 = fdiv(w2, 3)
        kk = w2 - 3 * c2
        tail = w2 >= 0.0
        i = jnp.where(tail, ex - sx * jnp.where(kk == 1.0, 1.0, 0.0), i)
        j = jnp.where(tail, ey - sy * jnp.where(kk == 2.0, 1.0, 0.0), j)
        return jnp.where(tail, c2, c), i, j, w < 15 * comps

    nowhere = -16.0 * wide_grid * wide_grid

    def coded(cell, dx=0, dy=0):
        c, i, j, real = cell
        return jnp.where(real, code(c, i - dx * cx, j - dy * cy), nowhere)

    def row_of(count):
        return fiota((1, count), 1)

    def deduped(cell, p):
        c, i, j, real = cell
        return (c, i, j, real if p < 2 else jnp.logical_and(real, jnp.logical_and(i > 0.0, i < cx - 1.0)))

    back_code = [code(lc, li, lj)[p : p + 1] for p in range(4)]
    edge_code = [coded(edge_cells(row_of(halo), p, 0, False)) for p in range(4)]
    deep_code = [[coded(edge_cells(row_of(halo), p, d, True)) for d in range(3)] for p in range(4)]
    beside_code = [coded(beside_cells(row_of(crows), p), -sides[p][0], -sides[p][1]) for p in range(4)]
    corner_code = [coded(corner_cells(row_of(dr), *corner[m]), *corner[m]) for m in range(4)]
    short_code = [coded(corner_cells(row_of(dr2), *corner[m]), *corner[m]) for m in range(4)]
    ycode[0:1, yedge:] = jnp.concatenate(
        [coded(deduped(edge_cells(row_of(halo), p, 0, False), p)) for p in range(4)], axis=1
    )
    line = []
    for p in range(4):
        line += [back_code[p]] + deep_code[p] + [beside_code[p]]
    line = jnp.concatenate(line + corner_code, axis=1)
    lines[...] = jnp.full(lines.shape, nowhere, F32)
    lines[0:1, : line.shape[1]] = line
    line = jnp.concatenate(back_code + [deep_code[p][0] for p in range(4)] + short_code, axis=1)
    lines[1:2, : line.shape[1]] = line

    def column_of(count):
        return fiota((count, 128), 0)

    rlist = [coded(corner_cells(column_of(dr2), *corner[m])) for m in range(4)]
    rlist += [coded(beside_cells(column_of(crows), p)) for p in range(4)]
    rlist += [coded(corner_cells(column_of(dr - dr2) + dr2, *corner[m])) for m in range(4)]
    rlist += [coded(edge_cells(column_of(halo), p, 0, True)) for p in range(4)]
    rowc[...] = jnp.concatenate(rlist, axis=0)

    def hits(rows, row):
        parts = []
        for at in range(0, row.shape[1], 128):
            piece = row[:, at : at + 128]
            parts.append(jnp.where(rows[:, : piece.shape[1]] == piece, 1.0, 0.0))
        return (jnp.concatenate(parts, axis=1) if len(parts) > 1 else parts[0]).astype(BF16)

    def adjacent(gap):
        return jnp.where(jnp.logical_or(gap == 1.0, gap == wide_grid), 1.0, 0.0)

    def coefficient(gap, weight):
        return jnp.where(gap == 0.0, -weight, adjacent(gap)).astype(BF16)

    gmat[...] = jnp.zeros(gmat.shape, BF16)
    first_rest = 4 * (dr2 + crows)
    gstat[...] = hits(rowc[first_rest:gpm, :], ycode[0:1, yedge:])

    rows = fiota((own, ov), 0)
    for h in range(2):
        two = [jnp.where(rows == lists[p : p + 1], 1.0, 0.0) for p in (2 * h, 2 * h + 1)]
        sel[:, 2 * ov * h : 2 * ov * (h + 1)] = jnp.concatenate(two, axis=1).astype(BF16)

    def layer_rows(ref, p, depth=0):
        if p >= 2:
            return ref[pl.ds(cy - 1 - depth if p == 2 else depth, comps * cx, stride=cy), :]
        skip = layer - cy - depth * cy if p == 0 else depth * cy
        return jnp.concatenate([ref[c * layer + skip : c * layer + skip + cy, :] for c in range(comps)], axis=0)

    def operate(x_ref, dst, src):
        zero = jnp.zeros((cy, nv), F32)
        for c in range(comps):
            at = pl.ds(c * layer, layer)
            x = x_ref[at, :]
            beside = jnp.concatenate([zero, x[:-cy]], axis=0) + jnp.concatenate([x[cy:], zero], axis=0)
            beside += pltpu.roll(x, 1, 0) * m_lo[...] + pltpu.roll(x, layer - 1, 0) * m_hi[...]
            value = beside - diag[...] * x
            dst[at, :] = value if src is None else src[at, :] + value

    def add_layers(dst, around):
        for c in range(comps):
            base = c * layer
            dst[base : base + cy, :] += around(0)[c * cy : (c + 1) * cy]
            dst[base + layer - cy : base + layer, :] += around(1)[c * cy : (c + 1) * cy]
        low = pl.ds(0, comps * cx, stride=cy)
        high = pl.ds(cy - 1, comps * cx, stride=cy)
        dst[low, :] = dst[low, :] + around(2)
        dst[high, :] = dst[high, :] + around(3)

    def ring_side(p):
        return ring[p * halo : p * halo + hrows[p], :]

    slot = b * gx + a

    def start_gather(t, cin):
        allbuf[t, slot] = cin.astype(BF16)
        here = allbuf.at[t, slot]
        rest = allbuf.at[t, pl.ds(0, n - 1)]
        gathering = remote(rest, rest, gs.at[t], gr.at[t], (to_a[0], to_b[1]))
        finish.append(gathering.wait_send)

        def go(chosen):
            each_other(lambda dev: remote(here, here, gs.at[t], gr.at[t], dev).start(), chosen)

        def arrived():
            gathering.wait_recv()
            return allbuf[t].astype(F32).reshape(kd, nv).astype(BF16)

        return go, arrived

    load_inv.wait()
    part = split(inv_v.at[:, pl.ds(0, own)], sub[0, :own, :])
    cpart = dot(basis_ref[:, :own], sub[0, :own, :])
    wait_margins()
    edge = sub[0, own:, :]
    go, arrived = start_gather(0, cpart + dot(basis_ref[:, own:], edge))
    pl.semaphore_wait(ready, gy - 1)
    go(0)
    q = (qr[0] + qr[1] + qr[2] + qr[3])[0:1]
    ycode[0:1, :yedge] = q
    tiles = (slice(0, 2 * ov), slice(2 * ov, 4 * ov))
    for tile in tiles:
        gmat[: 4 * dr2, tile] = hits(rowc[: 4 * dr2, :], q[:, tile])
        gmat[first_rest:gpm, tile] = hits(rowc[first_rest:gpm, :], q[:, tile])
    for h in range(2):
        at = slice(4 * dr2 + 2 * h * crows, 4 * dr2 + 2 * (h + 1) * crows)
        gmat[at, tiles[1 - h]] = hits(rowc[at, :], q[:, tiles[1 - h]])
    pmv[...] = part[own:] + dot(inv_v[own:, own:], edge)
    pm = pmv[...].astype(BF16)
    xs[...] = part[:own] + split(inv_v.at[pl.ds(0, own), pl.ds(own, 4 * ov)], edge)
    edges = jnp.concatenate([layer_rows(xs, p) for p in range(4)], axis=0).astype(BF16)
    made = split(gmat.at[pl.ds(0, gpm), :], pm)
    made_first = made[:first_rest].astype(BF16)
    made_rest = (made[first_rest:] + dot(gstat[...], edges)).astype(BF16)
    for p in range(4):
        msg_s[p, :ov, :] = pm[(p ^ 1) * ov : ((p ^ 1) + 1) * ov]
        msg_s[p, ov : ov + halo, :] = edges[p * halo : (p + 1) * halo]
        for d in range(1, 3):
            msg_s[p, ov + d * halo : ov + d * halo + hrows[p], :] = layer_rows(xs, p, d).astype(BF16)
        msg_s[p, ov + 3 * halo :, :] = made_first[4 * dr2 + p * crows : 4 * dr2 + (p + 1) * crows]
        dsend[p, :dr2, :] = made_first[p * dr2 : (p + 1) * dr2]
        dsend[p, dr2:, :] = made_rest[p * (dr - dr2) : (p + 1) * (dr - dr2)]
    wait_corners = trade(
        lambda p: [remote(dsend.at[p], ybuf.at[pl.ds(ycorner + p * dr, dr)], dsem_s.at[0, p], dsem_r.at[0, p], cdev[p])],
        has_c, has_cd,
    )
    wait_back = trade(
        lambda p: [remote(msg_s.at[p], ybuf.at[pl.ds(p * mrows, mrows)], nsem_s.at[1, p], nsem_r.at[1, p], up[p])],
        has_up, has_down,
    )
    go(1)
    for h in range(2):
        at = slice(gpm + 2 * h * halo, gpm + 2 * (h + 1) * halo)
        gmat[at, tiles[h]] = hits(rowc[at, :], q[:, tiles[h]])

    load_pmap.wait()
    wait_raw()
    wait_raw_c()
    ball[0] = basis_ref[...]
    sall[0] = crows_ref[...]
    spare = lanes - nine * kw
    stacked = jnp.concatenate([ball[...].astype(F32).reshape(nine * kw, -1), jnp.zeros((spare, own + 4 * ov), F32)], axis=0)
    bt[...] = stacked.T
    group = fdiv(fiota((1, lanes), 1), kw)

    def of(e, value):
        return jnp.where(group == e, value, 0.0)

    def margin(k):
        return bt[own + k * ov : own + (k + 1) * ov, :]

    theirs = jnp.concatenate([of(1.0 + p, margin(p ^ 1)) for p in range(4)], axis=0).astype(BF16)
    bextf[...] = of(0.0, bt[:own, :]) + dot(sel[...], theirs)
    around_b = jnp.concatenate([of(1.0 + p, layer_rows(bt, p)) for p in range(4)], axis=0)
    around_b += dot(gmat[gpm:, :], of(0.0, bt[own:, :]).astype(BF16))
    for m, (sx, sy) in enumerate(corner):
        ky, py = (0 if sx < 0 else 1), (3 if sy < 0 else 2)
        kx, px = (2 if sy < 0 else 3), (1 if sx < 0 else 0)
        pair = [qr[py, 1:2, ky * ov : (ky + 1) * ov], qr[px, 1:2, kx * ov : (kx + 1) * ov]]
        oh = hits(rowc[gpm:, :], jnp.concatenate(pair, axis=1))
        around_b += dot(oh, of(5.0 + m, jnp.concatenate([margin(ky), margin(kx)], axis=0)).astype(BF16))
    edge2[: 4 * halo, :] = around_b
    operate(bextf, abf, None)
    add_layers(abf, lambda p: edge2[p * halo : p * halo + hrows[p], :])
    bextb[...] = bextf[...].astype(BF16)
    abextb[...] = abf[...].astype(BF16)
    gather(1, abf)

    wide = min(kd, 256)
    pmf = jnp.broadcast_to(pmap_ref[...].astype(F32), (8, n))
    spare_s = jnp.zeros((spare, kd), F32)
    stacked_s = jnp.concatenate([sall[...].astype(F32).reshape(nine * kw, kd), spare_s], axis=0).astype(BF16)

    def order(c, _):
        q = fiota((1, wide), 1) + (c * wide).astype(F32)
        at_slot = fdiv(q, kw)
        slab = fdiv(at_slot, gx)
        dev = (at_slot - slab * gx) * gy + slab
        pick = jnp.where(fiota((n, wide), 0) == dev, 1.0, 0.0)
        place = dot(pmf, pick, precision=HIGH)[0:1] * kw + (q - at_slot * kw)
        perm = jnp.where(fiota((kd, wide), 0) == place, 1.0, 0.0).astype(BF16)
        at = pl.ds(pl.multiple_of(c * wide, wide), wide)
        sext[:, at] = dot(stacked_s, perm).astype(BF16)
        am_s[:, at] = dot(outs[1], sext[:, at]).astype(BF16)
        return 0

    lax.fori_loop(jnp.int32(0), jnp.int32(kd // wide), order, 0)
    wait_am = trade(
        lambda p: [remote(am_s.at[pl.ds(p * ov, ov)], am_r.at[pl.ds(p * ov, ov)], csem_s.at[4, p], csem_r.at[4, p], up[p])],
        has_up, has_down,
    )

    def as_column(line):
        return jnp.broadcast_to(jnp.broadcast_to(line, (8, 4 * ov)).T[:, 0:1], (4 * ov, 128))

    qb[...] = as_column(ycode[0:1, :yedge])
    wait_t()
    sb[...] = as_column((tr[0] + tr[1] + tr[2] + tr[3])[0:1])
    pm = pmv[...].astype(BF16)
    for h in range(0, cmarg.shape[1], 128):
        gap = jnp.abs(lines[0:1, h : h + 128] - qb[...])
        cmarg[:, h : h + 128] = coefficient(gap, sb[...])
    for p in range(4):
        at = slice(p * ov, (p + 1) * ov)
        line = jnp.concatenate([ycode[0:1, at], edge_code[p ^ 1]], axis=1)
        mc[p] = adjacent(jnp.abs(line - qb[at, : ov + halo])).astype(BF16)
        near_edge = jnp.concatenate([pm[at], msg_s[p ^ 1, ov : ov + halo, :]], axis=0)
        known = sub[0, own + p * ov : own + (p + 1) * ov, :].astype(F32)
        edge2[at, :] = known + dot(mc[p], near_edge) - sb[at, :] * pmv[at, :]

    rc = fiota((layer, 128), 0)
    ri = fdiv(rc, cy)
    here_code = code(0.0, ri, rc - ri * cy)

    def fill_own(c, _):
        at = pl.ds(pl.multiple_of(c * layer, layer), layer)
        shift = c.astype(F32) * (wide_grid * wide_grid)
        for h in range(0, cown.shape[1], 128):
            gap = jnp.abs(here_code + shift - lines[1:2, h : h + 128])
            cown[at, h : h + 128] = coefficient(gap, diag[:, :128])
        return 0

    lax.fori_loop(jnp.int32(0), jnp.int32(comps), fill_own, 0)

    r = fiota((2 * comps * cx, own), 0)
    lower = jnp.where(r >= comps * cx, 1.0, 0.0)
    wanted_row = (r - lower * (comps * cx)) * cy + (cy - 1) * (1.0 - lower)
    pick = jnp.where(fiota((2 * comps * cx, own), 1) == wanted_row, 1.0, 0.0).astype(BF16)
    inve[...] = dot(pick, inv_v[:own, :]).astype(BF16)

    operate(xs, mid, res_v)
    ring[...] = dot(gmat[gpm:, :], pm)
    add_layers(mid, ring_side)

    wait_am()
    gathered = arrived()
    cout = dot(sext[...], gathered).astype(BF16)
    edge2[: 4 * ov, :] += dot(am_r[...], gathered)
    mid[...] += dot(abextb[...], cout)

    wait_back()
    wait_corners()

    def piece(p, at, count):
        return ybuf[p * mrows + at : p * mrows + at + count, :]

    pieces = 4 * (mrows + dr)
    sub[1, own:, :] = (edge2[: 4 * ov, :] + dot(cmarg[:, :pieces], ybuf[...])).astype(BF16)
    backs = jnp.concatenate([piece(p, 0, ov) for p in range(4)], axis=0)
    rest = [piece(p, ov, halo) for p in range(4)]
    rest += [ybuf[ycorner + m * dr : ycorner + m * dr + dr2, :] for m in range(4)]
    sol_ref[...] = split(cown, jnp.concatenate([backs] + rest, axis=0))
    value = mid[...] + sol_ref[...]
    mid[...] = value
    sub[1, :own, :] = value.astype(BF16)

    go, arrived = start_gather(1, dot(basis_ref[...], sub[1]))
    go(0)
    lhs = [inv_v[own:, :]]
    lhs += [inv_v[c * layer + layer - cy : (c + 1) * layer, :] for c in range(comps)]
    lhs += [inv_v[c * layer : c * layer + cy, :] for c in range(comps)]
    made = split(jnp.concatenate(lhs + [inve[...]], axis=0), sub[1])
    pm = made[: 4 * ov].astype(BF16)
    at = 4 * ov
    for p in range(4):
        msg2_s[p, :ov, :] = pm[(p ^ 1) * ov : ((p ^ 1) + 1) * ov]
        msg2_s[p, ov : ov + hrows[p], :] = made[at : at + hrows[p]].astype(BF16)
        at += hrows[p]
    dsend2[...] = dot(gmat[: 4 * dr2, :], pm).astype(BF16)
    wait_corners = trade(
        lambda p: [remote(dsend2.at[pl.ds(p * dr2, dr2)], drecv2.at[pl.ds(p * dr2, dr2)], dsem_s.at[1, p], dsem_r.at[1, p], cdev[p])],
        has_c, has_cd,
    )
    wait_back = trade(
        lambda p: [remote(msg2_s.at[p], msg2_r.at[p], nsem_s.at[2, p], nsem_r.at[2, p], up[p])],
        has_up, has_down,
    )
    go(1)
    sol_ref[...] = xs[...] + dot(bextb[...], cout)
    sol_ref[...] += dot(sel[...], backs)
    xs[...] = split(inv_v.at[pl.ds(0, own), :], sub[1])
    sol_ref[...] += xs[...]
    operate(xs, fin_ref, mid)
    ring[...] = dot(gmat[gpm:, :], pm)
    add_layers(fin_ref, ring_side)
    wait_back()
    wait_corners()
    backs = jnp.concatenate([msg2_r[p, :ov, :] for p in range(4)], axis=0)
    rest = jnp.concatenate([msg2_r[p, ov:, :] for p in range(4)] + [drecv2[...]], axis=0)
    both = jnp.concatenate([backs, rest], axis=0)
    xs[...] = split(cown, both)
    fin_ref[...] += xs[...]
    sol_ref[...] += split(sel, backs)
    gathered = arrived()
    cout = dot(sext[...], gathered).astype(BF16)
    fin_ref[...] += split(abextb, cout)
    sol_ref[...] += split(bextb, cout)
    for end in finish:
        end()


def emit(sol_ref, fin_ref, sol_hbm, fin_hbm, sem):
    pairs = ((sol_ref, sol_hbm), (fin_ref, fin_hbm))
    copies = [pltpu.make_async_copy(x, y, sem.at[k]) for k, (x, y) in enumerate(pairs)]
    for c in copies:
        c.start()
    for c in copies:
        c.wait()


def solution(mesh):
    gx, gy = mesh.shape["gx"], mesh.shape["gy"]

    def per_device(residual, stiffness, local_inverse, coarse_basis, coarse_rows, send_rows, partition_map):
        comps, cx, cy, nv = residual.shape
        own, layer = comps * cx * cy, cx * cy
        m = local_inverse.shape[-1]
        ov = send_rows.shape[-1]
        kw, kd = coarse_rows.shape[-2:]
        halo = comps * max(cx, cy)
        def whole(count, of):
            return -(-count // of) * of

        lanes = whole(9 * kw, 128)
        dr, dr2 = whole(15 * comps, 16), whole(4 * comps, 16)
        crows = whole(6 * comps, 16)
        mrows = ov + 3 * halo + crows
        width = whole(4 * (mrows + dr), 128)
        grows = 4 * (halo + crows + dr)
        vm = pl.BlockSpec(memory_space=pltpu.VMEM)
        anywhere = pl.BlockSpec(memory_space=pl.ANY)
        dma = pltpu.SemaphoreType.DMA
        out = pl.pallas_call(
            functools.partial(kernel, gx, gy, (comps, cx, cy, nv)),
            out_shape=[pltpu.VMEM((own, nv), F32)] * 2,
            in_specs=[anywhere] * 7,
            out_specs=[vm, vm],
            scratch_shapes=[
                pltpu.VMEM((own, nv), F32),
                pltpu.VMEM((cx, cy), F32),
                pltpu.VMEM((m, m), BF16),
                pltpu.VMEM((kw, m), BF16),
                pltpu.VMEM((kw, kd), BF16),
                pltpu.VMEM((4, ov), jnp.int32),
                pltpu.VMEM((1, gx * gy), jnp.int32),
                pltpu.VMEM((2, m, nv), BF16),
                pltpu.VMEM((own, 4 * ov), BF16),
                pltpu.VMEM((4, ov, 2 * halo), BF16),
                pltpu.VMEM((2, 4 * ov, nv), BF16),
                pltpu.VMEM((4 * (mrows + dr), nv), BF16),
                pltpu.VMEM((8, 4 * ov + 4 * halo), F32),
                pltpu.VMEM((8, width), F32),
                pltpu.VMEM((grows, 128), F32),
                pltpu.VMEM((4 * ov, 128), F32),
                pltpu.VMEM((4 * ov, 128), F32),
                pltpu.VMEM((grows, 4 * ov), BF16),
                pltpu.VMEM((4 * (dr - dr2), 4 * halo), BF16),
                pltpu.VMEM((own, 4 * (ov + halo + dr2)), BF16),
                pltpu.VMEM((4 * ov, width), BF16),
                pltpu.VMEM((4, ov, ov + halo), BF16),
                pltpu.VMEM((2 * comps * cx, m), BF16),
                pltpu.VMEM((4 * ov, nv), F32),
                pltpu.VMEM((4 * halo, nv), F32),
                pltpu.VMEM((4, mrows, nv), BF16),
                pltpu.VMEM((4, dr, nv), BF16),
                pltpu.VMEM((4, ov + halo, nv), BF16),
                pltpu.VMEM((4, ov + halo, nv), BF16),
                pltpu.VMEM((4 * dr2, nv), BF16),
                pltpu.VMEM((4 * dr2, nv), BF16),
                pltpu.VMEM((4, 8, 4 * ov), F32),
                pltpu.VMEM((4, 8, 4 * ov), F32),
                pltpu.VMEM((4, 8, 4 * ov), F32),
                pltpu.VMEM((4, 8, 4 * ov), F32),
                pltpu.VMEM((2, gx * gy, kw, nv), BF16),
                pltpu.VMEM((9, kw, m), BF16),
                pltpu.VMEM((9, kw, kd), BF16),
                pltpu.VMEM((lanes, kd), BF16),
                pltpu.VMEM((m, lanes), F32),
                pltpu.VMEM((own, lanes), F32),
                pltpu.VMEM((own, lanes), F32),
                pltpu.VMEM((own, lanes), BF16),
                pltpu.VMEM((own, lanes), BF16),
                pltpu.VMEM((4 * ov, kd), BF16),
                pltpu.VMEM((4 * ov, kd), BF16),
                pltpu.VMEM((max(4 * ov, 4 * halo), nv), F32),
                pltpu.VMEM((layer, nv), F32),
                pltpu.VMEM((layer, nv), F32),
                pltpu.VMEM((layer, nv), F32),
                pltpu.VMEM((own, nv), F32),
                pltpu.VMEM((own, nv), F32),
                dma((7,)),
                pltpu.SemaphoreType.REGULAR,
                dma((3, 4)),
                dma((3, 4)),
                dma((2, 4)),
                dma((2, 4)),
                dma((5, 4)),
                dma((5, 4)),
                dma((2, 4)),
                dma((2, 4)),
                dma((2,)),
                dma((2,)),
            ],
            compiler_params=pltpu.CompilerParams(collective_id=0, has_side_effects=True),
        )(
            residual.reshape(own, nv),
            stiffness,
            local_inverse[0, 0],
            coarse_basis[0, 0],
            coarse_rows[0, 0],
            send_rows[0, 0],
            partition_map.reshape(1, -1),
        )
        out = pl.pallas_call(
            emit,
            out_shape=[jax.ShapeDtypeStruct((own, nv), F32)] * 2,
            in_specs=[vm, vm],
            out_specs=[anywhere, anywhere],
            scratch_shapes=[dma((2,))],
        )(*[pltpu.with_memory_space_constraint(o, pltpu.VMEM) for o in out])
        return tuple(o.reshape(residual.shape) for o in out)

    placed = (
        P(None, "gx", "gy", None),
        P("gx", "gy"),
        P("gx", "gy", None, None),
        P("gx", "gy", None, None),
        P("gx", "gy", None, None),
        P("gx", "gy", None, None),
        P(),
    )
    return jax.shard_map(
        per_device,
        mesh=mesh,
        in_specs=placed,
        out_specs=(P(None, "gx", "gy", None), P(None, "gx", "gy", None)),
        check_vma=False,
    )
```

```python
import functools

import jax
import jax.numpy as jnp
from jax import lax
from jax.experimental import pallas as pl
from jax.experimental.pallas import tpu as pltpu
from jax.sharding import PartitionSpec as P

MESH = pl.DeviceIdType.MESH
F32 = jnp.float32
BF16 = jnp.bfloat16
HIGH = lax.Precision.HIGHEST


def dot(x, y, **kw):
    return jnp.dot(x, y, preferred_element_type=F32, **kw)


def split(x, y):
    cut = x.shape[0] // 32 * 16
    return jnp.concatenate([dot(x[:cut, :], y), dot(x[cut:, :], y)], axis=0)


def tdot(x, y):
    return lax.dot_general(x, y, (((0,), (0,)), ((), ())), preferred_element_type=F32)


def fiota(shape, axis):
    return lax.broadcasted_iota(jnp.int32, shape, axis).astype(F32)


def fdiv(x, n):
    return jnp.floor((x + 0.5) * (1.0 / n))


def kernel(
    gx, gy, dims,
    res_hbm, stiff_hbm, inv_hbm, basis_hbm, crows_hbm, lists_hbm, pmap_hbm,
    sol_ref, fin_ref,
    res_v, stiff_ref, inv_v, basis_ref, crows_ref, lists_ref, pmap_ref, sub, sel, near, outs,
    ybuf, ycode, lines, rowc, qb, sb, gmat, gstat, cown, cmarg, mc, inve, pmv, ring, msg_s, dsend,
    msg2_s, msg2_r, dsend2, drecv2,
    qs, qr, qd_s, qd_r, ts, tr, allbuf, ball, sall, sext, bt, bextf, abf, bextb, abextb, yb, mbb, edge2,
    diag, m_lo, m_hi, xs, mid,
    lsem, ready, nsem_s, nsem_r, dsem_s, dsem_r, csem_s, csem_r, rsem_s, rsem_r, gs, gr,
):
    comps, cx, cy, nv = dims
    halo = comps * max(cx, cy)
    hrows = (comps * cy, comps * cy, comps * cx, comps * cx)
    own = comps * cx * cy
    layer = cx * cy
    ov = lists_ref.shape[1]
    kw, kd = crows_ref.shape
    n = gx * gy
    mrows = msg_s.shape[1]
    crows = mrows - ov - 3 * halo
    dr, dr2 = dsend.shape[1], dsend2.shape[0] // 4
    yedge = 4 * ov
    ycorner = 4 * mrows
    gpm = 4 * (dr + crows)
    nine = ball.shape[0]
    lanes = bextf.shape[1]
    a = lax.axis_index("gx")
    b = lax.axis_index("gy")

    wanted = [
        (lists_hbm, lists_ref), (res_hbm, res_v), (pmap_hbm, pmap_ref), (crows_hbm, crows_ref),
        (basis_hbm, basis_ref), (stiff_hbm, stiff_ref), (inv_hbm, inv_v),
    ]
    loads = [pltpu.make_async_copy(x, y, lsem.at[k]) for k, (x, y) in enumerate(wanted)]
    load_lists, load_res, load_pmap, load_crows, load_basis, load_stiff, load_inv = loads
    for load in loads:
        load.start()

    def flip(x, k):
        y, bit = x, 1
        while bit <= k:
            if k & bit:
                y = y + bit * (1 - 2 * lax.rem(lax.div(x, bit), 2))
            bit *= 2
        return y

    paired = gx & (gx - 1) == 0 and gy & (gy - 1) == 0
    others = [(i, j) for i in range(gx) for j in range(gy) if i or j]
    if paired:
        others.sort(key=lambda o: -((o[0] >> 1) + bin(o[1]).count("1") + 0.4 * (o[0] & 1)))
        to_a = [flip(a, i) for i in range(gx)]
        to_b = [flip(b, j) for j in range(gy)]
    else:
        to_a = [lax.rem(a + i, gx) for i in range(gx)]
        to_b = [lax.rem(b + j, gy) for j in range(gy)]

    half = len(others) // 2

    def each_other(act, chosen=None):
        if n <= 64:
            for i, j in others if chosen is None else (others[:half], others[half:])[chosen]:
                act((to_a[i], to_b[j]))
            return
        if chosen == 1:
            return

        def row(i, _):
            ai = lax.rem(a + i, gx)
            for j in range(1, gy):
                act((ai, lax.rem(b + j, gy)))
            pl.when(i > 0)(lambda: act((ai, b)))
            return 0

        lax.fori_loop(jnp.int32(0), jnp.int32(gx), row, 0)

    barrier = pltpu.get_barrier_semaphore()

    def peers(size):
        return sorted(range(1, size), key=lambda o: min(o, size - o))

    def signal(sem, dev):
        pl.semaphore_signal(sem, inc=1, device_id=dev, device_id_type=MESH)

    for o in peers(gy):
        signal(barrier, (a, lax.rem(b + o, gy)))
    for o in peers(gx):
        signal(barrier, (lax.rem(a + o, gx), b))

    up = [(a + 1, b), (a - 1, b), (a, b + 1), (a, b - 1)]
    has_up = [a < gx - 1, a > 0, b < gy - 1, b > 0]
    down = [up[p ^ 1] for p in range(4)]
    has_down = [has_up[p ^ 1] for p in range(4)]
    corner = [(1, 1), (-1, -1), (1, -1), (-1, 1)]
    cdev = [(a + sx, b + sy) for sx, sy in corner]
    has_c = [
        jnp.logical_and(has_up[0 if sx > 0 else 1], has_up[2 if sy > 0 else 3]) for sx, sy in corner
    ]
    finish = []

    for p in range(4):
        pl.when(has_c[p])(lambda p=p: signal(barrier, cdev[p]))

    def send(copies, conds, wait):
        for p in (2, 3, 0, 1):
            @pl.when(conds[p])
            def _(p=p):
                for c in copies(p):
                    getattr(c, wait)()

    def trade(copies, to, fro):
        send(copies, to, "start")
        finish.append(lambda: send(copies, to, "wait_send"))
        return lambda: send(copies, fro, "wait_recv")

    def remote(src, dst, s, r, dev):
        return pltpu.make_async_remote_copy(
            src_ref=src, dst_ref=dst, send_sem=s, recv_sem=r, device_id=dev, device_id_type=MESH
        )

    wide_grid = 4 * max(cx, cy)

    def code(c, i, j):
        return (c * wide_grid + (i + cx)) * wide_grid + (j + cy)

    load_lists.wait()
    lists = lists_ref[...].astype(F32)
    columns = lists.T
    for p in range(4):
        count = 2 * hrows[p]
        q = fiota((1, count), 1)
        if p < 2:
            c = fdiv(q, 2 * cy)
            row = c * layer + (layer - 2 * cy) * (1 - p) + (q - c * 2 * cy)
        else:
            second = jnp.where(q >= comps * cx, 1.0, 0.0)
            row = (q - second * (comps * cx)) * cy + (cy - 2) * (3 - p) + second
        hit = jnp.broadcast_to(columns[:, (p ^ 1) : (p ^ 1) + 1], (ov, count)) == jnp.broadcast_to(row, (ov, count))
        near[p, :, :count] = jnp.where(hit, 1.0, 0.0).astype(BF16)

    lc = fdiv(lists, layer)
    li = fdiv(lists - lc * layer, cy)
    lj = lists - lc * layer - li * cy
    block = fdiv(fiota((1, 4 * ov), 1), ov)

    def in_line(x):
        return jnp.concatenate([x[(p ^ 1) : (p ^ 1) + 1] for p in range(4)], axis=1)

    sides = ((-1, 0), (1, 0), (0, -1), (0, 1))
    for p, (dx, dy) in enumerate(sides):
        line = in_line(code(lc, li + dx * cx, lj + dy * cy))
        qs[p, 0:1, :] = jnp.where(block == p, line, 0.0)
        qs[p, 1:2, :] = line

    load_res.wait()

    def gather(t, src):
        for p in range(4):
            if p < 2:
                skip = (layer - 2 * cy) * (1 - p)
                rows = [src[c * layer + skip : c * layer + skip + 2 * cy, :] for c in range(comps)]
            else:
                rows = [src[pl.ds((cy - 2) * (3 - p) + k, comps * cx, stride=cy), :] for k in range(2)]
            rows = jnp.concatenate(rows, axis=0).astype(BF16)
            outs[t, p * ov : (p + 1) * ov, :] = dot(near[p, :, : 2 * hrows[p]], rows).astype(BF16)

    gather(0, res_v)
    met = gx + gy - 2 + sum(c.astype(jnp.int32) for c in has_c)
    pl.semaphore_wait(barrier, met)

    def start_margins(t):
        return trade(
            lambda p: [
                remote(outs.at[t, pl.ds(p * ov, ov)], sub.at[t, pl.ds(own + p * ov, ov)],
                       nsem_s.at[0, p], nsem_r.at[0, p], up[p]),
                remote(qs.at[p], qr.at[p], csem_s.at[0, p], csem_r.at[0, p], up[p]),
            ],
            has_up, has_down,
        )

    wait_margins = start_margins(0)
    has_cd = [has_c[p ^ 1] for p in range(4)]
    for o in peers(gy):
        signal(ready, (a, lax.rem(b + o, gy)))
    for m, (sx, sy) in enumerate(corner):
        qd_s[m, 0:1, :] = in_line(code(lc, li - sx * cx, lj - sy * cy))
    load_basis.wait()
    load_crows.wait()
    wait_raw = trade(
        lambda p: [
            remote(basis_ref, ball.at[1 + p], csem_s.at[1, p], csem_r.at[1, p], up[p]),
            remote(crows_ref, sall.at[1 + p], csem_s.at[2, p], csem_r.at[2, p], up[p]),
        ],
        has_up, has_down,
    )
    wait_raw_c = trade(
        lambda p: [
            remote(basis_ref, ball.at[5 + p], rsem_s.at[0, p], rsem_r.at[0, p], cdev[p]),
            remote(qd_s.at[p], qd_r.at[p], rsem_s.at[2, p], rsem_r.at[2, p], cdev[p]),
            remote(crows_ref, sall.at[5 + p], rsem_s.at[1, p], rsem_r.at[1, p], cdev[p]),
        ],
        has_c, has_cd,
    )
    sub[0, :own, :] = res_v[...].astype(BF16)

    for p in range(4):
        @pl.when(jnp.logical_not(has_down[p]))
        def _(p=p):
            sub[0, own + p * ov : own + (p + 1) * ov, :] = jnp.zeros((ov, nv), BF16)
            ybuf[p * mrows : (p + 1) * mrows, :] = jnp.zeros((mrows, nv), BF16)
            msg2_r[p] = jnp.zeros(msg2_r.shape[1:], BF16)
            qr[p] = jnp.zeros(qr.shape[1:], F32)
            tr[p] = jnp.zeros(tr.shape[1:], F32)
            ball[1 + p] = jnp.zeros(ball.shape[1:], BF16)
            sall[1 + p] = jnp.zeros(sall.shape[1:], BF16)

        @pl.when(jnp.logical_not(has_cd[p]))
        def _(p=p):
            ybuf[ycorner + p * dr : ycorner + (p + 1) * dr, :] = jnp.zeros((dr, nv), BF16)
            drecv2[p * dr2 : (p + 1) * dr2, :] = jnp.zeros((dr2, nv), BF16)
            ball[5 + p] = jnp.zeros(ball.shape[1:], BF16)
            qd_r[p] = jnp.zeros(qd_r.shape[1:], F32)
            sall[5 + p] = jnp.zeros(sall.shape[1:], BF16)

    load_stiff.wait()
    r1 = fiota((layer, cy), 0)
    first = fdiv(r1, cy)
    mine = jnp.where(fiota((layer, cx), 1) == fdiv(fiota((layer, cx), 0), cy), 1.0, 0.0)
    spread = dot(mine, stiff_ref[...], precision=HIGH)
    spread = jnp.where(fiota((layer, cy), 1) == r1 - first * cy, spread, 0.0)
    diag[...] = jnp.broadcast_to(4.0 + jnp.sum(spread, axis=1, keepdims=True), (layer, nv))
    rr = fiota((layer, nv), 0)
    second = rr - fdiv(rr, cy) * cy
    m_lo[...] = jnp.where(second == 0.0, 0.0, 1.0)
    m_hi[...] = jnp.where(second == cy - 1.0, 0.0, 1.0)

    cells = jnp.where(fiota((layer, 4 * ov), 0) == in_line(li * cy + lj), 1.0, 0.0)
    at_cells = lax.dot_general(
        diag[...], cells, (((0,), (0,)), ((), ())), precision=HIGH, preferred_element_type=F32
    )[0:8]
    for p in range(4):
        ts[p] = jnp.where(jnp.broadcast_to(block, (8, 4 * ov)) == p, at_cells, 0.0)
    wait_t = trade(
        lambda p: [remote(ts.at[p], tr.at[p], csem_s.at[3, p], csem_r.at[3, p], up[p])], has_up, has_down
    )

    def edge_cells(w, p, depth, outside):
        per = cy if p < 2 else cx
        c = fdiv(w, per)
        along = w - c * per
        size = cx if p < 2 else cy
        if outside:
            off = along * 0.0 + (-1.0 - depth, size + depth)[p % 2]
        else:
            off = along * 0.0 + (size - 1.0 - depth, 1.0 * depth)[p % 2]
        return (c, off, along, w < hrows[p]) if p < 2 else (c, along, off, w < hrows[p])

    def beside_cells(w, p):
        v = fdiv(w, 3 * comps)
        u = 1.0 - 2.0 * v
        c = fdiv(w - v * (3 * comps), 3)
        kk = w - v * (3 * comps) - 3 * c
        deep, far = jnp.where(kk == 1.0, 1.0, 0.0), jnp.where(kk == 2.0, 1.0, 0.0)
        size, size2 = (cx, cy) if p < 2 else (cy, cx)
        along = (size - 1.0 - deep) if p % 2 == 0 else deep
        out = jnp.where(v == 0.0, size2 + far, -1.0 - far)
        return (c, along, out, v < 2.0) if p < 2 else (c, out, along, v < 2.0)

    def corner_cells(w, sx, sy):
        ex, ey = (cx - 1.0 if sx > 0 else 0.0), (cy - 1.0 if sy > 0 else 0.0)
        ox, oy = (1.0 * cx if sx > 0 else -1.0), (1.0 * cy if sy > 0 else -1.0)
        g = fdiv(w, 2 * comps)
        depth = fdiv(g, 2)
        kind = g - 2 * depth
        c = fdiv(w - g * (2 * comps), 2)
        k = w - g * (2 * comps) - 2 * c
        i = jnp.where(kind == 0.0, ex - sx * depth, ox + sx * k)
        j = jnp.where(kind == 0.0, oy + sy * k, ey - sy * depth)
        w2 = w - 12 * comps
        c2 = fdiv(w2, 3)
        kk = w2 - 3 * c2
        tail = w2 >= 0.0
        i = jnp.where(tail, ex - sx * jnp.where(kk == 1.0, 1.0, 0.0), i)
        j = jnp.where(tail, ey - sy * jnp.where(kk == 2.0, 1.0, 0.0), j)
        return jnp.where(tail, c2, c), i, j, w < 15 * comps

    nowhere = -16.0 * wide_grid * wide_grid

    def coded(cell, dx=0, dy=0):
        c, i, j, real = cell
        return jnp.where(real, code(c, i - dx * cx, j - dy * cy), nowhere)

    def row_of(count):
        return fiota((1, count), 1)

    def deduped(cell, p):
        c, i, j, real = cell
        return (c, i, j, real if p < 2 else jnp.logical_and(real, jnp.logical_and(i > 0.0, i < cx - 1.0)))

    back_code = [code(lc, li, lj)[p : p + 1] for p in range(4)]
    edge_code = [coded(edge_cells(row_of(halo), p, 0, False)) for p in range(4)]
    deep_code = [[coded(edge_cells(row_of(halo), p, d, True)) for d in range(3)] for p in range(4)]
    beside_code = [coded(beside_cells(row_of(crows), p), -sides[p][0], -sides[p][1]) for p in range(4)]
    corner_code = [coded(corner_cells(row_of(dr), *corner[m]), *corner[m]) for m in range(4)]
    short_code = [coded(corner_cells(row_of(dr2), *corner[m]), *corner[m]) for m in range(4)]
    ycode[0:1, yedge:] = jnp.concatenate(
        [coded(deduped(edge_cells(row_of(halo), p, 0, False), p)) for p in range(4)], axis=1
    )
    line = []
    for p in range(4):
        line += [back_code[p]] + deep_code[p] + [beside_code[p]]
    line = jnp.concatenate(line + corner_code, axis=1)
    lines[...] = jnp.full(lines.shape, nowhere, F32)
    lines[0:1, : line.shape[1]] = line
    line = jnp.concatenate(back_code + [deep_code[p][0] for p in range(4)] + short_code, axis=1)
    lines[1:2, : line.shape[1]] = line

    def column_of(count):
        return fiota((count, 128), 0)

    rlist = [coded(corner_cells(column_of(dr2), *corner[m])) for m in range(4)]
    rlist += [coded(beside_cells(column_of(crows), p)) for p in range(4)]
    rlist += [coded(corner_cells(column_of(dr - dr2) + dr2, *corner[m])) for m in range(4)]
    rlist += [coded(edge_cells(column_of(halo), p, 0, True)) for p in range(4)]
    rowc[...] = jnp.concatenate(rlist, axis=0)

    def hits(rows, row):
        parts = []
        for at in range(0, row.shape[1], 128):
            piece = row[:, at : at + 128]
            parts.append(jnp.where(rows[:, : piece.shape[1]] == piece, 1.0, 0.0))
        return (jnp.concatenate(parts, axis=1) if len(parts) > 1 else parts[0]).astype(BF16)

    def adjacent(gap):
        return jnp.where(jnp.logical_or(gap == 1.0, gap == wide_grid), 1.0, 0.0)

    def coefficient(gap, weight):
        return jnp.where(gap == 0.0, -weight, adjacent(gap)).astype(BF16)

    gmat[...] = jnp.zeros(gmat.shape, BF16)
    first_rest = 4 * (dr2 + crows)
    gstat[...] = hits(rowc[first_rest:gpm, :], ycode[0:1, yedge:])

    rows = fiota((own, ov), 0)
    for h in range(2):
        two = [jnp.where(rows == lists[p : p + 1], 1.0, 0.0) for p in (2 * h, 2 * h + 1)]
        sel[:, 2 * ov * h : 2 * ov * (h + 1)] = jnp.concatenate(two, axis=1).astype(BF16)

    def layer_rows(ref, p, depth=0):
        if p >= 2:
            return ref[pl.ds(cy - 1 - depth if p == 2 else depth, comps * cx, stride=cy), :]
        skip = layer - cy - depth * cy if p == 0 else depth * cy
        return jnp.concatenate([ref[c * layer + skip : c * layer + skip + cy, :] for c in range(comps)], axis=0)

    def operate(x_ref, dst, src):
        zero = jnp.zeros((cy, nv), F32)
        for c in range(comps):
            at = pl.ds(c * layer, layer)
            x = x_ref[at, :]
            beside = jnp.concatenate([zero, x[:-cy]], axis=0) + jnp.concatenate([x[cy:], zero], axis=0)
            beside += pltpu.roll(x, 1, 0) * m_lo[...] + pltpu.roll(x, layer - 1, 0) * m_hi[...]
            value = beside - diag[...] * x
            dst[at, :] = value if src is None else src[at, :] + value

    def add_layers(dst, around):
        for c in range(comps):
            base = c * layer
            dst[base : base + cy, :] += around(0)[c * cy : (c + 1) * cy]
            dst[base + layer - cy : base + layer, :] += around(1)[c * cy : (c + 1) * cy]
        low = pl.ds(0, comps * cx, stride=cy)
        high = pl.ds(cy - 1, comps * cx, stride=cy)
        dst[low, :] = dst[low, :] + around(2)
        dst[high, :] = dst[high, :] + around(3)

    def ring_side(p):
        return ring[p * halo : p * halo + hrows[p], :]

    slot = b * gx + a

    def start_gather(t, cin):
        allbuf[t, slot] = cin.astype(BF16)
        here = allbuf.at[t, slot]
        rest = allbuf.at[t, pl.ds(0, n - 1)]
        gathering = remote(rest, rest, gs.at[t], gr.at[t], (to_a[0], to_b[1]))
        finish.append(gathering.wait_send)

        def go(chosen):
            each_other(lambda dev: remote(here, here, gs.at[t], gr.at[t], dev).start(), chosen)

        def arrived():
            gathering.wait_recv()
            return allbuf[t].astype(F32).reshape(kd, nv).astype(BF16)

        return go, arrived

    load_inv.wait()
    part = split(inv_v.at[:, pl.ds(0, own)], sub[0, :own, :])
    cpart = dot(basis_ref[:, :own], sub[0, :own, :])
    wait_margins()
    edge = sub[0, own:, :]
    go, arrived = start_gather(0, cpart + dot(basis_ref[:, own:], edge))
    pl.semaphore_wait(ready, gy - 1)
    go(0)
    q = (qr[0] + qr[1] + qr[2] + qr[3])[0:1]
    ycode[0:1, :yedge] = q
    tiles = (slice(0, 2 * ov), slice(2 * ov, 4 * ov))
    for tile in tiles:
        gmat[: 4 * dr2, tile] = hits(rowc[: 4 * dr2, :], q[:, tile])
        gmat[first_rest:gpm, tile] = hits(rowc[first_rest:gpm, :], q[:, tile])
    for h in range(2):
        at = slice(4 * dr2 + 2 * h * crows, 4 * dr2 + 2 * (h + 1) * crows)
        gmat[at, tiles[1 - h]] = hits(rowc[at, :], q[:, tiles[1 - h]])
    pmv[...] = part[own:] + dot(inv_v[own:, own:], edge)
    pm = pmv[...].astype(BF16)
    xs[...] = part[:own] + split(inv_v.at[pl.ds(0, own), pl.ds(own, 4 * ov)], edge)
    edges = jnp.concatenate([layer_rows(xs, p) for p in range(4)], axis=0).astype(BF16)
    made = split(gmat.at[pl.ds(0, gpm), :], pm)
    made_first = made[:first_rest].astype(BF16)
    made_rest = (made[first_rest:] + dot(gstat[...], edges)).astype(BF16)
    for p in range(4):
        msg_s[p, :ov, :] = pm[(p ^ 1) * ov : ((p ^ 1) + 1) * ov]
        msg_s[p, ov : ov + halo, :] = edges[p * halo : (p + 1) * halo]
        for d in range(1, 3):
            msg_s[p, ov + d * halo : ov + d * halo + hrows[p], :] = layer_rows(xs, p, d).astype(BF16)
        msg_s[p, ov + 3 * halo :, :] = made_first[4 * dr2 + p * crows : 4 * dr2 + (p + 1) * crows]
        dsend[p, :dr2, :] = made_first[p * dr2 : (p + 1) * dr2]
        dsend[p, dr2:, :] = made_rest[p * (dr - dr2) : (p + 1) * (dr - dr2)]
    wait_corners = trade(
        lambda p: [remote(dsend.at[p], ybuf.at[pl.ds(ycorner + p * dr, dr)], dsem_s.at[0, p], dsem_r.at[0, p], cdev[p])],
        has_c, has_cd,
    )
    wait_back = trade(
        lambda p: [remote(msg_s.at[p], ybuf.at[pl.ds(p * mrows, mrows)], nsem_s.at[1, p], nsem_r.at[1, p], up[p])],
        has_up, has_down,
    )
    go(1)
    for h in range(2):
        at = slice(gpm + 2 * h * halo, gpm + 2 * (h + 1) * halo)
        gmat[at, tiles[h]] = hits(rowc[at, :], q[:, tiles[h]])

    load_pmap.wait()
    wait_raw()
    wait_raw_c()
    ball[0] = basis_ref[...]
    sall[0] = crows_ref[...]
    spare = lanes - nine * kw
    stacked = jnp.concatenate([ball[...].astype(F32).reshape(nine * kw, -1), jnp.zeros((spare, own + 4 * ov), F32)], axis=0)
    bt[...] = stacked.T
    group = fdiv(fiota((1, lanes), 1), kw)

    def of(e, value):
        return jnp.where(group == e, value, 0.0)

    def margin(k):
        return bt[own + k * ov : own + (k + 1) * ov, :]

    theirs = jnp.concatenate([of(1.0 + p, margin(p ^ 1)) for p in range(4)], axis=0).astype(BF16)
    bextf[...] = of(0.0, bt[:own, :]) + dot(sel[...], theirs)
    around_b = jnp.concatenate([of(1.0 + p, layer_rows(bt, p)) for p in range(4)], axis=0)
    around_b += dot(gmat[gpm:, :], of(0.0, bt[own:, :]).astype(BF16))
    for m, (sx, sy) in enumerate(corner):
        ky, py = (0 if sx < 0 else 1), (3 if sy < 0 else 2)
        kx, px = (2 if sy < 0 else 3), (1 if sx < 0 else 0)
        pair = [qr[py, 1:2, ky * ov : (ky + 1) * ov], qr[px, 1:2, kx * ov : (kx + 1) * ov]]
        oh = hits(rowc[gpm:, :], jnp.concatenate(pair, axis=1))
        around_b += dot(oh, of(5.0 + m, jnp.concatenate([margin(ky), margin(kx)], axis=0)).astype(BF16))
    edge2[: 4 * halo, :] = around_b
    operate(bextf, abf, None)
    add_layers(abf, lambda p: edge2[p * halo : p * halo + hrows[p], :])
    bextb[...] = bextf[...].astype(BF16)
    abextb[...] = abf[...].astype(BF16)

    for p in range(4):
        pieces = [of(1.0 + p, margin(p ^ 1))] + [of(1.0 + p, layer_rows(bt, p, d)) for d in range(3)]
        yb[p * mrows : p * mrows + ov + 3 * halo, :] = jnp.concatenate(pieces, axis=0).astype(BF16)
        cells = coded(beside_cells(column_of(crows), p), -sides[p][0], -sides[p][1])
        row = []
        for u, k in ((-1, 2), (1, 3)) if p < 2 else ((-1, 0), (1, 1)):
            way = (-sides[p][0], -u) if p < 2 else (-u, -sides[p][1])
            row.append(qd_r[corner.index(way), 0:1, k * ov : (k + 1) * ov])
        k = 2 if p < 2 else 0
        theirs = of(1.0 + p, bt[own + k * ov : own + (k + 2) * ov, :]).astype(BF16)
        made = dot(hits(cells, jnp.concatenate(row, axis=1)), theirs)
        yb[p * mrows + ov + 3 * halo : (p + 1) * mrows, :] = made.astype(BF16)
    for m, (sx, sy) in enumerate(corner):
        ky, py = (0 if sx < 0 else 1), (3 if sy < 0 else 2)
        kx, px = (2 if sy < 0 else 3), (1 if sx < 0 else 0)
        pair = [qr[py, 1:2, ky * ov : (ky + 1) * ov], qr[px, 1:2, kx * ov : (kx + 1) * ov]]
        cells = coded(corner_cells(column_of(dr), sx, sy), sx, sy)
        theirs = of(5.0 + m, jnp.concatenate([margin(ky), margin(kx)], axis=0)).astype(BF16)
        made = dot(hits(cells, jnp.concatenate(pair, axis=1)), theirs)
        theirs = jnp.concatenate([layer_rows(bt, q) for q in range(4)], axis=0)
        rest = dot(gstat[m * (dr - dr2) : (m + 1) * (dr - dr2), :], of(5.0 + m, theirs).astype(BF16))
        at = ycorner + m * dr
        yb[at : at + dr2, :] = made[:dr2].astype(BF16)
        yb[at + dr2 : at + dr, :] = (made[dr2:] + rest).astype(BF16)

    wide = min(kd, 256)
    pmf = jnp.broadcast_to(pmap_ref[...].astype(F32), (8, n))
    spare_s = jnp.zeros((spare, kd), F32)
    stacked_s = jnp.concatenate([sall[...].astype(F32).reshape(nine * kw, kd), spare_s], axis=0).astype(BF16)

    def order(c, _):
        q = fiota((1, wide), 1) + (c * wide).astype(F32)
        at_slot = fdiv(q, kw)
        slab = fdiv(at_slot, gx)
        dev = (at_slot - slab * gx) * gy + slab
        pick = jnp.where(fiota((n, wide), 0) == dev, 1.0, 0.0)
        place = dot(pmf, pick, precision=HIGH)[0:1] * kw + (q - at_slot * kw)
        perm = jnp.where(fiota((kd, wide), 0) == place, 1.0, 0.0).astype(BF16)
        at = pl.ds(pl.multiple_of(c * wide, wide), wide)
        sext[:, at] = dot(stacked_s, perm).astype(BF16)
        return 0

    lax.fori_loop(jnp.int32(0), jnp.int32(kd // wide), order, 0)
    def as_column(line):
        return jnp.broadcast_to(jnp.broadcast_to(line, (8, 4 * ov)).T[:, 0:1], (4 * ov, 128))

    qb[...] = as_column(ycode[0:1, :yedge])
    wait_t()
    sb[...] = as_column((tr[0] + tr[1] + tr[2] + tr[3])[0:1])
    pm = pmv[...].astype(BF16)
    for h in range(0, cmarg.shape[1], 128):
        gap = jnp.abs(lines[0:1, h : h + 128] - qb[...])
        cmarg[:, h : h + 128] = coefficient(gap, sb[...])
    mix = dot(cmarg[:, : 4 * (mrows + dr)], yb[...])
    for p in range(4):
        at = slice(p * ov, (p + 1) * ov)
        line = jnp.concatenate([ycode[0:1, at], edge_code[p ^ 1]], axis=1)
        mc[p] = adjacent(jnp.abs(line - qb[at, : ov + halo])).astype(BF16)
        near_edge = jnp.concatenate([pm[at], msg_s[p ^ 1, ov : ov + halo, :]], axis=0)
        near_b = [of(0.0, margin(p)), of(0.0, layer_rows(bt, p ^ 1))]
        near_b = jnp.concatenate(near_b, axis=0).astype(BF16)
        mine = dot(mc[p], near_b) - sb[at, :] * of(0.0, margin(p))
        mbb[at, :] = (mix[at] + mine).astype(BF16)
        known = sub[0, own + p * ov : own + (p + 1) * ov, :].astype(F32)
        edge2[at, :] = known + dot(mc[p], near_edge) - sb[at, :] * pmv[at, :]

    rc = fiota((layer, 128), 0)
    ri = fdiv(rc, cy)
    here_code = code(0.0, ri, rc - ri * cy)

    def fill_own(c, _):
        at = pl.ds(pl.multiple_of(c * layer, layer), layer)
        shift = c.astype(F32) * (wide_grid * wide_grid)
        for h in range(0, cown.shape[1], 128):
            gap = jnp.abs(here_code + shift - lines[1:2, h : h + 128])
            cown[at, h : h + 128] = coefficient(gap, diag[:, :128])
        return 0

    lax.fori_loop(jnp.int32(0), jnp.int32(comps), fill_own, 0)

    r = fiota((2 * comps * cx, own), 0)
    lower = jnp.where(r >= comps * cx, 1.0, 0.0)
    wanted_row = (r - lower * (comps * cx)) * cy + (cy - 1) * (1.0 - lower)
    pick = jnp.where(fiota((2 * comps * cx, own), 1) == wanted_row, 1.0, 0.0).astype(BF16)
    inve[...] = dot(pick, inv_v[:own, :]).astype(BF16)

    operate(xs, mid, res_v)
    ring[...] = dot(gmat[gpm:, :], pm)
    add_layers(mid, ring_side)

    gathered = arrived()
    cout = dot(sext[...], gathered).astype(BF16)
    edge2[: 4 * ov, :] += dot(mbb[...], cout)
    mid[...] += dot(abextb[...], cout)

    wait_back()
    wait_corners()

    def piece(p, at, count):
        return ybuf[p * mrows + at : p * mrows + at + count, :]

    pieces = 4 * (mrows + dr)
    sub[1, own:, :] = (edge2[: 4 * ov, :] + dot(cmarg[:, :pieces], ybuf[...])).astype(BF16)
    backs = jnp.concatenate([piece(p, 0, ov) for p in range(4)], axis=0)
    rest = [piece(p, ov, halo) for p in range(4)]
    rest += [ybuf[ycorner + m * dr : ycorner + m * dr + dr2, :] for m in range(4)]
    sol_ref[...] = split(cown, jnp.concatenate([backs] + rest, axis=0))
    value = mid[...] + sol_ref[...]
    mid[...] = value
    sub[1, :own, :] = value.astype(BF16)

    go, arrived = start_gather(1, dot(basis_ref[...], sub[1]))
    go(0)
    lhs = [inv_v[own:, :]]
    lhs += [inv_v[c * layer + layer - cy : (c + 1) * layer, :] for c in range(comps)]
    lhs += [inv_v[c * layer : c * layer + cy, :] for c in range(comps)]
    made = split(jnp.concatenate(lhs + [inve[...]], axis=0), sub[1])
    pm = made[: 4 * ov].astype(BF16)
    at = 4 * ov
    for p in range(4):
        msg2_s[p, :ov, :] = pm[(p ^ 1) * ov : ((p ^ 1) + 1) * ov]
        msg2_s[p, ov : ov + hrows[p], :] = made[at : at + hrows[p]].astype(BF16)
        at += hrows[p]
    wait_back = trade(
        lambda p: [remote(msg2_s.at[p], msg2_r.at[p], nsem_s.at[2, p], nsem_r.at[2, p], up[p])],
        has_up, has_down,
    )
    dsend2[...] = dot(gmat[: 4 * dr2, :], pm).astype(BF16)
    wait_corners = trade(
        lambda p: [remote(dsend2.at[pl.ds(p * dr2, dr2)], drecv2.at[pl.ds(p * dr2, dr2)], dsem_s.at[1, p], dsem_r.at[1, p], cdev[p])],
        has_c, has_cd,
    )
    go(1)
    sol_ref[...] = xs[...] + dot(bextb[...], cout)
    sol_ref[...] += dot(sel[...], backs)
    xs[...] = split(inv_v.at[pl.ds(0, own), :], sub[1])
    sol_ref[...] += xs[...]
    operate(xs, fin_ref, mid)
    ring[...] = dot(gmat[gpm:, :], pm)
    add_layers(fin_ref, ring_side)
    wait_back()
    wait_corners()
    backs = jnp.concatenate([msg2_r[p, :ov, :] for p in range(4)], axis=0)
    rest = jnp.concatenate([msg2_r[p, ov:, :] for p in range(4)] + [drecv2[...]], axis=0)
    both = jnp.concatenate([backs, rest], axis=0)
    xs[...] = split(cown, both)
    fin_ref[...] += xs[...]
    sol_ref[...] += split(sel, backs)
    gathered = arrived()
    cout = dot(sext[...], gathered).astype(BF16)
    fin_ref[...] += split(abextb, cout)
    sol_ref[...] += split(bextb, cout)
    for end in finish:
        end()


def emit(sol_ref, fin_ref, sol_hbm, fin_hbm, sem):
    parts = sem.shape[0] // 2
    size = sol_ref.shape[0] // parts
    copies = []
    for k in range(parts):
        at = pl.ds(k * size, size)
        for h, (x, y) in enumerate(((sol_ref, sol_hbm), (fin_ref, fin_hbm))):
            copies.append(pltpu.make_async_copy(x.at[at], y.at[at], sem.at[2 * k + h]))
    for c in copies:
        c.start()
    for c in copies:
        c.wait()


def solution(mesh):
    gx, gy = mesh.shape["gx"], mesh.shape["gy"]

    def per_device(residual, stiffness, local_inverse, coarse_basis, coarse_rows, send_rows, partition_map):
        comps, cx, cy, nv = residual.shape
        own, layer = comps * cx * cy, cx * cy
        m = local_inverse.shape[-1]
        ov = send_rows.shape[-1]
        kw, kd = coarse_rows.shape[-2:]
        halo = comps * max(cx, cy)
        def whole(count, of):
            return -(-count // of) * of

        lanes = whole(9 * kw, 128)
        dr, dr2 = whole(15 * comps, 16), whole(4 * comps, 16)
        crows = whole(6 * comps, 16)
        mrows = ov + 3 * halo + crows
        width = whole(4 * (mrows + dr), 128)
        grows = 4 * (halo + crows + dr)
        vm = pl.BlockSpec(memory_space=pltpu.VMEM)
        anywhere = pl.BlockSpec(memory_space=pl.ANY)
        dma = pltpu.SemaphoreType.DMA
        out = pl.pallas_call(
            functools.partial(kernel, gx, gy, (comps, cx, cy, nv)),
            out_shape=[pltpu.VMEM((own, nv), F32)] * 2,
            in_specs=[anywhere] * 7,
            out_specs=[vm, vm],
            scratch_shapes=[
                pltpu.VMEM((own, nv), F32),
                pltpu.VMEM((cx, cy), F32),
                pltpu.VMEM((m, m), BF16),
                pltpu.VMEM((kw, m), BF16),
                pltpu.VMEM((kw, kd), BF16),
                pltpu.VMEM((4, ov), jnp.int32),
                pltpu.VMEM((1, gx * gy), jnp.int32),
                pltpu.VMEM((2, m, nv), BF16),
                pltpu.VMEM((own, 4 * ov), BF16),
                pltpu.VMEM((4, ov, 2 * halo), BF16),
                pltpu.VMEM((2, 4 * ov, nv), BF16),
                pltpu.VMEM((4 * (mrows + dr), nv), BF16),
                pltpu.VMEM((8, 4 * ov + 4 * halo), F32),
                pltpu.VMEM((8, width), F32),
                pltpu.VMEM((grows, 128), F32),
                pltpu.VMEM((4 * ov, 128), F32),
                pltpu.VMEM((4 * ov, 128), F32),
                pltpu.VMEM((grows, 4 * ov), BF16),
                pltpu.VMEM((4 * (dr - dr2), 4 * halo), BF16),
                pltpu.VMEM((own, 4 * (ov + halo + dr2)), BF16),
                pltpu.VMEM((4 * ov, width), BF16),
                pltpu.VMEM((4, ov, ov + halo), BF16),
                pltpu.VMEM((2 * comps * cx, m), BF16),
                pltpu.VMEM((4 * ov, nv), F32),
                pltpu.VMEM((4 * halo, nv), F32),
                pltpu.VMEM((4, mrows, nv), BF16),
                pltpu.VMEM((4, dr, nv), BF16),
                pltpu.VMEM((4, ov + halo, nv), BF16),
                pltpu.VMEM((4, ov + halo, nv), BF16),
                pltpu.VMEM((4 * dr2, nv), BF16),
                pltpu.VMEM((4 * dr2, nv), BF16),
                pltpu.VMEM((4, 8, 4 * ov), F32),
                pltpu.VMEM((4, 8, 4 * ov), F32),
                pltpu.VMEM((4, 8, 4 * ov), F32),
                pltpu.VMEM((4, 8, 4 * ov), F32),
                pltpu.VMEM((4, 8, 4 * ov), F32),
                pltpu.VMEM((4, 8, 4 * ov), F32),
                pltpu.VMEM((2, gx * gy, kw, nv), BF16),
                pltpu.VMEM((9, kw, m), BF16),
                pltpu.VMEM((9, kw, kd), BF16),
                pltpu.VMEM((lanes, kd), BF16),
                pltpu.VMEM((m, lanes), F32),
                pltpu.VMEM((own, lanes), F32),
                pltpu.VMEM((own, lanes), F32),
                pltpu.VMEM((own, lanes), BF16),
                pltpu.VMEM((own, lanes), BF16),
                pltpu.VMEM((4 * (mrows + dr), lanes), BF16),
                pltpu.VMEM((4 * ov, lanes), BF16),
                pltpu.VMEM((max(4 * ov, 4 * halo), nv), F32),
                pltpu.VMEM((layer, nv), F32),
                pltpu.VMEM((layer, nv), F32),
                pltpu.VMEM((layer, nv), F32),
                pltpu.VMEM((own, nv), F32),
                pltpu.VMEM((own, nv), F32),
                dma((7,)),
                pltpu.SemaphoreType.REGULAR,
                dma((3, 4)),
                dma((3, 4)),
                dma((2, 4)),
                dma((2, 4)),
                dma((5, 4)),
                dma((5, 4)),
                dma((3, 4)),
                dma((3, 4)),
                dma((2,)),
                dma((2,)),
            ],
            compiler_params=pltpu.CompilerParams(collective_id=0, has_side_effects=True),
        )(
            residual.reshape(own, nv),
            stiffness,
            local_inverse[0, 0],
            coarse_basis[0, 0],
            coarse_rows[0, 0],
            send_rows[0, 0],
            partition_map.reshape(1, -1),
        )
        out = pl.pallas_call(
            emit,
            out_shape=[jax.ShapeDtypeStruct((own, nv), F32)] * 2,
            in_specs=[vm, vm],
            out_specs=[anywhere, anywhere],
            scratch_shapes=[dma((2 * comps,))],
        )(*[pltpu.with_memory_space_constraint(o, pltpu.VMEM) for o in out])
        return tuple(o.reshape(residual.shape) for o in out)

    placed = (
        P(None, "gx", "gy", None),
        P("gx", "gy"),
        P("gx", "gy", None, None),
        P("gx", "gy", None, None),
        P("gx", "gy", None, None),
        P("gx", "gy", None, None),
        P(),
    )
    return jax.shard_map(
        per_device,
        mesh=mesh,
        in_specs=placed,
        out_specs=(P(None, "gx", "gy", None), P(None, "gx", "gy", None)),
        check_vma=False,
    )
```

```python
import functools

import jax
import jax.numpy as jnp
from jax import lax
from jax.experimental import pallas as pl
from jax.experimental.pallas import tpu as pltpu
from jax.sharding import PartitionSpec as P

MESH = pl.DeviceIdType.MESH
F32 = jnp.float32
BF16 = jnp.bfloat16
HIGH = lax.Precision.HIGHEST


def dot(x, y, **kw):
    return jnp.dot(x, y, preferred_element_type=F32, **kw)


def split(x, y):
    cut = x.shape[0] // 32 * 16
    return jnp.concatenate([dot(x[:cut, :], y), dot(x[cut:, :], y)], axis=0)


def tdot(x, y):
    return lax.dot_general(x, y, (((0,), (0,)), ((), ())), preferred_element_type=F32)


def fiota(shape, axis):
    return lax.broadcasted_iota(jnp.int32, shape, axis).astype(F32)


def fdiv(x, n):
    return jnp.floor((x + 0.5) * (1.0 / n))


def kernel(
    gx, gy, dims,
    res_hbm, stiff_hbm, inv_hbm, basis_hbm, crows_hbm, lists_hbm, pmap_hbm,
    sol_ref, fin_ref,
    res_v, stiff_ref, inv_v, basis_ref, crows_ref, lists_ref, pmap_ref, sub, sel, near, outs,
    ybuf, ycode, lines, rowc, qb, sb, gmat, gstat, cown, cmarg, mc, inve, pmv, ring, msg_s, dsend,
    msg2_s, msg2_r, dsend2, drecv2,
    qs, qr, qd_s, qd_r, ts, tr, allbuf, ball, sall, sext, bt, bextf, abf, bextb, abextb, yb, mbb, edge2,
    diag, m_lo, m_hi, xs, mid,
    lsem, ready, nsem_s, nsem_r, dsem_s, dsem_r, csem_s, csem_r, rsem_s, rsem_r, gs, gr,
):
    comps, cx, cy, nv = dims
    halo = comps * max(cx, cy)
    hrows = (comps * cy, comps * cy, comps * cx, comps * cx)
    own = comps * cx * cy
    layer = cx * cy
    ov = lists_ref.shape[1]
    kw, kd = crows_ref.shape
    n = gx * gy
    mrows = msg_s.shape[1]
    crows = mrows - ov - 3 * halo
    dr, dr2 = dsend.shape[1], dsend2.shape[0] // 4
    yedge = 4 * ov
    ycorner = 4 * mrows
    gpm = 4 * (dr + crows)
    nine = ball.shape[0]
    lanes = bextf.shape[1]
    a = lax.axis_index("gx")
    b = lax.axis_index("gy")

    wanted = [
        (lists_hbm, lists_ref), (res_hbm, res_v), (pmap_hbm, pmap_ref), (crows_hbm, crows_ref),
        (basis_hbm, basis_ref), (stiff_hbm, stiff_ref), (inv_hbm, inv_v),
    ]
    loads = [pltpu.make_async_copy(x, y, lsem.at[k]) for k, (x, y) in enumerate(wanted)]
    load_lists, load_res, load_pmap, load_crows, load_basis, load_stiff, load_inv = loads
    for load in loads:
        load.start()

    def flip(x, k):
        y, bit = x, 1
        while bit <= k:
            if k & bit:
                y = y + bit * (1 - 2 * lax.rem(lax.div(x, bit), 2))
            bit *= 2
        return y

    paired = gx & (gx - 1) == 0 and gy & (gy - 1) == 0
    others = [(i, j) for i in range(gx) for j in range(gy) if i or j]
    if paired:
        others.sort(key=lambda o: -((o[0] >> 1) + bin(o[1]).count("1") + 0.4 * (o[0] & 1)))
        to_a = [flip(a, i) for i in range(gx)]
        to_b = [flip(b, j) for j in range(gy)]
    else:
        to_a = [lax.rem(a + i, gx) for i in range(gx)]
        to_b = [lax.rem(b + j, gy) for j in range(gy)]

    half = len(others) // 2

    def each_other(act, chosen=None):
        if n <= 64:
            for i, j in others if chosen is None else (others[:half], others[half:])[chosen]:
                act((to_a[i], to_b[j]))
            return
        if chosen == 1:
            return

        def row(i, _):
            ai = lax.rem(a + i, gx)
            for j in range(1, gy):
                act((ai, lax.rem(b + j, gy)))
            pl.when(i > 0)(lambda: act((ai, b)))
            return 0

        lax.fori_loop(jnp.int32(0), jnp.int32(gx), row, 0)

    barrier = pltpu.get_barrier_semaphore()

    def peers(size):
        return sorted(range(1, size), key=lambda o: min(o, size - o))

    def signal(sem, dev):
        pl.semaphore_signal(sem, inc=1, device_id=dev, device_id_type=MESH)

    for o in peers(gy):
        signal(barrier, (a, lax.rem(b + o, gy)))
    for o in peers(gx):
        signal(barrier, (lax.rem(a + o, gx), b))

    up = [(a + 1, b), (a - 1, b), (a, b + 1), (a, b - 1)]
    has_up = [a < gx - 1, a > 0, b < gy - 1, b > 0]
    down = [up[p ^ 1] for p in range(4)]
    has_down = [has_up[p ^ 1] for p in range(4)]
    corner = [(1, 1), (-1, -1), (1, -1), (-1, 1)]
    cdev = [(a + sx, b + sy) for sx, sy in corner]
    has_c = [
        jnp.logical_and(has_up[0 if sx > 0 else 1], has_up[2 if sy > 0 else 3]) for sx, sy in corner
    ]
    finish = []

    for p in range(4):
        pl.when(has_c[p])(lambda p=p: signal(barrier, cdev[p]))

    def send(copies, conds, wait):
        for p in (2, 3, 0, 1):
            @pl.when(conds[p])
            def _(p=p):
                for c in copies(p):
                    getattr(c, wait)()

    def trade(copies, to, fro):
        send(copies, to, "start")
        finish.append(lambda: send(copies, to, "wait_send"))
        return lambda: send(copies, fro, "wait_recv")

    def remote(src, dst, s, r, dev):
        return pltpu.make_async_remote_copy(
            src_ref=src, dst_ref=dst, send_sem=s, recv_sem=r, device_id=dev, device_id_type=MESH
        )

    wide_grid = 4 * max(cx, cy)

    def code(c, i, j):
        return (c * wide_grid + (i + cx)) * wide_grid + (j + cy)

    load_lists.wait()
    lists = lists_ref[...].astype(F32)
    columns = lists.T
    for p in range(4):
        count = 2 * hrows[p]
        q = fiota((1, count), 1)
        if p < 2:
            c = fdiv(q, 2 * cy)
            row = c * layer + (layer - 2 * cy) * (1 - p) + (q - c * 2 * cy)
        else:
            second = jnp.where(q >= comps * cx, 1.0, 0.0)
            row = (q - second * (comps * cx)) * cy + (cy - 2) * (3 - p) + second
        hit = jnp.broadcast_to(columns[:, (p ^ 1) : (p ^ 1) + 1], (ov, count)) == jnp.broadcast_to(row, (ov, count))
        near[p, :, :count] = jnp.where(hit, 1.0, 0.0).astype(BF16)

    lc = fdiv(lists, layer)
    li = fdiv(lists - lc * layer, cy)
    lj = lists - lc * layer - li * cy
    block = fdiv(fiota((1, 4 * ov), 1), ov)

    def in_line(x):
        return jnp.concatenate([x[(p ^ 1) : (p ^ 1) + 1] for p in range(4)], axis=1)

    sides = ((-1, 0), (1, 0), (0, -1), (0, 1))
    for p, (dx, dy) in enumerate(sides):
        line = in_line(code(lc, li + dx * cx, lj + dy * cy))
        qs[p, 0:1, :] = jnp.where(block == p, line, 0.0)
        qs[p, 1:2, :] = line

    load_res.wait()

    def gather(t, src):
        for p in range(4):
            if p < 2:
                skip = (layer - 2 * cy) * (1 - p)
                rows = [src[c * layer + skip : c * layer + skip + 2 * cy, :] for c in range(comps)]
            else:
                rows = [src[pl.ds((cy - 2) * (3 - p) + k, comps * cx, stride=cy), :] for k in range(2)]
            rows = jnp.concatenate(rows, axis=0).astype(BF16)
            outs[t, p * ov : (p + 1) * ov, :] = dot(near[p, :, : 2 * hrows[p]], rows).astype(BF16)

    gather(0, res_v)
    met = gx + gy - 2 + sum(c.astype(jnp.int32) for c in has_c)
    pl.semaphore_wait(barrier, met)

    def start_margins(t):
        return trade(
            lambda p: [
                remote(outs.at[t, pl.ds(p * ov, ov)], sub.at[t, pl.ds(own + p * ov, ov)],
                       nsem_s.at[0, p], nsem_r.at[0, p], up[p]),
                remote(qs.at[p], qr.at[p], csem_s.at[0, p], csem_r.at[0, p], up[p]),
            ],
            has_up, has_down,
        )

    wait_margins = start_margins(0)
    has_cd = [has_c[p ^ 1] for p in range(4)]
    for o in peers(gy):
        signal(ready, (a, lax.rem(b + o, gy)))
    for m, (sx, sy) in enumerate(corner):
        qd_s[m, 0:1, :] = in_line(code(lc, li - sx * cx, lj - sy * cy))
    load_basis.wait()
    load_crows.wait()
    wait_raw = trade(
        lambda p: [
            remote(basis_ref, ball.at[1 + p], csem_s.at[1, p], csem_r.at[1, p], up[p]),
            remote(crows_ref, sall.at[1 + p], csem_s.at[2, p], csem_r.at[2, p], up[p]),
        ],
        has_up, has_down,
    )
    wait_raw_c = trade(
        lambda p: [
            remote(basis_ref, ball.at[5 + p], rsem_s.at[0, p], rsem_r.at[0, p], cdev[p]),
            remote(qd_s.at[p], qd_r.at[p], rsem_s.at[2, p], rsem_r.at[2, p], cdev[p]),
            remote(crows_ref, sall.at[5 + p], rsem_s.at[1, p], rsem_r.at[1, p], cdev[p]),
        ],
        has_c, has_cd,
    )
    sub[0, :own, :] = res_v[...].astype(BF16)

    for p in range(4):
        @pl.when(jnp.logical_not(has_down[p]))
        def _(p=p):
            sub[0, own + p * ov : own + (p + 1) * ov, :] = jnp.zeros((ov, nv), BF16)
            ybuf[p * mrows : (p + 1) * mrows, :] = jnp.zeros((mrows, nv), BF16)
            msg2_r[p] = jnp.zeros(msg2_r.shape[1:], BF16)
            qr[p] = jnp.zeros(qr.shape[1:], F32)
            tr[p] = jnp.zeros(tr.shape[1:], F32)
            ball[1 + p] = jnp.zeros(ball.shape[1:], BF16)
            sall[1 + p] = jnp.zeros(sall.shape[1:], BF16)

        @pl.when(jnp.logical_not(has_cd[p]))
        def _(p=p):
            ybuf[ycorner + p * dr : ycorner + (p + 1) * dr, :] = jnp.zeros((dr, nv), BF16)
            drecv2[p * dr2 : (p + 1) * dr2, :] = jnp.zeros((dr2, nv), BF16)
            ball[5 + p] = jnp.zeros(ball.shape[1:], BF16)
            qd_r[p] = jnp.zeros(qd_r.shape[1:], F32)
            sall[5 + p] = jnp.zeros(sall.shape[1:], BF16)

    load_stiff.wait()
    r1 = fiota((layer, cy), 0)
    first = fdiv(r1, cy)
    mine = jnp.where(fiota((layer, cx), 1) == fdiv(fiota((layer, cx), 0), cy), 1.0, 0.0)
    spread = dot(mine, stiff_ref[...], precision=HIGH)
    spread = jnp.where(fiota((layer, cy), 1) == r1 - first * cy, spread, 0.0)
    diag[...] = jnp.broadcast_to(4.0 + jnp.sum(spread, axis=1, keepdims=True), (layer, nv))
    rr = fiota((layer, nv), 0)
    second = rr - fdiv(rr, cy) * cy
    m_lo[...] = jnp.where(second == 0.0, 0.0, 1.0)
    m_hi[...] = jnp.where(second == cy - 1.0, 0.0, 1.0)

    cells = jnp.where(fiota((layer, 4 * ov), 0) == in_line(li * cy + lj), 1.0, 0.0)
    at_cells = lax.dot_general(
        diag[...], cells, (((0,), (0,)), ((), ())), precision=HIGH, preferred_element_type=F32
    )[0:8]
    for p in range(4):
        ts[p] = jnp.where(jnp.broadcast_to(block, (8, 4 * ov)) == p, at_cells, 0.0)
    wait_t = trade(
        lambda p: [remote(ts.at[p], tr.at[p], csem_s.at[3, p], csem_r.at[3, p], up[p])], has_up, has_down
    )

    def edge_cells(w, p, depth, outside):
        per = cy if p < 2 else cx
        c = fdiv(w, per)
        along = w - c * per
        size = cx if p < 2 else cy
        if outside:
            off = along * 0.0 + (-1.0 - depth, size + depth)[p % 2]
        else:
            off = along * 0.0 + (size - 1.0 - depth, 1.0 * depth)[p % 2]
        return (c, off, along, w < hrows[p]) if p < 2 else (c, along, off, w < hrows[p])

    def beside_cells(w, p):
        v = fdiv(w, 3 * comps)
        u = 1.0 - 2.0 * v
        c = fdiv(w - v * (3 * comps), 3)
        kk = w - v * (3 * comps) - 3 * c
        deep, far = jnp.where(kk == 1.0, 1.0, 0.0), jnp.where(kk == 2.0, 1.0, 0.0)
        size, size2 = (cx, cy) if p < 2 else (cy, cx)
        along = (size - 1.0 - deep) if p % 2 == 0 else deep
        out = jnp.where(v == 0.0, size2 + far, -1.0 - far)
        return (c, along, out, v < 2.0) if p < 2 else (c, out, along, v < 2.0)

    def corner_cells(w, sx, sy):
        ex, ey = (cx - 1.0 if sx > 0 else 0.0), (cy - 1.0 if sy > 0 else 0.0)
        ox, oy = (1.0 * cx if sx > 0 else -1.0), (1.0 * cy if sy > 0 else -1.0)
        g = fdiv(w, 2 * comps)
        depth = fdiv(g, 2)
        kind = g - 2 * depth
        c = fdiv(w - g * (2 * comps), 2)
        k = w - g * (2 * comps) - 2 * c
        i = jnp.where(kind == 0.0, ex - sx * depth, ox + sx * k)
        j = jnp.where(kind == 0.0, oy + sy * k, ey - sy * depth)
        w2 = w - 12 * comps
        c2 = fdiv(w2, 3)
        kk = w2 - 3 * c2
        tail = w2 >= 0.0
        i = jnp.where(tail, ex - sx * jnp.where(kk == 1.0, 1.0, 0.0), i)
        j = jnp.where(tail, ey - sy * jnp.where(kk == 2.0, 1.0, 0.0), j)
        return jnp.where(tail, c2, c), i, j, w < 15 * comps

    nowhere = -16.0 * wide_grid * wide_grid

    def coded(cell, dx=0, dy=0):
        c, i, j, real = cell
        return jnp.where(real, code(c, i - dx * cx, j - dy * cy), nowhere)

    def row_of(count):
        return fiota((1, count), 1)

    def deduped(cell, p):
        c, i, j, real = cell
        return (c, i, j, real if p < 2 else jnp.logical_and(real, jnp.logical_and(i > 0.0, i < cx - 1.0)))

    back_code = [code(lc, li, lj)[p : p + 1] for p in range(4)]
    edge_code = [coded(edge_cells(row_of(halo), p, 0, False)) for p in range(4)]
    deep_code = [[coded(edge_cells(row_of(halo), p, d, True)) for d in range(3)] for p in range(4)]
    beside_code = [coded(beside_cells(row_of(crows), p), -sides[p][0], -sides[p][1]) for p in range(4)]
    corner_code = [coded(corner_cells(row_of(dr), *corner[m]), *corner[m]) for m in range(4)]
    short_code = [coded(corner_cells(row_of(dr2), *corner[m]), *corner[m]) for m in range(4)]
    ycode[0:1, yedge:] = jnp.concatenate(
        [coded(deduped(edge_cells(row_of(halo), p, 0, False), p)) for p in range(4)], axis=1
    )
    line = []
    for p in range(4):
        line += [back_code[p]] + deep_code[p] + [beside_code[p]]
    line = jnp.concatenate(line + corner_code, axis=1)
    lines[...] = jnp.full(lines.shape, nowhere, F32)
    lines[0:1, : line.shape[1]] = line
    line = jnp.concatenate(back_code + [deep_code[p][0] for p in range(4)] + short_code, axis=1)
    lines[1:2, : line.shape[1]] = line

    def column_of(count):
        return fiota((count, 128), 0)

    rlist = [coded(corner_cells(column_of(dr2), *corner[m])) for m in range(4)]
    rlist += [coded(beside_cells(column_of(crows), p)) for p in range(4)]
    rlist += [coded(corner_cells(column_of(dr - dr2) + dr2, *corner[m])) for m in range(4)]
    rlist += [coded(edge_cells(column_of(halo), p, 0, True)) for p in range(4)]
    rowc[...] = jnp.concatenate(rlist, axis=0)

    def hits(rows, row):
        parts = []
        for at in range(0, row.shape[1], 128):
            piece = row[:, at : at + 128]
            parts.append(jnp.where(rows[:, : piece.shape[1]] == piece, 1.0, 0.0))
        return (jnp.concatenate(parts, axis=1) if len(parts) > 1 else parts[0]).astype(BF16)

    def adjacent(gap):
        return jnp.where(jnp.logical_or(gap == 1.0, gap == wide_grid), 1.0, 0.0)

    def coefficient(gap, weight):
        return jnp.where(gap == 0.0, -weight, adjacent(gap)).astype(BF16)

    gmat[...] = jnp.zeros(gmat.shape, BF16)
    first_rest = 4 * (dr2 + crows)
    gstat[...] = hits(rowc[first_rest:gpm, :], ycode[0:1, yedge:])

    rows = fiota((own, ov), 0)
    for h in range(2):
        two = [jnp.where(rows == lists[p : p + 1], 1.0, 0.0) for p in (2 * h, 2 * h + 1)]
        sel[:, 2 * ov * h : 2 * ov * (h + 1)] = jnp.concatenate(two, axis=1).astype(BF16)

    def layer_rows(ref, p, depth=0):
        if p >= 2:
            return ref[pl.ds(cy - 1 - depth if p == 2 else depth, comps * cx, stride=cy), :]
        skip = layer - cy - depth * cy if p == 0 else depth * cy
        return jnp.concatenate([ref[c * layer + skip : c * layer + skip + cy, :] for c in range(comps)], axis=0)

    def operate(x_ref, dst, src):
        zero = jnp.zeros((cy, nv), F32)
        for c in range(comps):
            at = pl.ds(c * layer, layer)
            x = x_ref[at, :]
            beside = jnp.concatenate([zero, x[:-cy]], axis=0) + jnp.concatenate([x[cy:], zero], axis=0)
            beside += pltpu.roll(x, 1, 0) * m_lo[...] + pltpu.roll(x, layer - 1, 0) * m_hi[...]
            value = beside - diag[...] * x
            dst[at, :] = value if src is None else src[at, :] + value

    def add_layers(dst, around):
        for c in range(comps):
            base = c * layer
            dst[base : base + cy, :] += around(0)[c * cy : (c + 1) * cy]
            dst[base + layer - cy : base + layer, :] += around(1)[c * cy : (c + 1) * cy]
        low = pl.ds(0, comps * cx, stride=cy)
        high = pl.ds(cy - 1, comps * cx, stride=cy)
        dst[low, :] = dst[low, :] + around(2)
        dst[high, :] = dst[high, :] + around(3)

    def ring_side(p):
        return ring[p * halo : p * halo + hrows[p], :]

    slot = b * gx + a

    def start_gather(t, cin):
        allbuf[t, slot] = cin.astype(BF16)
        here = allbuf.at[t, slot]
        rest = allbuf.at[t, pl.ds(0, n - 1)]
        gathering = remote(rest, rest, gs.at[t], gr.at[t], (to_a[0], to_b[1]))
        finish.append(gathering.wait_send)

        def go(chosen):
            each_other(lambda dev: remote(here, here, gs.at[t], gr.at[t], dev).start(), chosen)

        def arrived():
            gathering.wait_recv()
            return allbuf[t].astype(F32).reshape(kd, nv).astype(BF16)

        return go, arrived

    load_inv.wait()
    part = split(inv_v.at[:, pl.ds(0, own)], sub[0, :own, :])
    cpart = dot(basis_ref[:, :own], sub[0, :own, :])
    wait_margins()
    edge = sub[0, own:, :]
    go, arrived = start_gather(0, cpart + dot(basis_ref[:, own:], edge))
    pl.semaphore_wait(ready, gy - 1)
    go(0)
    q = (qr[0] + qr[1] + qr[2] + qr[3])[0:1]
    ycode[0:1, :yedge] = q
    tiles = (slice(0, 2 * ov), slice(2 * ov, 4 * ov))
    for tile in tiles:
        gmat[: 4 * dr2, tile] = hits(rowc[: 4 * dr2, :], q[:, tile])
        gmat[first_rest:gpm, tile] = hits(rowc[first_rest:gpm, :], q[:, tile])
    for h in range(2):
        at = slice(4 * dr2 + 2 * h * crows, 4 * dr2 + 2 * (h + 1) * crows)
        gmat[at, tiles[1 - h]] = hits(rowc[at, :], q[:, tiles[1 - h]])
    pmv[...] = part[own:] + dot(inv_v[own:, own:], edge)
    pm = pmv[...].astype(BF16)
    xs[...] = part[:own] + split(inv_v.at[pl.ds(0, own), pl.ds(own, 4 * ov)], edge)
    edges = jnp.concatenate([layer_rows(xs, p) for p in range(4)], axis=0).astype(BF16)
    made = split(gmat.at[pl.ds(0, gpm), :], pm)
    made_first = made[:first_rest].astype(BF16)
    made_rest = (made[first_rest:] + dot(gstat[...], edges)).astype(BF16)
    for p in range(4):
        msg_s[p, :ov, :] = pm[(p ^ 1) * ov : ((p ^ 1) + 1) * ov]
        msg_s[p, ov : ov + halo, :] = edges[p * halo : (p + 1) * halo]
        for d in range(1, 3):
            msg_s[p, ov + d * halo : ov + d * halo + hrows[p], :] = layer_rows(xs, p, d).astype(BF16)
        msg_s[p, ov + 3 * halo :, :] = made_first[4 * dr2 + p * crows : 4 * dr2 + (p + 1) * crows]
        dsend[p, :dr2, :] = made_first[p * dr2 : (p + 1) * dr2]
        dsend[p, dr2:, :] = made_rest[p * (dr - dr2) : (p + 1) * (dr - dr2)]
    wait_back = trade(
        lambda p: [remote(msg_s.at[p], ybuf.at[pl.ds(p * mrows, mrows)], nsem_s.at[1, p], nsem_r.at[1, p], up[p])],
        has_up, has_down,
    )
    wait_corners = trade(
        lambda p: [remote(dsend.at[p], ybuf.at[pl.ds(ycorner + p * dr, dr)], dsem_s.at[0, p], dsem_r.at[0, p], cdev[p])],
        has_c, has_cd,
    )
    go(1)
    for h in range(2):
        at = slice(gpm + 2 * h * halo, gpm + 2 * (h + 1) * halo)
        gmat[at, tiles[h]] = hits(rowc[at, :], q[:, tiles[h]])

    load_pmap.wait()
    wait_raw()
    wait_raw_c()
    ball[0] = basis_ref[...]
    sall[0] = crows_ref[...]
    spare = lanes - nine * kw
    stacked = jnp.concatenate([ball[...].astype(F32).reshape(nine * kw, -1), jnp.zeros((spare, own + 4 * ov), F32)], axis=0)
    bt[...] = stacked.T
    group = fdiv(fiota((1, lanes), 1), kw)

    def of(e, value):
        return jnp.where(group == e, value, 0.0)

    def margin(k):
        return bt[own + k * ov : own + (k + 1) * ov, :]

    theirs = jnp.concatenate([of(1.0 + p, margin(p ^ 1)) for p in range(4)], axis=0).astype(BF16)
    bextf[...] = of(0.0, bt[:own, :]) + dot(sel[...], theirs)
    around_b = jnp.concatenate([of(1.0 + p, layer_rows(bt, p)) for p in range(4)], axis=0)
    around_b += dot(gmat[gpm:, :], of(0.0, bt[own:, :]).astype(BF16))
    for m, (sx, sy) in enumerate(corner):
        ky, py = (0 if sx < 0 else 1), (3 if sy < 0 else 2)
        kx, px = (2 if sy < 0 else 3), (1 if sx < 0 else 0)
        pair = [qr[py, 1:2, ky * ov : (ky + 1) * ov], qr[px, 1:2, kx * ov : (kx + 1) * ov]]
        oh = hits(rowc[gpm:, :], jnp.concatenate(pair, axis=1))
        around_b += dot(oh, of(5.0 + m, jnp.concatenate([margin(ky), margin(kx)], axis=0)).astype(BF16))
    edge2[: 4 * halo, :] = around_b
    operate(bextf, abf, None)
    add_layers(abf, lambda p: edge2[p * halo : p * halo + hrows[p], :])
    bextb[...] = bextf[...].astype(BF16)
    abextb[...] = abf[...].astype(BF16)

    for p in range(4):
        pieces = [of(1.0 + p, margin(p ^ 1))] + [of(1.0 + p, layer_rows(bt, p, d)) for d in range(3)]
        yb[p * mrows : p * mrows + ov + 3 * halo, :] = jnp.concatenate(pieces, axis=0).astype(BF16)
        cells = coded(beside_cells(column_of(crows), p), -sides[p][0], -sides[p][1])
        row = []
        for u, k in ((-1, 2), (1, 3)) if p < 2 else ((-1, 0), (1, 1)):
            way = (-sides[p][0], -u) if p < 2 else (-u, -sides[p][1])
            row.append(qd_r[corner.index(way), 0:1, k * ov : (k + 1) * ov])
        k = 2 if p < 2 else 0
        theirs = of(1.0 + p, bt[own + k * ov : own + (k + 2) * ov, :]).astype(BF16)
        made = dot(hits(cells, jnp.concatenate(row, axis=1)), theirs)
        yb[p * mrows + ov + 3 * halo : (p + 1) * mrows, :] = made.astype(BF16)
    for m, (sx, sy) in enumerate(corner):
        ky, py = (0 if sx < 0 else 1), (3 if sy < 0 else 2)
        kx, px = (2 if sy < 0 else 3), (1 if sx < 0 else 0)
        pair = [qr[py, 1:2, ky * ov : (ky + 1) * ov], qr[px, 1:2, kx * ov : (kx + 1) * ov]]
        cells = coded(corner_cells(column_of(dr), sx, sy), sx, sy)
        theirs = of(5.0 + m, jnp.concatenate([margin(ky), margin(kx)], axis=0)).astype(BF16)
        made = dot(hits(cells, jnp.concatenate(pair, axis=1)), theirs)
        theirs = jnp.concatenate([layer_rows(bt, q) for q in range(4)], axis=0)
        rest = dot(gstat[m * (dr - dr2) : (m + 1) * (dr - dr2), :], of(5.0 + m, theirs).astype(BF16))
        at = ycorner + m * dr
        yb[at : at + dr2, :] = made[:dr2].astype(BF16)
        yb[at + dr2 : at + dr, :] = (made[dr2:] + rest).astype(BF16)

    wide = min(kd, 256)
    pmf = jnp.broadcast_to(pmap_ref[...].astype(F32), (8, n))
    spare_s = jnp.zeros((spare, kd), F32)
    stacked_s = jnp.concatenate([sall[...].astype(F32).reshape(nine * kw, kd), spare_s], axis=0).astype(BF16)

    def order(c, _):
        q = fiota((1, wide), 1) + (c * wide).astype(F32)
        at_slot = fdiv(q, kw)
        slab = fdiv(at_slot, gx)
        dev = (at_slot - slab * gx) * gy + slab
        pick = jnp.where(fiota((n, wide), 0) == dev, 1.0, 0.0)
        place = dot(pmf, pick, precision=HIGH)[0:1] * kw + (q - at_slot * kw)
        perm = jnp.where(fiota((kd, wide), 0) == place, 1.0, 0.0).astype(BF16)
        at = pl.ds(pl.multiple_of(c * wide, wide), wide)
        sext[:, at] = dot(stacked_s, perm).astype(BF16)
        return 0

    lax.fori_loop(jnp.int32(0), jnp.int32(kd // wide), order, 0)
    def as_column(line):
        return jnp.broadcast_to(jnp.broadcast_to(line, (8, 4 * ov)).T[:, 0:1], (4 * ov, 128))

    qb[...] = as_column(ycode[0:1, :yedge])
    wait_t()
    sb[...] = as_column((tr[0] + tr[1] + tr[2] + tr[3])[0:1])
    pm = pmv[...].astype(BF16)
    for h in range(0, cmarg.shape[1], 128):
        gap = jnp.abs(lines[0:1, h : h + 128] - qb[...])
        cmarg[:, h : h + 128] = coefficient(gap, sb[...])
    mix = dot(cmarg[:, : 4 * (mrows + dr)], yb[...])
    for p in range(4):
        at = slice(p * ov, (p + 1) * ov)
        line = jnp.concatenate([ycode[0:1, at], edge_code[p ^ 1]], axis=1)
        mc[p] = adjacent(jnp.abs(line - qb[at, : ov + halo])).astype(BF16)
        near_edge = jnp.concatenate([pm[at], msg_s[p ^ 1, ov : ov + halo, :]], axis=0)
        near_b = [of(0.0, margin(p)), of(0.0, layer_rows(bt, p ^ 1))]
        near_b = jnp.concatenate(near_b, axis=0).astype(BF16)
        mine = dot(mc[p], near_b) - sb[at, :] * of(0.0, margin(p))
        mbb[at, :] = (mix[at] + mine).astype(BF16)
        known = sub[0, own + p * ov : own + (p + 1) * ov, :].astype(F32)
        edge2[at, :] = known + dot(mc[p], near_edge) - sb[at, :] * pmv[at, :]

    rc = fiota((layer, 128), 0)
    ri = fdiv(rc, cy)
    here_code = code(0.0, ri, rc - ri * cy)

    def fill_own(c, _):
        at = pl.ds(pl.multiple_of(c * layer, layer), layer)
        shift = c.astype(F32) * (wide_grid * wide_grid)
        for h in range(0, cown.shape[1], 128):
            gap = jnp.abs(here_code + shift - lines[1:2, h : h + 128])
            cown[at, h : h + 128] = coefficient(gap, diag[:, :128])
        return 0

    lax.fori_loop(jnp.int32(0), jnp.int32(comps), fill_own, 0)

    r = fiota((2 * comps * cx, own), 0)
    lower = jnp.where(r >= comps * cx, 1.0, 0.0)
    wanted_row = (r - lower * (comps * cx)) * cy + (cy - 1) * (1.0 - lower)
    pick = jnp.where(fiota((2 * comps * cx, own), 1) == wanted_row, 1.0, 0.0).astype(BF16)
    inve[...] = dot(pick, inv_v[:own, :]).astype(BF16)

    operate(xs, mid, res_v)
    ring[...] = dot(gmat[gpm:, :], pm)
    add_layers(mid, ring_side)

    gathered = arrived()
    cout = dot(sext[...], gathered).astype(BF16)
    edge2[: 4 * ov, :] += dot(mbb[...], cout)
    mid[...] += dot(abextb[...], cout)

    wait_back()
    wait_corners()

    def piece(p, at, count):
        return ybuf[p * mrows + at : p * mrows + at + count, :]

    pieces = 4 * (mrows + dr)
    sub[1, own:, :] = (edge2[: 4 * ov, :] + dot(cmarg[:, :pieces], ybuf[...])).astype(BF16)
    backs = jnp.concatenate([piece(p, 0, ov) for p in range(4)], axis=0)
    rest = [piece(p, ov, halo) for p in range(4)]
    rest += [ybuf[ycorner + m * dr : ycorner + m * dr + dr2, :] for m in range(4)]
    sol_ref[...] = split(cown, jnp.concatenate([backs] + rest, axis=0))
    value = mid[...] + sol_ref[...]
    mid[...] = value
    sub[1, :own, :] = value.astype(BF16)

    go, arrived = start_gather(1, dot(basis_ref[...], sub[1]))
    go(0)
    lhs = [inv_v[own:, :]]
    lhs += [inv_v[c * layer + layer - cy : (c + 1) * layer, :] for c in range(comps)]
    lhs += [inv_v[c * layer : c * layer + cy, :] for c in range(comps)]
    made = split(jnp.concatenate(lhs + [inve[...]], axis=0), sub[1])
    pm = made[: 4 * ov].astype(BF16)
    at = 4 * ov
    for p in range(4):
        msg2_s[p, :ov, :] = pm[(p ^ 1) * ov : ((p ^ 1) + 1) * ov]
        msg2_s[p, ov : ov + hrows[p], :] = made[at : at + hrows[p]].astype(BF16)
        at += hrows[p]
    wait_back = trade(
        lambda p: [remote(msg2_s.at[p], msg2_r.at[p], nsem_s.at[2, p], nsem_r.at[2, p], up[p])],
        has_up, has_down,
    )
    dsend2[...] = dot(gmat[: 4 * dr2, :], pm).astype(BF16)
    wait_corners = trade(
        lambda p: [remote(dsend2.at[pl.ds(p * dr2, dr2)], drecv2.at[pl.ds(p * dr2, dr2)], dsem_s.at[1, p], dsem_r.at[1, p], cdev[p])],
        has_c, has_cd,
    )
    go(1)
    sol_ref[...] = xs[...] + dot(bextb[...], cout)
    sol_ref[...] += dot(sel[...], backs)
    xs[...] = split(inv_v.at[pl.ds(0, own), :], sub[1])
    sol_ref[...] += xs[...]
    operate(xs, fin_ref, mid)
    ring[...] = dot(gmat[gpm:, :], pm)
    add_layers(fin_ref, ring_side)
    wait_back()
    wait_corners()
    backs = jnp.concatenate([msg2_r[p, :ov, :] for p in range(4)], axis=0)
    rest = jnp.concatenate([msg2_r[p, ov:, :] for p in range(4)] + [drecv2[...]], axis=0)
    both = jnp.concatenate([backs, rest], axis=0)
    xs[...] = split(cown, both)
    fin_ref[...] += xs[...]
    sol_ref[...] += split(sel, backs)
    gathered = arrived()
    cout = dot(sext[...], gathered).astype(BF16)
    fin_ref[...] += split(abextb, cout)
    sol_ref[...] += split(bextb, cout)
    for end in finish:
        end()


def emit(sol_ref, fin_ref, sol_hbm, fin_hbm, sem):
    parts = sem.shape[0] // 2
    size = sol_ref.shape[0] // parts
    copies = []
    for k in range(parts):
        at = pl.ds(k * size, size)
        for h, (x, y) in enumerate(((sol_ref, sol_hbm), (fin_ref, fin_hbm))):
            copies.append(pltpu.make_async_copy(x.at[at], y.at[at], sem.at[2 * k + h]))
    for c in copies:
        c.start()
    for c in copies:
        c.wait()


def solution(mesh):
    gx, gy = mesh.shape["gx"], mesh.shape["gy"]

    def per_device(residual, stiffness, local_inverse, coarse_basis, coarse_rows, send_rows, partition_map):
        comps, cx, cy, nv = residual.shape
        own, layer = comps * cx * cy, cx * cy
        m = local_inverse.shape[-1]
        ov = send_rows.shape[-1]
        kw, kd = coarse_rows.shape[-2:]
        halo = comps * max(cx, cy)
        def whole(count, of):
            return -(-count // of) * of

        lanes = whole(9 * kw, 128)
        dr, dr2 = whole(15 * comps, 16), whole(4 * comps, 16)
        crows = whole(6 * comps, 16)
        mrows = ov + 3 * halo + crows
        width = whole(4 * (mrows + dr), 128)
        grows = 4 * (halo + crows + dr)
        vm = pl.BlockSpec(memory_space=pltpu.VMEM)
        anywhere = pl.BlockSpec(memory_space=pl.ANY)
        dma = pltpu.SemaphoreType.DMA
        out = pl.pallas_call(
            functools.partial(kernel, gx, gy, (comps, cx, cy, nv)),
            out_shape=[pltpu.VMEM((own, nv), F32)] * 2,
            in_specs=[anywhere] * 7,
            out_specs=[vm, vm],
            scratch_shapes=[
                pltpu.VMEM((own, nv), F32),
                pltpu.VMEM((cx, cy), F32),
                pltpu.VMEM((m, m), BF16),
                pltpu.VMEM((kw, m), BF16),
                pltpu.VMEM((kw, kd), BF16),
                pltpu.VMEM((4, ov), jnp.int32),
                pltpu.VMEM((1, gx * gy), jnp.int32),
                pltpu.VMEM((2, m, nv), BF16),
                pltpu.VMEM((own, 4 * ov), BF16),
                pltpu.VMEM((4, ov, 2 * halo), BF16),
                pltpu.VMEM((2, 4 * ov, nv), BF16),
                pltpu.VMEM((4 * (mrows + dr), nv), BF16),
                pltpu.VMEM((8, 4 * ov + 4 * halo), F32),
                pltpu.VMEM((8, width), F32),
                pltpu.VMEM((grows, 128), F32),
                pltpu.VMEM((4 * ov, 128), F32),
                pltpu.VMEM((4 * ov, 128), F32),
                pltpu.VMEM((grows, 4 * ov), BF16),
                pltpu.VMEM((4 * (dr - dr2), 4 * halo), BF16),
                pltpu.VMEM((own, 4 * (ov + halo + dr2)), BF16),
                pltpu.VMEM((4 * ov, width), BF16),
                pltpu.VMEM((4, ov, ov + halo), BF16),
                pltpu.VMEM((2 * comps * cx, m), BF16),
                pltpu.VMEM((4 * ov, nv), F32),
                pltpu.VMEM((4 * halo, nv), F32),
                pltpu.VMEM((4, mrows, nv), BF16),
                pltpu.VMEM((4, dr, nv), BF16),
                pltpu.VMEM((4, ov + halo, nv), BF16),
                pltpu.VMEM((4, ov + halo, nv), BF16),
                pltpu.VMEM((4 * dr2, nv), BF16),
                pltpu.VMEM((4 * dr2, nv), BF16),
                pltpu.VMEM((4, 8, 4 * ov), F32),
                pltpu.VMEM((4, 8, 4 * ov), F32),
                pltpu.VMEM((4, 8, 4 * ov), F32),
                pltpu.VMEM((4, 8, 4 * ov), F32),
                pltpu.VMEM((4, 8, 4 * ov), F32),
                pltpu.VMEM((4, 8, 4 * ov), F32),
                pltpu.VMEM((2, gx * gy, kw, nv), BF16),
                pltpu.VMEM((9, kw, m), BF16),
                pltpu.VMEM((9, kw, kd), BF16),
                pltpu.VMEM((lanes, kd), BF16),
                pltpu.VMEM((m, lanes), F32),
                pltpu.VMEM((own, lanes), F32),
                pltpu.VMEM((own, lanes), F32),
                pltpu.VMEM((own, lanes), BF16),
                pltpu.VMEM((own, lanes), BF16),
                pltpu.VMEM((4 * (mrows + dr), lanes), BF16),
                pltpu.VMEM((4 * ov, lanes), BF16),
                pltpu.VMEM((max(4 * ov, 4 * halo), nv), F32),
                pltpu.VMEM((layer, nv), F32),
                pltpu.VMEM((layer, nv), F32),
                pltpu.VMEM((layer, nv), F32),
                pltpu.VMEM((own, nv), F32),
                pltpu.VMEM((own, nv), F32),
                dma((7,)),
                pltpu.SemaphoreType.REGULAR,
                dma((3, 4)),
                dma((3, 4)),
                dma((2, 4)),
                dma((2, 4)),
                dma((5, 4)),
                dma((5, 4)),
                dma((3, 4)),
                dma((3, 4)),
                dma((2,)),
                dma((2,)),
            ],
            compiler_params=pltpu.CompilerParams(collective_id=0, has_side_effects=True),
        )(
            residual.reshape(own, nv),
            stiffness,
            local_inverse[0, 0],
            coarse_basis[0, 0],
            coarse_rows[0, 0],
            send_rows[0, 0],
            partition_map.reshape(1, -1),
        )
        out = pl.pallas_call(
            emit,
            out_shape=[jax.ShapeDtypeStruct((own, nv), F32)] * 2,
            in_specs=[vm, vm],
            out_specs=[anywhere, anywhere],
            scratch_shapes=[dma((2 * comps,))],
        )(*[pltpu.with_memory_space_constraint(o, pltpu.VMEM) for o in out])
        return tuple(o.reshape(residual.shape) for o in out)

    placed = (
        P(None, "gx", "gy", None),
        P("gx", "gy"),
        P("gx", "gy", None, None),
        P("gx", "gy", None, None),
        P("gx", "gy", None, None),
        P("gx", "gy", None, None),
        P(),
    )
    return jax.shard_map(
        per_device,
        mesh=mesh,
        in_specs=placed,
        out_specs=(P(None, "gx", "gy", None), P(None, "gx", "gy", None)),
        check_vma=False,
    )
```
